32 devices in a mesh: tile: 16 (over z, y, core), band: 2 (over x).
Axes of the slice: x: 2, y: 2, z: 4, core: 2. Of those that a mesh axis runs over, the one named last changes fastest.
Arguments:
- stamps: bfloat16 [4096, 64, 128], P(('band', 'tile')), parts along dimension 0, may hold values from -6 to 6
- tile_of: int32 [4096, 1], P(('band', 'tile')), parts along dimension 0, may hold values from 0 to 15; in each aligned block of 128 rows (0 to 127, 128 to 255, ...) at most 10 rows name the same one
- row_offset: int32 [4096], P(('band', 'tile')), parts along dimension 0, may hold values from 0 to 7
- col_offset: int32 [4096], P(('band', 'tile')), parts along dimension 0, may hold values from 0 to 3
- psf_model: int32 [4096], P(('band', 'tile')), parts along dimension 0, may hold values from 0 to 17
- psf_rows: float32 [36, 3, 15], P('band'), parts along dimension 0, may hold values from -1.5 to 1.5
- psf_cols: float32 [36, 3, 15], P('band'), parts along dimension 0, may hold values from -1.5 to 1.5
- cotangent: bfloat16 [8192, 512], P(('band', 'tile')), parts along dimension 0, may hold values from -6 to 6
Outputs:
- tile_image: bfloat16 [8192, 512], P(('band', 'tile')), parts along dimension 0
- stamp_grad: bfloat16 [4096, 64, 128], P(('band', 'tile')), parts along dimension 0
The draws below stay inside these ranges and needn't reach their ends.
There are 2 independent parts, one for each index of `band`. The reference program is written for one: setup_inputs(seed, part) draws one part's arguments, and reference() takes and returns one part's arrays. A program takes and returns all parts, laid end to end along the dimension named above; each array names one. Nothing has to cross between parts.
Inputs may be any that keep to these rules, and one draw needn't show every extreme that they name: `tile_of`: at most 10 of the stamps of one device lie on one tile, and in every draw some device places exactly 10 stamps on some tile.
All inputs are finite; a program needn't handle non-finite values.
Results may differ from the reference program's by a relative error of at most 0.007.
Values may be sent and summed in bfloat16 or wider, within the bound.
A program may use at most 128 MiB of HBM per device.

```python
import math
import jax
import jax.numpy as jnp
import numpy as np
from jax import lax

SY = 64
SX = 128
KW = 15
TERMS = 3
NPSF = 18
STAMPS = 128
TY = 256
TX = 512
BY = 32
NTILES = 16
STAMPS_ALL = 2048
SKY = 4096
CAP = 10


def touch_ends(drawn, stream_key, low, largest):
    longest = drawn.shape.index(max(drawn.shape))
    spots = []
    for shift in (0, 1):
        where = [jax.random.randint(jax.random.fold_in(stream_key, axis), (), 0, length) for axis, length in enumerate(drawn.shape)]
        where[longest] = (where[longest] + shift) % drawn.shape[longest]
        spots.append(tuple(where))
    return drawn.at[spots[0]].set(low).at[spots[1]].set(largest)


def steps_of(own_key, extent, shards, low, largest):
    def one(dim, shards_of):
        steps = jax.random.uniform(jax.random.fold_in(jax.random.fold_in(own_key, 6), dim), (shards_of,), jnp.float32, low / len(shards), largest / len(shards))
        return jnp.repeat(jnp.exp(steps), extent[dim] // shards_of).reshape((-1,) + (1,) * (len(extent) - dim - 1))

    factor_of = one(*shards[0])
    for cut in shards[1:]:
        factor_of = factor_of * one(*cut)
    return factor_of


def shared_out(key, own, number, rows, number_of, top, limit, skew):
    order = jax.random.permutation(key, number_of)
    packed, ordinary = load_shares(number_of, rows * top, limit, skew, True), load_shares(number_of, rows * top, limit, skew, False)
    places = jnp.arange(number_of)

    def named(tallies, rotation):
        used = int((tallies > 0).sum())
        fixed = max(1, used // 4)
        shifted = fixed + (places - fixed + rotation * (used - fixed)) % max(1, number_of - fixed)
        return jnp.zeros((number_of,), jnp.int32).at[order[jnp.where(places < fixed, places, shifted)]].set(jnp.asarray(tallies, jnp.int32))

    tallies = jnp.where(number % 4 == 0, named(packed, number // 4), named(ordinary, number - number // 4 - 1))
    mixed = jax.random.permutation(jax.random.fold_in(own, 3), number_of)
    source_of, sink = mixed[0:number_of // 2 * 2:2], mixed[1:number_of // 2 * 2:2]
    room = jnp.minimum(tallies[source_of] - 1, limit - tallies[sink]) // 2
    room = jnp.where((source_of == order[0]) | (sink == order[0]) | (tallies[sink] == 0), 0, jnp.maximum(room, 0))
    shifted = jax.random.randint(jax.random.fold_in(own, 4), (number_of // 2,), 0, 1 << 20) % (room + 1)
    tallies = tallies.at[source_of].add(-shifted).at[sink].add(shifted)
    members = jnp.searchsorted(jnp.cumsum(tallies), jnp.arange(rows * top), side="right").astype(jnp.int32)
    grid = members.reshape(top, rows).T
    grid = grid[jax.random.permutation(jax.random.fold_in(own, 1), rows)]
    rotation = jax.random.randint(jax.random.fold_in(own, 2), (rows, 1), 0, top)
    return jnp.take_along_axis(grid, (jnp.arange(top)[None, :] + rotation) % top, axis=1)


def load_shares(amount, total, reach, skew, full):
    loads = [(1 << 20) // math.isqrt(standing ** skew) + 1 for standing in range(1, amount + 1)]
    largest = reach if full else min(reach, max(-(-total // amount), total * loads[0] // sum(loads)))
    least = 1 if total - largest >= amount - 1 else 0
    holding, rest = [largest] + [least] * (amount - 1), total - largest - least * (amount - 1)
    while rest > 0:
        movable = [i for i in range(1, amount) if holding[i] < largest] or [i for i in range(1, amount) if holding[i] < reach]
        whole, budget = sum([loads[i] for i in movable]), rest
        for i in movable:
            extra = min(reach - holding[i], max(1, budget * loads[i] // whole), rest)
            holding[i] = holding[i] + extra
            rest = rest - extra
    return np.array(holding)


def normal_values(stream_key, dims, spread, reach, cuts=(), kind=jnp.bfloat16):
    array = spread * jax.random.normal(stream_key, dims, jnp.float32)
    if cuts:
        array = array * steps_of(stream_key, dims, cuts, -0.22, 0.18)
    return jnp.clip(array, -reach, reach).astype(kind)


def setup_inputs(seed: int = 0, part: int = 0) -> dict:
    arg_keys = jax.random.split(jax.random.key(seed), 9)
    part_keys = jax.random.split(jax.random.fold_in(arg_keys[8], part), 9)
    stamps = normal_values(part_keys[0], (STAMPS_ALL, SY, SX), 1.0, 6.0, ((0, 16),))
    tile_of_keys = jax.random.split(jax.random.fold_in(part_keys[1], 1), STAMPS_ALL // STAMPS)
    tile_of_turns = jax.random.permutation(jax.random.fold_in(part_keys[1], 3), STAMPS_ALL // STAMPS)
    tile_of = jax.vmap(lambda own, number: shared_out(jax.random.fold_in(part_keys[1], 2), own, number, STAMPS, NTILES, 1, CAP, 1))(tile_of_keys, tile_of_turns).reshape((STAMPS_ALL, 1))
    row_offset = touch_ends(jax.random.randint(part_keys[2], (STAMPS_ALL,), 0, TY // BY), jax.random.fold_in(part_keys[2], 1), 0, (TY // BY) - 1).astype(jnp.int32)
    col_offset = touch_ends(jax.random.randint(part_keys[3], (STAMPS_ALL,), 0, TX // SX), jax.random.fold_in(part_keys[3], 1), 0, (TX // SX) - 1).astype(jnp.int32)
    psf_model = touch_ends(jax.random.randint(part_keys[4], (STAMPS_ALL,), 0, NPSF), jax.random.fold_in(part_keys[4], 1), 0, NPSF - 1).astype(jnp.int32)
    psf_rows = normal_values(part_keys[5], (NPSF, TERMS, KW), KW ** -0.5, 1.5, (), jnp.float32)
    psf_cols = normal_values(part_keys[6], (NPSF, TERMS, KW), KW ** -0.5, 1.5, (), jnp.float32)
    cotangent = normal_values(part_keys[7], (SKY, TX), 1.0, 6.0, ((0, 16),))
    return dict(stamps=stamps, tile_of=tile_of, row_offset=row_offset, col_offset=col_offset, psf_model=psf_model, psf_rows=psf_rows, psf_cols=psf_cols, cotangent=cotangent)


def operators(profiles, size):
    half_width = (KW - 1) // 2
    places = jnp.arange(size, dtype=jnp.int32)
    offsets = places[None, :] - places[:, None] + half_width
    inside = (offsets >= 0) & (offsets < KW)
    tap_values = jnp.take(profiles, jnp.clip(offsets, 0, KW - 1), axis=2)
    return jnp.where(inside, tap_values, jnp.zeros_like(tap_values)).astype(jnp.bfloat16)


def convolve_block(images, models, row_ops, col_ops):
    row_mats = row_ops[models].astype(jnp.float32)
    col_mats = col_ops[models].astype(jnp.float32)
    row_pass = jnp.einsum("bkij,bjx->bkix", row_mats, images.astype(jnp.float32)).astype(jnp.bfloat16)
    return jnp.einsum("bkix,bkyx->biy", row_pass.astype(jnp.float32), col_mats).astype(jnp.bfloat16)


def transpose_block(windows, models, row_ops, col_ops):
    row_mats = row_ops[models].astype(jnp.float32)
    col_mats = col_ops[models].astype(jnp.float32)
    back_pass = jnp.einsum("biy,bkyx->bkix", windows.astype(jnp.float32), col_mats).astype(jnp.bfloat16)
    return jnp.einsum("bkji,bkjx->bix", row_mats, back_pass.astype(jnp.float32)).astype(jnp.bfloat16)


def reference(stamps, tile_of, row_offset, col_offset, psf_model, psf_rows, psf_cols, cotangent):
    row_ops = operators(psf_rows, SY)
    col_ops = operators(psf_cols, SX)
    grouped_models = psf_model.reshape(NTILES, STAMPS)

    def forward_group(inputs):
        return convolve_block(inputs[0], inputs[1], row_ops, col_ops)

    convolved = lax.map(forward_group, (stamps.reshape(NTILES, STAMPS, SY, SX), grouped_models))
    convolved = convolved.reshape(STAMPS_ALL, SY, SX)
    row_blocks = TY // BY
    col_blocks = TX // SX
    upper_block = tile_of[:, 0] * row_blocks + row_offset
    block_ids = (jnp.stack([upper_block, upper_block + 1], axis=1) * col_blocks + col_offset[:, None]).astype(jnp.int32)
    block_count = (NTILES * row_blocks + 1) * col_blocks
    pieces = convolved.reshape(STAMPS_ALL * 2, BY * SX).astype(jnp.float32)
    summed = jax.ops.segment_sum(pieces, block_ids.reshape(-1), num_segments=block_count)
    sky_rows = summed.reshape(NTILES * row_blocks + 1, col_blocks, BY, SX).transpose(0, 2, 1, 3)
    sky_rows = sky_rows.reshape((NTILES * row_blocks + 1) * BY, TX)
    tile_image = sky_rows[: NTILES * TY].astype(jnp.bfloat16)
    padded = jnp.concatenate([cotangent, jnp.zeros((BY, TX), cotangent.dtype)], axis=0)
    blocks = padded.reshape(NTILES * row_blocks + 1, BY, col_blocks, SX).transpose(0, 2, 1, 3)
    blocks = blocks.reshape(block_count, BY * SX)
    windows = blocks[block_ids.reshape(-1)].reshape(NTILES, STAMPS, SY, SX)

    def backward_group(inputs):
        return transpose_block(inputs[0], inputs[1], row_ops, col_ops)

    gradients = lax.map(backward_group, (windows, grouped_models)).reshape(STAMPS_ALL, SY, SX)
    return tile_image, gradients
```

```python
from functools import partial

import jax
import jax.numpy as jnp
from jax import lax
from jax.experimental import pallas as pl
from jax.experimental.pallas import tpu as pltpu
from jax.sharding import PartitionSpec as P


def passed_along(array, axis, by):
    peers = lax.axis_size(axis)
    pairs = [(i, i + by) for i in range(peers) if 0 <= i + by < peers]
    return lax.ppermute(array, axis, pairs)


def for_sending(array):

    def short(part):
        return part.astype(jnp.bfloat16) if part.dtype == jnp.float32 else part

    return jax.tree.map(short, array)


def band_table(taps_count, size):
    half_width = (taps_count - 1) // 2
    places = jnp.arange(size, dtype=jnp.int32)
    offsets = places[None, :] - places[:, None] + half_width
    taps_index = jnp.arange(taps_count, dtype=jnp.int32)
    table = (offsets[None, :, :] == taps_index[:, None, None]).astype(jnp.float32)
    return table.reshape((taps_count, size * size))


def build_ops(profiles, size):
    model_total, term_total, taps_count = profiles.shape
    table = band_table(taps_count, size)
    mats = jnp.dot(
        profiles.reshape((model_total * term_total, taps_count)),
        table,
        precision=lax.Precision.HIGHEST,
    )
    return mats.reshape((model_total, term_total, size, size)).astype(jnp.bfloat16)


def chosen(ops, models):
    model_total, term_total, size, _ = ops.shape
    picks = (models[:, None] == jnp.arange(model_total, dtype=jnp.int32)[None, :]).astype(ops.dtype)
    mats = jnp.dot(picks, ops.reshape((model_total, -1)), preferred_element_type=jnp.float32)
    return mats.astype(ops.dtype).reshape((models.shape[0], term_total, size, size))


def convolve_some(images, row_mats, col_mats):
    row_pass = jnp.einsum(
        "bkij,bjx->bkix", row_mats, images, preferred_element_type=jnp.float32
    ).astype(jnp.bfloat16)
    return jnp.einsum(
        "bkix,bkyx->biy", row_pass, col_mats, preferred_element_type=jnp.float32
    ).astype(jnp.bfloat16)


def transpose_some(windows, row_mats, col_mats):
    back_pass = jnp.einsum(
        "biy,bkyx->bkix", windows, col_mats, preferred_element_type=jnp.float32
    ).astype(jnp.bfloat16)
    return jnp.einsum(
        "bkji,bkjx->bix", row_mats, back_pass, preferred_element_type=jnp.float32
    ).astype(jnp.bfloat16)


def apply_all(function, images, models, row_ops, col_ops):
    batch = divisor(images.shape[0], 32)

    def some(inputs):
        part, part_models = inputs
        return function(part, chosen(row_ops, part_models), chosen(col_ops, part_models))

    cut = images.reshape((-1, batch) + images.shape[1:])
    return lax.map(some, (cut, models.astype(jnp.int32).reshape((-1, batch)))).reshape(images.shape)


def per_device(stamps, tile_of, row_offset, col_offset, psf_model, psf_rows, psf_cols, cotangent):
    peer_count = lax.axis_size("tile")
    stamp_count, stamp_rows, stamp_cols = stamps.shape
    block_rows = stamp_rows // 2
    tile_rows, tile_cols = cotangent.shape
    row_blocks = tile_rows // block_rows
    col_blocks = tile_cols // stamp_cols
    capacity = max(2, (5 * stamp_count + 4 * peer_count - 1) // (4 * peer_count))
    slot_total = peer_count * capacity
    row_ops = build_ops(psf_rows, stamp_rows)
    col_ops = build_ops(psf_cols, stamp_cols)
    target = tile_of[:, 0]
    order = jnp.arange(stamp_count, dtype=jnp.int32)
    earlier = (target[None, :] == target[:, None]) & (order[None, :] < order[:, None])
    slots = target * capacity + jnp.sum(earlier.astype(jnp.int32), axis=1)
    slot_ids = jnp.arange(slot_total, dtype=jnp.int32)
    matches = slots[None, :] == slot_ids[:, None]
    place = matches.astype(jnp.bfloat16)
    details = jnp.stack([jnp.ones_like(target), row_offset, col_offset, psf_model], axis=1)
    detail_send = jnp.sum(jnp.where(matches[:, :, None], details[None, :, :], 0), axis=1)
    detail_send = detail_send.reshape(peer_count, capacity, 4)
    raw_send = jnp.dot(
        place,
        stamps.reshape((stamp_count, stamp_rows * stamp_cols)),
        preferred_element_type=jnp.float32,
    )
    raw_send = raw_send.astype(jnp.bfloat16).reshape(peer_count, capacity, stamp_rows, stamp_cols)
    raw_part = lax.all_to_all(raw_send, "tile", split_axis=0, concat_axis=0, tiled=True)
    info_part = lax.all_to_all(detail_send, "tile", split_axis=0, concat_axis=0, tiled=True)
    flat = raw_part.reshape((-1, stamp_rows, stamp_cols))
    result = apply_all(convolve_some, flat, info_part.reshape((-1, 4))[:, 3], row_ops, col_ops)
    received = result.reshape(raw_part.shape)
    info_flat = info_part.reshape((slot_total, 4))
    upper_block = info_flat[:, 1]
    block_ids = jnp.stack([upper_block, upper_block + 1], axis=1) * col_blocks + info_flat[:, 2:3]
    targets = jnp.arange((row_blocks + 1) * col_blocks, dtype=jnp.int32)
    placing = (block_ids.reshape(-1)[None, :] == targets[:, None]).astype(jnp.bfloat16)
    pieces = received.reshape((slot_total * 2, block_rows * stamp_cols))
    extended = jnp.dot(placing, pieces, preferred_element_type=jnp.float32)
    extended = extended.reshape(row_blocks + 1, col_blocks, block_rows, stamp_cols).transpose(
        0, 2, 1, 3
    )
    extended = extended.reshape((row_blocks + 1) * block_rows, tile_cols)
    arriving = passed_along(extended[tile_rows:].astype(jnp.bfloat16), "tile", 1).astype(
        jnp.float32
    )
    tile_sum = extended[:tile_rows].at[:block_rows].add(arriving)
    tile_image = tile_sum.astype(jnp.bfloat16)
    rim = passed_along(cotangent[:block_rows], "tile", -1)
    padded = jnp.concatenate([cotangent, rim], axis=0)
    blocks = padded.reshape(row_blocks + 1, block_rows, col_blocks, stamp_cols).transpose(
        0, 2, 1, 3
    )
    blocks = blocks.reshape((row_blocks + 1) * col_blocks, block_rows * stamp_cols)
    windows = lax.dot_general(
        placing, blocks, (((0,), (0,)), ((), ())), preferred_element_type=jnp.float32
    )
    windows = windows.astype(jnp.bfloat16).reshape(slot_total, stamp_rows, stamp_cols)
    slot_grads = apply_all(transpose_some, windows, info_flat[:, 3], row_ops, col_ops)
    slot_grads = slot_grads.reshape(peer_count, capacity, stamp_rows, stamp_cols)
    returned = lax.all_to_all(
        for_sending(slot_grads), "tile", split_axis=0, concat_axis=0, tiled=True
    ).astype(slot_grads.dtype)
    stamp_grad = lax.dot_general(
        place,
        returned.reshape((slot_total, stamp_rows * stamp_cols)),
        (((0,), (0,)), ((), ())),
        preferred_element_type=jnp.float32,
    )
    stamp_grad = stamp_grad.astype(jnp.bfloat16).reshape(stamp_count, stamp_rows, stamp_cols)
    return (tile_image, stamp_grad)


MESH = pl.DeviceIdType.MESH


def band_matrix(taps, lanes):
    count = taps.shape[1]
    half = (count - 1) // 2
    row = jnp.concatenate([taps, jnp.zeros((1, lanes - count), jnp.float32)], axis=1)
    spread = jnp.broadcast_to(row, (lanes, lanes))
    turned = pltpu.roll(spread, lanes - half, 1, stride=1, stride_axis=0)
    down = lax.broadcasted_iota(jnp.int32, (lanes, lanes), 0)
    across = lax.broadcasted_iota(jnp.int32, (lanes, lanes), 1)
    return jnp.where(jnp.abs(across - down) <= half, turned, 0.0)


def build_bands(taps_ref, row_fwd, row_bwd, col_fwd, col_bwd):
    models, terms = taps_ref.shape[0] // 2, taps_ref.shape[1]
    size = row_bwd.shape[1]
    lanes = col_bwd.shape[1]

    def build(m, carry):
        taps_rows, taps_cols = taps_ref[m], taps_ref[models + m]
        turned = []
        for k in range(terms):
            mat = band_matrix(taps_rows[k:k + 1], lanes)
            row_fwd[m, k * size:(k + 1) * size, :] = mat[:size, :size].astype(jnp.bfloat16)
            turned.append(mat.T[:size, :size].astype(jnp.bfloat16))
            mat = band_matrix(taps_cols[k:k + 1], lanes)
            col_bwd[m, :, k * lanes:(k + 1) * lanes] = mat.astype(jnp.bfloat16)
            col_fwd[m, k * lanes:(k + 1) * lanes, :] = mat.T.astype(jnp.bfloat16)
        row_bwd[m] = jnp.concatenate(turned, axis=1)
        return carry

    lax.fori_loop(0, models, build, 0)


def into_blocks(cot_ref, blocks_ref):
    block_count, block_rows, stamp_cols = blocks_ref.shape
    across = cot_ref.shape[1] // stamp_cols
    for b in range(block_count):
        top, left = b // across * block_rows, b % across * stamp_cols
        blocks_ref[b] = cot_ref[top:top + block_rows, left:left + stamp_cols]


def add_kernel(model_bits, col_blocks, group, codes, conv_ref, strip_ref, total):
    count, stamp_rows, stamp_cols = conv_ref.shape
    block_rows = stamp_rows // 2
    strip_rows = strip_ref.shape[0]

    def clear(i, carry):
        spot = pl.ds(pl.multiple_of(i * block_rows, block_rows), block_rows)
        total[spot, :] = jnp.zeros((block_rows, total.shape[1]), jnp.float32)
        return carry

    lax.fori_loop(0, total.shape[0] // block_rows, clear, 0)

    def some(g, carry):
        for u in range(group):
            block = codes[g * group + u] >> model_bits
            top = pl.multiple_of((block // col_blocks) * block_rows, block_rows)
            left = pl.multiple_of((block % col_blocks) * stamp_cols, stamp_cols)
            spot = (pl.ds(top, stamp_rows), pl.ds(left, stamp_cols))
            total[spot] = total[spot] + conv_ref[g * group + u].astype(jnp.float32)
        return carry

    lax.fori_loop(0, count // group, some, 0)

    def put(i, carry):
        spot = pl.ds(pl.multiple_of(i * block_rows, block_rows), block_rows)
        strip_ref[spot, :] = total[spot, :].astype(jnp.bfloat16)
        return carry

    lax.fori_loop(0, strip_rows // block_rows, put, 0)


class Place:
    def __init__(self, peers):
        self.planes = peers // 4
        self.me = lax.axis_index("tile")
        self.core = lax.rem(self.me, 2)
        self.row = lax.rem(self.me // 2, 2)
        self.plane = self.me // 4

    def at(self, shift=0, row=0, core=0):
        plane = lax.rem(self.plane + shift + self.planes, self.planes)
        y = 1 - self.row if row else self.row
        c = 1 - self.core if core else self.core
        return plane * 4 + y * 2 + c

    def greet(self):
        barrier = pltpu.get_barrier_semaphore()
        others = [self.at(d) for d in range(1, self.planes)] + [self.at(row=1), self.at(core=1)]
        for other in others:
            pl.semaphore_signal(barrier, inc=1, device_id={"tile": other}, device_id_type=MESH)
        pl.semaphore_wait(barrier, len(others))


def remote(src, dst, send, recv, device):
    return pltpu.make_async_remote_copy(src_ref=src, dst_ref=dst, send_sem=send, recv_sem=recv,
                                        device_id={"tile": device}, device_id_type=MESH)


def forward_kernel(peers, terms, model_bits, group, codes, taps_ref, stamps_hbm, pixels_ref,
                   conv_ref, sky, row_bwd, col_bwd, row_ops, col_ops, stamps_ref, cot_ref,
                   stamps_sem, own_sem, z_send, z_recv, y_send, y_recv, c_send, c_recv):
    place = Place(peers)
    planes = place.planes
    count, stamp_rows, stamp_cols = stamps_ref.shape
    groups = count // group

    def some(g, carry):
        models = [codes[g * group + u] & ((1 << model_bits) - 1) for u in range(group)]
        firsts = [jnp.dot(row_ops[models[u]], stamps_ref[g * group + u],
                          preferred_element_type=jnp.float32).astype(jnp.bfloat16)
                  for u in range(group)]
        for u in range(group):
            wide = jnp.concatenate(
                [firsts[u][k * stamp_rows:(k + 1) * stamp_rows] for k in range(terms)], axis=1)
            conv_ref[g * group + u] = jnp.dot(
                wide, col_ops[models[u]], preferred_element_type=jnp.float32).astype(jnp.bfloat16)
        return carry

    reached = [0]

    def compute(share):
        stop = min(groups, reached[0] + share)
        if stop > reached[0]:
            lax.fori_loop(reached[0], stop, some, 0)
        reached[0] = stop

    fetch = pltpu.make_async_copy(stamps_hbm, stamps_ref, stamps_sem)
    fetch.start()
    into_blocks(pixels_ref, cot_ref)
    sky[peers] = jnp.zeros(sky.shape[1:], jnp.bfloat16)
    place.greet()
    own = pltpu.make_async_copy(cot_ref, sky.at[place.me], own_sem)
    own.start()
    p = place.plane
    last = planes - 1

    def z_copy(tile, source, slot, step):
        return remote(source, sky.at[tile], z_send.at[slot], z_recv.at[slot], place.at(step))

    def y_copy(tile, source, slot):
        return remote(source, sky.at[tile], y_send.at[slot], y_recv.at[slot], place.at(row=1))

    def c_copy(tile, source, slot):
        return remote(source, sky.at[tile], c_send.at[slot], c_recv.at[slot], place.at(core=1))

    def streams(i, body):
        pl.when(p >= i)(lambda: body(-i, i, 1, p < last))
        pl.when(p + i <= last)(lambda: body(i, last + i, -1, p > 0))

    pl.when(p < last)(lambda: z_copy(place.me, cot_ref, 1, 1).start())
    pl.when(p > 0)(lambda: z_copy(place.me, cot_ref, last + 1, -1).start())
    y_copy(place.me, cot_ref, 0).start()
    c_copy(place.me, cot_ref, 0).start()
    build_bands(taps_ref, row_ops, row_bwd, col_ops, col_bwd)
    fetch.wait()
    compute(groups // 8)
    for i in range(1, planes):

        def arrived(shift, slot, step, more):
            tile = place.at(shift)
            source = sky.at[tile]
            z_copy(tile, source, slot, step).wait_recv()
            if i < last:
                pl.when(more)(lambda: z_copy(tile, source, slot + 1, step).start())
            y_copy(tile, source, slot).start()
            c_copy(tile, source, slot).start()

        streams(i, arrived)
        compute(groups * 3 // 8 if i < last else groups)

    half = 2 * last + 1

    def crossed(shift, slot):
        tile = place.at(shift, row=1)
        y_copy(tile, sky.at[tile], slot).wait_recv()
        c_copy(tile, sky.at[tile], half + slot).start()

    def finished(shift, slot):
        for row in range(2):
            tile = place.at(shift, row=row, core=1)
            c_copy(tile, sky.at[tile], row * half + slot).wait_recv()
            c_copy(tile, sky.at[tile], row * half + slot).wait_send()
        y_copy(tile, sky.at[tile], slot).wait_send()

    crossed(0, 0)
    for i in range(1, planes):
        streams(i, lambda shift, slot, step, more: crossed(shift, slot))
    finished(0, 0)
    own.wait()
    pl.when(p < last)(lambda: z_copy(place.me, cot_ref, 1, 1).wait_send())
    pl.when(p > 0)(lambda: z_copy(place.me, cot_ref, last + 1, -1).wait_send())
    for i in range(1, planes):

        def ended(shift, slot, step, more):
            finished(shift, slot)
            if i < last:
                tile = place.at(shift)
                pl.when(more)(lambda: z_copy(tile, sky.at[tile], slot + 1, step).wait_send())

        streams(i, ended)


def backward_kernel(peers, terms, model_bits, col_blocks, group, codes, row_ops, col_ops, sky,
                    strip, grads_ref, tile_ref, from_c, out_y, from_y, out_z, from_z,
                    z_send, z_recv, y_send, y_recv, c_send, c_recv):
    place = Place(peers)
    planes = place.planes
    count, stamp_rows, stamp_cols = grads_ref.shape
    groups = count // group
    block_rows = stamp_rows // 2
    tile_rows = tile_ref.shape[0]

    def some(g, carry):
        firsts, models = [], []
        for u in range(group):
            code = codes[g * group + u]
            model = code & ((1 << model_bits) - 1)
            block = code >> model_bits
            window = jnp.concatenate([sky[block], sky[block + col_blocks]], axis=0)
            models.append(model)
            firsts.append(jnp.dot(window, col_ops[model],
                                  preferred_element_type=jnp.float32).astype(jnp.bfloat16))
        for u in range(group):
            tall = jnp.concatenate(
                [firsts[u][:, k * stamp_cols:(k + 1) * stamp_cols] for k in range(terms)], axis=0)
            grads_ref[g * group + u] = jnp.dot(
                row_ops[models[u]], tall, preferred_element_type=jnp.float32).astype(jnp.bfloat16)
        return carry

    reached = [0]

    def compute(share):
        stop = min(groups, reached[0] + share)
        if stop > reached[0]:
            lax.fori_loop(reached[0], stop, some, 0)
        reached[0] = stop

    def summed(store, *parts):
        def body(i, carry):
            spot = pl.ds(pl.multiple_of(i * block_rows, block_rows), block_rows)
            out = parts[0][0][parts[0][1], spot, :].astype(jnp.float32)
            for ref, index in parts[1:]:
                out = out + ref[index, spot, :].astype(jnp.float32)
            store(spot, out.astype(jnp.bfloat16))
            return carry

        lax.fori_loop(0, tile_rows // block_rows, body, 0)

    place.greet()
    p = place.plane
    last = planes - 1
    upper = p // 2
    mirrored = (1 - 2 * upper) * p + last * upper
    targets = [last * upper + (1 - 2 * upper) * q for q in (3, 2, 1 - mirrored, mirrored)]
    shifts = [q - p for q in targets]
    to_c, to_y = [], []
    for e in range(2 * planes):
        far = 1 if e < planes else 0
        source = strip.at[place.at(shifts[e % planes], row=far, core=1)]
        to_c.append(remote(source, from_c.at[e], c_send.at[e], c_recv.at[e], place.at(core=1)))
        to_c[-1].start()
    for i in range(planes):
        to_c[i].wait_recv()

        def keep(spot, value, i=i):
            out_y[i, spot, :] = value

        summed(keep, (strip, place.at(shifts[i], row=1)), (from_c, i))
        to_y.append(remote(out_y.at[i], from_y.at[i], y_send.at[i], y_recv.at[i], place.at(row=1)))
        to_y[-1].start()
    compute(groups * 3 // 8)

    def z_copy(i, slot, step):
        return remote(out_z.at[i], from_z.at[slot], z_send.at[i], z_recv.at[slot], place.at(step))

    for i in range(last):
        to_c[planes + i].wait_recv()
        to_y[i].wait_recv()
        target = targets[i]
        parts = [(strip, place.at(shifts[i])), (from_c, planes + i), (from_y, i)]

        def keep(spot, value):
            out_z[i, spot, :] = value

        def pass_on(slot, step, first):
            @pl.when(first)
            def _():
                summed(keep, *parts)

            @pl.when(jnp.logical_not(first))
            def _():
                z_copy(i, slot, step).wait_recv()
                summed(keep, *parts, (from_z, slot))

            z_copy(i, slot, step).start()

        pl.when(target > p)(lambda: pass_on(target, 1, p == 0))
        pl.when(target < p)(lambda: pass_on(planes + target, -1, p == last))
        compute(groups * 2 // 8)
    compute(groups)
    to_c[2 * planes - 1].wait_recv()
    to_y[last].wait_recv()
    parts = [(strip, place.me), (from_c, 2 * planes - 1), (from_y, last)]

    def finish(*slots):
        for slot in slots:
            z_copy(0, slot, 1).wait_recv()

        def keep(spot, value):
            tile_ref[spot, :] = value

        summed(keep, *parts, *[(from_z, slot) for slot in slots])

    pl.when(p == 0)(lambda: finish(planes + p))
    pl.when(p == last)(lambda: finish(p))
    pl.when(jnp.logical_and(p > 0, p < last))(lambda: finish(p, planes + p))
    for copy in to_c + to_y:
        copy.wait_send()
    for i in range(last):
        z_copy(i, i, 1).wait_send()


def divisor(number, wanted):
    return max(d for d in range(1, wanted + 1) if number % d == 0)


def in_place(stamps, tile_of, row_offset, col_offset, psf_model, psf_rows, psf_cols, cotangent):
    peers = lax.axis_size("tile")
    planes = peers // 4
    stamp_count, stamp_rows, stamp_cols = stamps.shape
    models, terms, taps = psf_rows.shape
    block_rows = stamp_rows // 2
    tile_rows, tile_cols = cotangent.shape
    row_blocks = tile_rows // block_rows
    col_blocks = tile_cols // stamp_cols
    strip_rows = peers * tile_rows
    model_bits = max(1, (models - 1).bit_length())
    upper = tile_of[:, 0] * row_blocks + row_offset
    codes = ((upper * col_blocks + col_offset) << model_bits) + psf_model
    group = divisor(stamp_count, 16)
    flops = 2 * stamp_count * terms * stamp_rows * stamp_cols * (stamp_rows + stamp_cols)
    cost = pl.CostEstimate(flops=8 * flops, bytes_accessed=40 << 20, transcendentals=0)
    smem = pl.BlockSpec(memory_space=pltpu.SMEM)
    vmem = pl.BlockSpec(memory_space=pltpu.VMEM)
    anywhere = pl.BlockSpec(memory_space=pl.ANY)
    short = jnp.bfloat16
    dma = pltpu.SemaphoreType.DMA
    limit = 44 << 20
    block_shape = (row_blocks * col_blocks, block_rows, stamp_cols)

    conv, sky, row_bwd, col_bwd = pl.pallas_call(
        partial(forward_kernel, peers, terms, model_bits, group),
        out_shape=(
            jax.ShapeDtypeStruct(stamps.shape, short),
            jax.ShapeDtypeStruct((peers + 1,) + block_shape, short),
            jax.ShapeDtypeStruct((models, stamp_rows, terms * stamp_rows), short),
            jax.ShapeDtypeStruct((models, stamp_cols, terms * stamp_cols), short),
        ),
        in_specs=[smem, vmem, anywhere, vmem],
        out_specs=(vmem,) * 4,
        scratch_shapes=[
            pltpu.VMEM((models, terms * stamp_rows, stamp_rows), short),
            pltpu.VMEM((models, terms * stamp_cols, stamp_cols), short),
            pltpu.VMEM(stamps.shape, short),
            pltpu.VMEM(block_shape, short),
        ] + [dma, dma] + [dma((2 * planes - 1,))] * 4 + [dma((4 * planes - 2,))] * 2,
        compiler_params=pltpu.CompilerParams(collective_id=0, has_side_effects=True,
                                             vmem_limit_bytes=limit),
        cost_estimate=cost,
    )(codes, jnp.concatenate([psf_rows, psf_cols], axis=0), stamps, cotangent)
    strip = pl.pallas_call(
        partial(add_kernel, model_bits, col_blocks, group),
        out_shape=jax.ShapeDtypeStruct((strip_rows, tile_cols), short),
        in_specs=[smem, vmem],
        out_specs=vmem,
        scratch_shapes=[pltpu.VMEM((strip_rows + block_rows, tile_cols), jnp.float32)],
        compiler_params=pltpu.CompilerParams(vmem_limit_bytes=limit),
    )(codes, conv)
    tile = (tile_rows, tile_cols)
    stamp_grad, tile_image = pl.pallas_call(
        partial(backward_kernel, peers, terms, model_bits, col_blocks, group),
        out_shape=(
            jax.ShapeDtypeStruct(stamps.shape, short),
            jax.ShapeDtypeStruct(tile, short),
        ),
        in_specs=[smem, vmem, vmem, vmem, vmem],
        out_specs=(vmem, vmem),
        scratch_shapes=[
            pltpu.VMEM((2 * planes,) + tile, short),
            pltpu.VMEM((planes,) + tile, short),
            pltpu.VMEM((planes,) + tile, short),
            pltpu.VMEM((planes,) + tile, short),
            pltpu.VMEM((2 * planes,) + tile, short),
            dma((planes,)), dma((2 * planes,)), dma((planes,)), dma((planes,)),
            dma((2 * planes,)), dma((2 * planes,)),
        ],
        compiler_params=pltpu.CompilerParams(collective_id=1, has_side_effects=True,
                                             vmem_limit_bytes=limit),
        cost_estimate=cost,
    )(codes, row_bwd, col_bwd, sky.reshape((-1,) + block_shape[1:]),
      strip.reshape((peers,) + tile))
    return tile_image, stamp_grad


def strip_fits(peers, cotangent):
    rows, cols = cotangent.shape
    return peers == 16 and peers * rows * cols * 4 <= 12 << 20


def per_device_any(*args):
    if strip_fits(lax.axis_size("tile"), args[-1]):
        return in_place(*args)
    return per_device(*args)


def solution(mesh):
    in_specs = (
        P(("band", "tile"), None, None),
        P(("band", "tile"), None),
        P(("band", "tile")),
        P(("band", "tile")),
        P(("band", "tile")),
        P("band", None, None),
        P("band", None, None),
        P(("band", "tile"), None),
    )
    out_specs = (P(("band", "tile"), None), P(("band", "tile"), None, None))
    return jax.shard_map(
        per_device_any, mesh=mesh, in_specs=in_specs, out_specs=out_specs, check_vma=False
    )
```

```python
from functools import partial

import jax
import jax.numpy as jnp
from jax import lax
from jax.experimental import pallas as pl
from jax.experimental.pallas import tpu as pltpu
from jax.sharding import PartitionSpec as P


def passed_along(array, axis, by):
    peers = lax.axis_size(axis)
    pairs = [(i, i + by) for i in range(peers) if 0 <= i + by < peers]
    return lax.ppermute(array, axis, pairs)


def for_sending(array):

    def short(part):
        return part.astype(jnp.bfloat16) if part.dtype == jnp.float32 else part

    return jax.tree.map(short, array)


def band_table(taps_count, size):
    half_width = (taps_count - 1) // 2
    places = jnp.arange(size, dtype=jnp.int32)
    offsets = places[None, :] - places[:, None] + half_width
    taps_index = jnp.arange(taps_count, dtype=jnp.int32)
    table = (offsets[None, :, :] == taps_index[:, None, None]).astype(jnp.float32)
    return table.reshape((taps_count, size * size))


def build_ops(profiles, size):
    model_total, term_total, taps_count = profiles.shape
    table = band_table(taps_count, size)
    mats = jnp.dot(
        profiles.reshape((model_total * term_total, taps_count)),
        table,
        precision=lax.Precision.HIGHEST,
    )
    return mats.reshape((model_total, term_total, size, size)).astype(jnp.bfloat16)


def chosen(ops, models):
    model_total, term_total, size, _ = ops.shape
    picks = (models[:, None] == jnp.arange(model_total, dtype=jnp.int32)[None, :]).astype(ops.dtype)
    mats = jnp.dot(picks, ops.reshape((model_total, -1)), preferred_element_type=jnp.float32)
    return mats.astype(ops.dtype).reshape((models.shape[0], term_total, size, size))


def convolve_some(images, row_mats, col_mats):
    row_pass = jnp.einsum(
        "bkij,bjx->bkix", row_mats, images, preferred_element_type=jnp.float32
    ).astype(jnp.bfloat16)
    return jnp.einsum(
        "bkix,bkyx->biy", row_pass, col_mats, preferred_element_type=jnp.float32
    ).astype(jnp.bfloat16)


def transpose_some(windows, row_mats, col_mats):
    back_pass = jnp.einsum(
        "biy,bkyx->bkix", windows, col_mats, preferred_element_type=jnp.float32
    ).astype(jnp.bfloat16)
    return jnp.einsum(
        "bkji,bkjx->bix", row_mats, back_pass, preferred_element_type=jnp.float32
    ).astype(jnp.bfloat16)


def apply_all(function, images, models, row_ops, col_ops):
    batch = divisor(images.shape[0], 32)

    def some(inputs):
        part, part_models = inputs
        return function(part, chosen(row_ops, part_models), chosen(col_ops, part_models))

    cut = images.reshape((-1, batch) + images.shape[1:])
    return lax.map(some, (cut, models.astype(jnp.int32).reshape((-1, batch)))).reshape(images.shape)


def per_device(stamps, tile_of, row_offset, col_offset, psf_model, psf_rows, psf_cols, cotangent):
    peer_count = lax.axis_size("tile")
    stamp_count, stamp_rows, stamp_cols = stamps.shape
    block_rows = stamp_rows // 2
    tile_rows, tile_cols = cotangent.shape
    row_blocks = tile_rows // block_rows
    col_blocks = tile_cols // stamp_cols
    capacity = max(2, (5 * stamp_count + 4 * peer_count - 1) // (4 * peer_count))
    slot_total = peer_count * capacity
    row_ops = build_ops(psf_rows, stamp_rows)
    col_ops = build_ops(psf_cols, stamp_cols)
    target = tile_of[:, 0]
    order = jnp.arange(stamp_count, dtype=jnp.int32)
    earlier = (target[None, :] == target[:, None]) & (order[None, :] < order[:, None])
    slots = target * capacity + jnp.sum(earlier.astype(jnp.int32), axis=1)
    slot_ids = jnp.arange(slot_total, dtype=jnp.int32)
    matches = slots[None, :] == slot_ids[:, None]
    place = matches.astype(jnp.bfloat16)
    details = jnp.stack([jnp.ones_like(target), row_offset, col_offset, psf_model], axis=1)
    detail_send = jnp.sum(jnp.where(matches[:, :, None], details[None, :, :], 0), axis=1)
    detail_send = detail_send.reshape(peer_count, capacity, 4)
    raw_send = jnp.dot(
        place,
        stamps.reshape((stamp_count, stamp_rows * stamp_cols)),
        preferred_element_type=jnp.float32,
    )
    raw_send = raw_send.astype(jnp.bfloat16).reshape(peer_count, capacity, stamp_rows, stamp_cols)
    raw_part = lax.all_to_all(raw_send, "tile", split_axis=0, concat_axis=0, tiled=True)
    info_part = lax.all_to_all(detail_send, "tile", split_axis=0, concat_axis=0, tiled=True)
    flat = raw_part.reshape((-1, stamp_rows, stamp_cols))
    result = apply_all(convolve_some, flat, info_part.reshape((-1, 4))[:, 3], row_ops, col_ops)
    received = result.reshape(raw_part.shape)
    info_flat = info_part.reshape((slot_total, 4))
    upper_block = info_flat[:, 1]
    block_ids = jnp.stack([upper_block, upper_block + 1], axis=1) * col_blocks + info_flat[:, 2:3]
    targets = jnp.arange((row_blocks + 1) * col_blocks, dtype=jnp.int32)
    placing = (block_ids.reshape(-1)[None, :] == targets[:, None]).astype(jnp.bfloat16)
    pieces = received.reshape((slot_total * 2, block_rows * stamp_cols))
    extended = jnp.dot(placing, pieces, preferred_element_type=jnp.float32)
    extended = extended.reshape(row_blocks + 1, col_blocks, block_rows, stamp_cols).transpose(
        0, 2, 1, 3
    )
    extended = extended.reshape((row_blocks + 1) * block_rows, tile_cols)
    arriving = passed_along(extended[tile_rows:].astype(jnp.bfloat16), "tile", 1).astype(
        jnp.float32
    )
    tile_sum = extended[:tile_rows].at[:block_rows].add(arriving)
    tile_image = tile_sum.astype(jnp.bfloat16)
    rim = passed_along(cotangent[:block_rows], "tile", -1)
    padded = jnp.concatenate([cotangent, rim], axis=0)
    blocks = padded.reshape(row_blocks + 1, block_rows, col_blocks, stamp_cols).transpose(
        0, 2, 1, 3
    )
    blocks = blocks.reshape((row_blocks + 1) * col_blocks, block_rows * stamp_cols)
    windows = lax.dot_general(
        placing, blocks, (((0,), (0,)), ((), ())), preferred_element_type=jnp.float32
    )
    windows = windows.astype(jnp.bfloat16).reshape(slot_total, stamp_rows, stamp_cols)
    slot_grads = apply_all(transpose_some, windows, info_flat[:, 3], row_ops, col_ops)
    slot_grads = slot_grads.reshape(peer_count, capacity, stamp_rows, stamp_cols)
    returned = lax.all_to_all(
        for_sending(slot_grads), "tile", split_axis=0, concat_axis=0, tiled=True
    ).astype(slot_grads.dtype)
    stamp_grad = lax.dot_general(
        place,
        returned.reshape((slot_total, stamp_rows * stamp_cols)),
        (((0,), (0,)), ((), ())),
        preferred_element_type=jnp.float32,
    )
    stamp_grad = stamp_grad.astype(jnp.bfloat16).reshape(stamp_count, stamp_rows, stamp_cols)
    return (tile_image, stamp_grad)


MESH = pl.DeviceIdType.MESH


def band_matrix(row, count, rows):
    lanes = row.shape[1]
    half = (count - 1) // 2
    spread = jnp.broadcast_to(row, (rows, lanes))
    turned = pltpu.roll(spread, lanes - half, 1, stride=1, stride_axis=0)
    down = lax.broadcasted_iota(jnp.int32, (rows, lanes), 0)
    across = lax.broadcasted_iota(jnp.int32, (rows, lanes), 1)
    return jnp.where(jnp.abs(across - down) <= half, turned, 0.0).astype(jnp.bfloat16)


def turn_taps(raw, turned):
    _, terms, count, models = raw.shape
    lanes = turned.shape[2]
    for a in range(2):
        for k in range(terms):
            values = raw[a, k]
            for way in range(2):
                rows = [values[count - 1 - t:count - t] for t in range(count)] if way else [values]
                tall = jnp.concatenate(rows + [jnp.zeros((lanes - count, models), jnp.float32)], axis=0)
                square = jnp.concatenate(
                    [tall, jnp.zeros((lanes, lanes - models), jnp.float32)], axis=1)
                turned[(a * 2 + way) * terms + k] = square.T[:turned.shape[1]]


def build_bands(turned, row_base, col_base, count, row_ops, col_ops):
    models, size, width = row_ops.shape
    lanes = col_ops.shape[1]
    terms = width // size

    def build(m, carry):
        row_ops[m] = jnp.concatenate(
            [band_matrix(turned[row_base * terms + k, pl.ds(m, 1)], count, size)[:, :size]
             for k in range(terms)], axis=1)
        for k in range(terms):
            col_ops[m, :, k * lanes:(k + 1) * lanes] = band_matrix(
                turned[col_base * terms + k, pl.ds(m, 1)], count, lanes)
        return carry

    lax.fori_loop(0, models, build, 0)


def fill_lists(fields, lists, row_blocks, col_blocks, lasts):
    lanes = fields.shape[2]
    upper = fields[0] * row_blocks + fields[1]
    block = upper * col_blocks + fields[2]
    square = jnp.broadcast_to(block, (lanes, lanes))
    turned = square.T
    down = lax.broadcasted_iota(jnp.int32, (lanes, lanes), 0)
    across = lax.broadcasted_iota(jnp.int32, (lanes, lanes), 1)
    lists[0:1, :] = jnp.zeros((1, lanes), jnp.int32)
    for r in range(lasts):
        hit = jnp.where(turned == across + r * lanes, down + 1, 0)
        lists[1 + r:2 + r, :] = jnp.max(hit, axis=0, keepdims=True)
    earlier = jnp.where((turned == square) & (down < across), down + 1, 0)
    lists[lasts + 1:lasts + 2, :] = jnp.max(earlier, axis=0, keepdims=True)
    lists[lasts + 2:lasts + 3, :] = upper
    lists[lasts + 3:lasts + 4, :] = fields[2]
    lists[lasts + 4:lasts + 5, :] = fields[3]


def remote(src, dst, send, recv, device):
    return pltpu.make_async_remote_copy(src_ref=src, dst_ref=dst, send_sem=send, recv_sem=recv,
                                        device_id={"tile": device}, device_id_type=MESH)


def whole_kernel(peers, cut, cut2, group, tile_of, row_of, col_of, model_of, row_taps, col_taps,
                 stamps_hbm, cot_hbm, tile_hbm, grads_hbm,
                 sky, sums, stamps_ref, row_fwd, col_fwd, row_bwd, col_bwd, fields, raw, turned,
                 tile_ref, grads_ref, lists_v, lists,
                 out_c, from_c, out_y, from_y, out_z, from_z, out_zb, from_zb, out_yb, from_yb,
                 own_sem, end_sem, za_s, za_r, zb_s, zb_r, ya_s, ya_r, yb_s, yb_r, ca_s, ca_r, cb_s, cb_r,
                 rc_s, rc_r, ry_s, ry_r, rz_s, rz_r, rzb_s, rzb_r, ryb_s, ryb_r):
    planes = peers // 4
    last = planes - 1
    me = lax.axis_index("tile")
    core = lax.rem(me, 2)
    row = lax.rem(me // 2, 2)
    p = me // 4
    count, stamp_rows, stamp_cols = stamps_ref.shape
    groups = count // group
    col_blocks, _, block_rows, _ = sky.shape
    row_blocks = tile_ref.shape[0]
    models = row_fwd.shape[0]
    lasts = peers * row_blocks * col_blocks // count
    PREV, UPPER, COL, MODEL = (lasts + 1 + i for i in range(4))
    rest = row_blocks - cut
    up_ok, down_ok = p < last, p > 0

    def tile_at(q, v=0, c=0):
        y = 1 - row if v else row
        return q * 4 + y * 2 + (1 - core if c else core)

    def part(tile, low, size):
        return sky.at[:, pl.ds(tile * row_blocks + low, size)]

    y_peer, c_peer = tile_at(p, 1), tile_at(p, 0, 1)
    up_peer, down_peer = tile_at(lax.min(p + 1, last)), tile_at(lax.max(p - 1, 0))

    def za(q, way):
        spot = part(tile_at(q), 0, cut)
        slot = way * planes + q
        return remote(spot, spot, za_s.at[slot], za_r.at[slot], down_peer if way else up_peer)

    def zb(q, v, way):
        spot = part(tile_at(q, v), cut, rest)
        slot = (way * 2 + v) * planes + q
        return remote(spot, spot, zb_s.at[slot], zb_r.at[slot], down_peer if way else up_peer)

    def ya(q, far=0):
        spot = part(tile_at(q, far), 0, cut)
        return remote(spot, spot, ya_s.at[q], ya_r.at[q], y_peer)

    def yb(far=0):
        spot = part(tile_at(p, far), cut, rest)
        return remote(spot, spot, yb_s, yb_r, y_peer)

    def ca(q, v, far=0):
        spot = part(tile_at(q, v, far), 0, cut)
        slot = v * planes + q
        return remote(spot, spot, ca_s.at[slot], ca_r.at[slot], c_peer)

    def cb(q, v, far=0):
        spot = part(tile_at(q, v, far), cut, rest)
        slot = v * planes + q
        return remote(spot, spot, cb_s.at[slot], cb_r.at[slot], c_peer)

    def streams(i, body):
        pl.when(p >= i)(lambda: body(p - i, 0, up_ok))
        pl.when(p + i <= last)(lambda: body(p + i, 1, down_ok))

    def a_step(i):
        def body(q, way, more):
            za(q, way).wait_recv()
            if i < last:
                pl.when(more)(lambda: za(q, way).start())
            ya(q).start()
            ca(q, 0).start()
        streams(i, body)

    def b_step(i):
        def body(q, way, more):
            for v in range(2):
                zb(q, v, way).wait_recv()
                if i < last:
                    pl.when(more)(lambda: zb(q, v, way).start())
                cb(q, v).start()
        streams(i, body)

    def y_step(i):
        def body(q, way, more):
            ya(q, 1).wait_recv()
            ca(q, 1).start()
        if i:
            streams(i, body)
        else:
            body(p, 0, None)

    def apply(g, row_ops, col_ops, image, put):
        chosen_models = [lists[MODEL, g * group + u] for u in range(group)]
        firsts = [jnp.dot(image(g * group + u), col_ops[chosen_models[u]],
                          preferred_element_type=jnp.float32).astype(jnp.bfloat16)
                  for u in range(group)]
        for u in range(group):
            tall = jnp.concatenate(
                [firsts[u][:, k * stamp_cols:(k + 1) * stamp_cols]
                 for k in range(firsts[u].shape[1] // stamp_cols)], axis=0)
            put(g * group + u, jnp.dot(row_ops[chosen_models[u]], tall,
                                       preferred_element_type=jnp.float32).astype(jnp.bfloat16))

    def add(s, value):
        sums[s + 1] = value.astype(jnp.float32) + sums[lists[PREV, s]]

    def forward(g, carry):
        apply(g, row_fwd, col_fwd, lambda s: stamps_ref[s], add)
        return carry

    def window(s):
        upper, col = lists[UPPER, s], lists[COL, s]
        return jnp.concatenate([sky[col, upper], sky[col, upper + 1]], axis=0)

    def grads_out(g):
        spot = pl.ds(g * group, group)
        return pltpu.make_async_copy(grads_ref.at[spot], grads_hbm.at[spot], end_sem.at[2 + g])

    def tile_out(slot, low, high):
        spot = pl.ds(low, high - low)
        return pltpu.make_async_copy(tile_ref.at[spot], tile_hbm.at[spot], end_sem.at[slot])

    def keep_grad(s, value):
        grads_ref[s] = value

    def backward(g, carry):
        apply(g, row_bwd, col_bwd, window, keep_grad)
        grads_out(g).start()
        return carry

    def runner(step):
        reached = [0]

        def run(number):
            stop = min(groups, reached[0] + number)
            if stop > reached[0]:
                lax.fori_loop(reached[0], stop, step, 0)
            reached[0] = stop
        return run

    compute, pull = runner(forward), runner(backward)

    def summed(tile, low, high, put, *others):
        base = tile * (row_blocks * col_blocks)
        width = lists.shape[1]

        def body(r, carry):
            for b in range(col_blocks):
                lower = base + (r * col_blocks + b + width)
                above = lower - col_blocks
                out = (sums[lists[lower // width, lax.rem(lower, width)], :block_rows]
                       + sums[lists[above // width, lax.rem(above, width)], block_rows:])
                for ref, index, shift in others:
                    out = out + ref[index, b, r - shift].astype(jnp.float32)
                put(b, r, out.astype(jnp.bfloat16))
            return carry

        lax.fori_loop(low, high, body, 0)

    half = p // 2
    mirrored = (1 - 2 * half) * p + last * half
    targets = [last * half + (1 - 2 * half) * q for q in (3, 2, 1 - mirrored, mirrored)]

    def rc(v, i):
        slot = v * planes + i
        return remote(out_c.at[slot], from_c.at[slot], rc_s.at[slot], rc_r.at[slot], c_peer)

    def ry(i):
        return remote(out_y.at[i], from_y.at[i], ry_s.at[i], ry_r.at[i], y_peer)

    def way_of(q):
        return jnp.where(q > p, 0, 1)

    def rz(i, slot, device):
        return remote(out_z.at[i], from_z.at[slot], rz_s.at[i], rz_r.at[slot], device)

    def rzb(v, i, slot, device):
        return remote(out_zb.at[v * planes + i], from_zb.at[v * 2 * planes + slot],
                      rzb_s.at[v * planes + i], rzb_r.at[v * 2 * planes + slot], device)

    def ryb():
        return remote(out_yb.at[0], from_yb.at[0], ryb_s, ryb_r, y_peer)

    def into(ref, index, shift):
        def put(b, r, value):
            ref[index, b, r - shift] = value
        return put

    def c_out(v, i):
        slot = v * planes + i
        summed(tile_at(targets[i], v, 1), 0, row_blocks, into(out_c, slot, 0))
        rc(v, i).start()

    def c_in(i):
        rc(0, i).wait_recv()
        rc(1, i).wait_recv()

    def y_out(i):
        summed(tile_at(targets[i], 1), 0, cut2, into(out_y, i, 0), (from_c, planes + i, 0))
        ry(i).start()

    def chain(i, make, tile, low, high, put, *others):
        q = targets[i]
        way = way_of(q)
        slot = way * planes + q
        device = jnp.where(q > p, up_peer, down_peer)
        first = jnp.logical_or(jnp.logical_and(q > p, p == 0), jnp.logical_and(q < p, p == last))
        copy, source, offset = make(slot, device)
        pl.when(first)(lambda: summed(tile, low, high, put, *others))

        @pl.when(jnp.logical_not(first))
        def _():
            copy.wait_recv()
            summed(tile, low, high, put, *others, (source, offset + slot, low))

        copy.start()

    def za_out(i):
        ry(i).wait_recv()
        chain(i, lambda slot, device: (rz(i, slot, device), from_z, 0), tile_at(targets[i]), 0, cut2,
              into(out_z, i, 0), (from_c, i, 0), (from_y, i, 0))

    def zb_out(v, i):
        chain(i, lambda slot, device: (rzb(v, i, slot, device), from_zb, v * 2 * planes),
              tile_at(targets[i], v), cut2, row_blocks, into(out_zb, v * planes + i, cut2),
              (from_c, v * planes + i, 0))

    def ending(make, body):
        def some(*ways):
            made = [make(way * planes + p) for way in ways]
            for copy, _ in made:
                copy.wait_recv()
            body(*[source for _, source in made])

        pl.when(p == 0)(lambda: some(1))
        pl.when(p == last)(lambda: some(0))
        pl.when(jnp.logical_and(p > 0, p < last))(lambda: some(0, 1))

    def yb_out():
        ending(lambda slot: (rzb(1, 0, slot, up_peer), (from_zb, 2 * planes + slot, cut2)),
               lambda *more: summed(tile_at(p, 1), cut2, row_blocks, into(out_yb, 0, cut2),
                                    (from_c, planes + last, 0), *more))
        ryb().start()

    def to_tile(b, r, value):
        tile_ref[r, :, b * stamp_cols:(b + 1) * stamp_cols] = value

    def a_end():
        ry(last).wait_recv()
        ending(lambda slot: (rz(0, slot, up_peer), (from_z, slot, 0)),
               lambda *more: summed(me, 0, cut2, to_tile, (from_c, last, 0), (from_y, last, 0), *more))

    def b_end():
        ryb().wait_recv()
        ending(lambda slot: (rzb(0, 0, slot, up_peer), (from_zb, slot, cut2)),
               lambda *more: summed(me, cut2, row_blocks, to_tile, (from_c, last, 0),
                                    (from_yb, 0, cut2), *more))

    barrier = pltpu.get_barrier_semaphore()

    def greet(device):
        pl.semaphore_signal(barrier, inc=1, device_id={"tile": device}, device_id_type=MESH)

    pl.when(up_ok)(lambda: greet(up_peer))
    pl.when(down_ok)(lambda: greet(down_peer))
    greet(y_peer)
    greet(c_peer)
    own = [pltpu.make_async_copy(cot_hbm.at[:, :, pl.ds(b * stamp_cols, stamp_cols)],
                                 sky.at[b, pl.ds(me * row_blocks, row_blocks)], own_sem.at[b])
           for b in range(col_blocks)]
    small = [pltpu.make_async_copy(source, target, own_sem.at[col_blocks + 2 + n])
             for n, (source, target) in enumerate(
                 [(array, fields.at[n]) for n, array in enumerate((tile_of, row_of, col_of, model_of))]
                 + [(row_taps, raw.at[0]), (col_taps, raw.at[1])])]
    fetch = pltpu.make_async_copy(stamps_hbm, stamps_ref, own_sem.at[col_blocks])
    for copy in own + small:
        copy.start()
    fetch.start()
    for b in range(col_blocks):
        sky[b, peers * row_blocks] = jnp.zeros((block_rows, stamp_cols), jnp.bfloat16)
    sums[0] = jnp.zeros((stamp_rows, stamp_cols), jnp.float32)
    for copy in own:
        copy.wait()
    pl.semaphore_wait(barrier, 2 + jnp.where(up_ok, 1, 0) + jnp.where(down_ok, 1, 0))
    whole = part(me, 0, row_blocks)
    own_c = remote(whole, whole, ca_s.at[p], ca_r.at[p], c_peer)
    pl.when(up_ok)(lambda: za(p, 0).start())
    pl.when(down_ok)(lambda: za(p, 1).start())
    yb().start()
    ya(p).start()
    own_c.start()
    for copy in small:
        copy.wait()
    fill_lists(fields, lists_v, row_blocks, col_blocks, lasts)
    listing = pltpu.make_async_copy(lists_v, lists, own_sem.at[col_blocks + 1])
    listing.start()
    turn_taps(raw, turned)
    taps = raw.shape[2]
    build_bands(turned, 0, 3, taps, row_fwd, col_fwd)
    listing.wait()
    fetch.wait()

    def ends(body):
        pl.when(jnp.logical_or(p == 0, p == last))(body)

    def middles(body):
        pl.when(jnp.logical_and(p > 0, p < last))(body)

    def zb_both(i):
        for v in range(2):
            zb_out(v, i)

    compute(4)
    yb(1).wait_recv()
    cb(p, 1).start()
    a_step(1)
    for v in range(2):
        pl.when(up_ok)(lambda: zb(p, v, 0).start())
        pl.when(down_ok)(lambda: zb(p, v, 1).start())
    compute(groups)
    for i in range(planes):
        c_out(0, i)
        c_out(1, i)
    y_step(0)
    a_step(2)
    for i in range(planes):
        c_in(i)

    @ends
    def _():
        for i in range(last):
            zb_both(i)

    for i in range(planes):
        y_out(i)
    b_step(1)
    y_step(1)
    build_bands(turned, 1, 2, taps, row_bwd, col_bwd)
    a_step(3)
    y_step(2)
    middles(lambda: zb_both(0))
    b_step(2)
    middles(lambda: zb_both(1))
    za_out(0)
    b_step(3)
    y_step(3)
    middles(lambda: zb_both(2))
    za_out(1)
    def arrived():
        for v in range(2):
            for q in range(planes):
                def two():
                    ca(q, v, 1).wait_recv()
                    cb(q, v, 1).wait_recv()

                if v:
                    two()
                else:
                    pl.when(q != p)(two)
        whole_far = part(c_peer, 0, row_blocks)
        remote(whole_far, whole_far, ca_s.at[p], ca_r.at[p], c_peer).wait_recv()

    arrived()
    pull(2)
    za_out(2)
    pull(2)
    yb_out()
    pull(groups)
    a_end()
    tile_out(0, 0, cut2).start()
    b_end()
    tile_out(1, cut2, row_blocks).start()
    for copy in (tile_out(0, 0, cut2), tile_out(1, cut2, row_blocks)):
        copy.wait()

    def written(g, carry):
        grads_out(g).wait()
        return carry

    lax.fori_loop(0, groups, written, 0)

    pl.when(up_ok)(lambda: za(p, 0).wait_send())
    pl.when(down_ok)(lambda: za(p, 1).wait_send())
    yb().wait_send()
    own_c.wait_send()
    cb(p, 1).wait_send()
    ca(p, 1).wait_send()
    ya(p).wait_send()
    for v in range(2):
        pl.when(up_ok)(lambda: zb(p, v, 0).wait_send())
        pl.when(down_ok)(lambda: zb(p, v, 1).wait_send())
    for i in range(1, planes):
        def ended(q, way, more):
            ya(q).wait_send()
            for v in range(2):
                ca(q, v).wait_send()
                cb(q, v).wait_send()
            if i < last:
                @pl.when(more)
                def _():
                    za(q, way).wait_send()
                    for v in range(2):
                        zb(q, v, way).wait_send()
        streams(i, ended)
    for i in range(planes):
        for v in range(2):
            rc(v, i).wait_send()
        ry(i).wait_send()
    for i in range(last):
        rz(i, i, up_peer).wait_send()
        for v in range(2):
            rzb(v, i, i, up_peer).wait_send()
    ryb().wait_send()


def divisor(number, wanted):
    return max(d for d in range(1, wanted + 1) if number % d == 0)


def hand_over(parts, tile_from, grads_from, tile_to, grads_to, tile_held, grads_held, sem_in, sem_out):
    size = grads_from.shape[0] // parts
    spots = [pl.ds(n * size, size) for n in range(parts)]
    copies = [(tile_from, tile_held, tile_to)] + [
        (grads_from.at[spot], grads_held.at[spot], grads_to.at[spot]) for spot in spots]
    copies = [(pltpu.make_async_copy(source, held, sem_in.at[n]),
               pltpu.make_async_copy(held, target, sem_out.at[n]))
              for n, (source, held, target) in enumerate(copies)]
    for fetch, _ in copies:
        fetch.start()
    for fetch, put in copies:
        fetch.wait()
        put.start()
    for _, put in copies:
        put.wait()


def in_place(stamps, tile_of, row_offset, col_offset, psf_model, psf_rows, psf_cols, cotangent):
    peers = lax.axis_size("tile")
    planes = peers // 4
    stamp_count, stamp_rows, stamp_cols = stamps.shape
    models, terms, taps = psf_rows.shape
    block_rows = stamp_rows // 2
    tile_rows, tile_cols = cotangent.shape
    row_blocks = tile_rows // block_rows
    col_blocks = tile_cols // stamp_cols
    cut = row_blocks * 5 // 8
    cut2 = row_blocks * 6 // 8
    group = divisor(stamp_count, 16)
    lasts = peers * row_blocks * col_blocks // stamp_count
    list_rows = -(-(lasts + 5) // 8) * 8
    model_rows = -(-models // 8) * 8
    flops = 2 * stamp_count * terms * stamp_rows * stamp_cols * (stamp_rows + stamp_cols)
    cost = pl.CostEstimate(flops=8 * flops, bytes_accessed=40 << 20, transcendentals=0)
    hbm = pl.BlockSpec(memory_space=pltpu.HBM)
    short = jnp.bfloat16
    dma = pltpu.SemaphoreType.DMA
    piece = (block_rows, stamp_cols)
    full, upper, lower = ((col_blocks, rows) + piece for rows in (row_blocks, cut2, row_blocks - cut2))
    line = lambda array: array.reshape((1, stamp_count))
    outs = (
        jax.ShapeDtypeStruct((row_blocks, block_rows, tile_cols), short),
        jax.ShapeDtypeStruct(stamps.shape, short),
    )
    row_op, col_op = ((models, size, terms * size) for size in (stamp_rows, stamp_cols))

    made = pl.pallas_call(
        partial(whole_kernel, peers, cut, cut2, group),
        out_shape=outs,
        in_specs=[hbm] * 8,
        out_specs=(hbm, hbm),
        scratch_shapes=[
            pltpu.VMEM((col_blocks, peers * row_blocks + 1) + piece, short),
            pltpu.VMEM((stamp_count + 1, stamp_rows, stamp_cols), jnp.float32),
            pltpu.VMEM(stamps.shape, short),
            pltpu.VMEM(row_op, short),
            pltpu.VMEM(col_op, short),
            pltpu.VMEM(row_op, short),
            pltpu.VMEM(col_op, short),
            pltpu.VMEM((4, 1, stamp_count), jnp.int32),
            pltpu.VMEM((2, terms, taps, models), jnp.float32),
            pltpu.VMEM((4 * terms, model_rows, stamp_count), jnp.float32),
            pltpu.VMEM(outs[0].shape, short),
            pltpu.VMEM(stamps.shape, short),
            pltpu.VMEM((list_rows, stamp_count), jnp.int32),
            pltpu.SMEM((list_rows, stamp_count), jnp.int32),
            pltpu.VMEM((2 * planes,) + full, short),
            pltpu.VMEM((2 * planes,) + full, short),
            pltpu.VMEM((planes,) + upper, short),
            pltpu.VMEM((planes,) + upper, short),
            pltpu.VMEM((planes,) + upper, short),
            pltpu.VMEM((2 * planes,) + upper, short),
            pltpu.VMEM((2 * planes,) + lower, short),
            pltpu.VMEM((4 * planes,) + lower, short),
            pltpu.VMEM((1,) + lower, short),
            pltpu.VMEM((1,) + lower, short),
            dma((col_blocks + 8,)), dma((2 + stamp_count // group,)),
        ] + [dma((2 * planes,))] * 2 + [dma((4 * planes,))] * 2 + [dma((planes,))] * 2 + [dma, dma]
        + [dma((2 * planes,))] * 4
        + [dma((2 * planes,))] * 2 + [dma((planes,))] * 2 + [dma((planes,)), dma((2 * planes,))]
        + [dma((2 * planes,)), dma((4 * planes,))] + [dma, dma],
        compiler_params=pltpu.CompilerParams(collective_id=0, has_side_effects=True,
                                             vmem_limit_bytes=60 << 20),
        cost_estimate=cost,
    )(tile_of.reshape((1, stamp_count)), line(row_offset), line(col_offset), line(psf_model),
      psf_rows.transpose(1, 2, 0), psf_cols.transpose(1, 2, 0),
      stamps, cotangent.reshape(outs[0].shape))
    parts = divisor(stamp_count, 8)
    tile_image, stamp_grad = pl.pallas_call(
        partial(hand_over, parts), out_shape=outs, in_specs=[hbm, hbm], out_specs=(hbm, hbm),
        scratch_shapes=[pltpu.VMEM(out.shape, short) for out in outs] + [dma((parts + 1,))] * 2,
    )(*made)
    return tile_image.reshape(cotangent.shape), stamp_grad


def fits(stamps, cotangent):
    count, rows, cols = stamps.shape
    peers = lax.axis_size("tile")
    return (peers == 16 and count == 128 and cols == 128 and rows % 32 == 0 and rows <= 128
            and peers * cotangent.shape[0] * cotangent.shape[1] * 4 <= 12 << 20)


def per_device_any(*args):
    if fits(args[0], args[-1]):
        return in_place(*args)
    return per_device(*args)


def solution(mesh):
    in_specs = (
        P(("band", "tile"), None, None),
        P(("band", "tile"), None),
        P(("band", "tile")),
        P(("band", "tile")),
        P(("band", "tile")),
        P("band", None, None),
        P("band", None, None),
        P(("band", "tile"), None),
    )
    out_specs = (P(("band", "tile"), None), P(("band", "tile"), None, None))
    return jax.shard_map(
        per_device_any, mesh=mesh, in_specs=in_specs, out_specs=out_specs, check_vma=False
    )
```

```python
from functools import partial

import jax
import jax.numpy as jnp
from jax import lax
from jax.experimental import pallas as pl
from jax.experimental.pallas import tpu as pltpu
from jax.sharding import PartitionSpec as P


def passed_along(array, axis, by):
    peers = lax.axis_size(axis)
    pairs = [(i, i + by) for i in range(peers) if 0 <= i + by < peers]
    return lax.ppermute(array, axis, pairs)


def for_sending(array):

    def short(part):
        return part.astype(jnp.bfloat16) if part.dtype == jnp.float32 else part

    return jax.tree.map(short, array)


def band_table(taps_count, size):
    half_width = (taps_count - 1) // 2
    places = jnp.arange(size, dtype=jnp.int32)
    offsets = places[None, :] - places[:, None] + half_width
    taps_index = jnp.arange(taps_count, dtype=jnp.int32)
    table = (offsets[None, :, :] == taps_index[:, None, None]).astype(jnp.float32)
    return table.reshape((taps_count, size * size))


def build_ops(profiles, size):
    model_total, term_total, taps_count = profiles.shape
    table = band_table(taps_count, size)
    mats = jnp.dot(
        profiles.reshape((model_total * term_total, taps_count)),
        table,
        precision=lax.Precision.HIGHEST,
    )
    return mats.reshape((model_total, term_total, size, size)).astype(jnp.bfloat16)


def chosen(ops, models):
    model_total, term_total, size, _ = ops.shape
    picks = (models[:, None] == jnp.arange(model_total, dtype=jnp.int32)[None, :]).astype(ops.dtype)
    mats = jnp.dot(picks, ops.reshape((model_total, -1)), preferred_element_type=jnp.float32)
    return mats.astype(ops.dtype).reshape((models.shape[0], term_total, size, size))


def convolve_some(images, row_mats, col_mats):
    row_pass = jnp.einsum(
        "bkij,bjx->bkix", row_mats, images, preferred_element_type=jnp.float32
    ).astype(jnp.bfloat16)
    return jnp.einsum(
        "bkix,bkyx->biy", row_pass, col_mats, preferred_element_type=jnp.float32
    ).astype(jnp.bfloat16)


def transpose_some(windows, row_mats, col_mats):
    back_pass = jnp.einsum(
        "biy,bkyx->bkix", windows, col_mats, preferred_element_type=jnp.float32
    ).astype(jnp.bfloat16)
    return jnp.einsum(
        "bkji,bkjx->bix", row_mats, back_pass, preferred_element_type=jnp.float32
    ).astype(jnp.bfloat16)


def apply_all(function, images, models, row_ops, col_ops):
    batch = divisor(images.shape[0], 32)

    def some(inputs):
        part, part_models = inputs
        return function(part, chosen(row_ops, part_models), chosen(col_ops, part_models))

    cut = images.reshape((-1, batch) + images.shape[1:])
    return lax.map(some, (cut, models.astype(jnp.int32).reshape((-1, batch)))).reshape(images.shape)


def per_device(stamps, tile_of, row_offset, col_offset, psf_model, psf_rows, psf_cols, cotangent):
    peer_count = lax.axis_size("tile")
    stamp_count, stamp_rows, stamp_cols = stamps.shape
    block_rows = stamp_rows // 2
    tile_rows, tile_cols = cotangent.shape
    row_blocks = tile_rows // block_rows
    col_blocks = tile_cols // stamp_cols
    capacity = max(2, (5 * stamp_count + 4 * peer_count - 1) // (4 * peer_count))
    slot_total = peer_count * capacity
    row_ops = build_ops(psf_rows, stamp_rows)
    col_ops = build_ops(psf_cols, stamp_cols)
    target = tile_of[:, 0]
    order = jnp.arange(stamp_count, dtype=jnp.int32)
    earlier = (target[None, :] == target[:, None]) & (order[None, :] < order[:, None])
    slots = target * capacity + jnp.sum(earlier.astype(jnp.int32), axis=1)
    slot_ids = jnp.arange(slot_total, dtype=jnp.int32)
    matches = slots[None, :] == slot_ids[:, None]
    place = matches.astype(jnp.bfloat16)
    details = jnp.stack([jnp.ones_like(target), row_offset, col_offset, psf_model], axis=1)
    detail_send = jnp.sum(jnp.where(matches[:, :, None], details[None, :, :], 0), axis=1)
    detail_send = detail_send.reshape(peer_count, capacity, 4)
    raw_send = jnp.dot(
        place,
        stamps.reshape((stamp_count, stamp_rows * stamp_cols)),
        preferred_element_type=jnp.float32,
    )
    raw_send = raw_send.astype(jnp.bfloat16).reshape(peer_count, capacity, stamp_rows, stamp_cols)
    raw_part = lax.all_to_all(raw_send, "tile", split_axis=0, concat_axis=0, tiled=True)
    info_part = lax.all_to_all(detail_send, "tile", split_axis=0, concat_axis=0, tiled=True)
    flat = raw_part.reshape((-1, stamp_rows, stamp_cols))
    result = apply_all(convolve_some, flat, info_part.reshape((-1, 4))[:, 3], row_ops, col_ops)
    received = result.reshape(raw_part.shape)
    info_flat = info_part.reshape((slot_total, 4))
    upper_block = info_flat[:, 1]
    block_ids = jnp.stack([upper_block, upper_block + 1], axis=1) * col_blocks + info_flat[:, 2:3]
    targets = jnp.arange((row_blocks + 1) * col_blocks, dtype=jnp.int32)
    placing = (block_ids.reshape(-1)[None, :] == targets[:, None]).astype(jnp.bfloat16)
    pieces = received.reshape((slot_total * 2, block_rows * stamp_cols))
    extended = jnp.dot(placing, pieces, preferred_element_type=jnp.float32)
    extended = extended.reshape(row_blocks + 1, col_blocks, block_rows, stamp_cols).transpose(
        0, 2, 1, 3
    )
    extended = extended.reshape((row_blocks + 1) * block_rows, tile_cols)
    arriving = passed_along(extended[tile_rows:].astype(jnp.bfloat16), "tile", 1).astype(
        jnp.float32
    )
    tile_sum = extended[:tile_rows].at[:block_rows].add(arriving)
    tile_image = tile_sum.astype(jnp.bfloat16)
    rim = passed_along(cotangent[:block_rows], "tile", -1)
    padded = jnp.concatenate([cotangent, rim], axis=0)
    blocks = padded.reshape(row_blocks + 1, block_rows, col_blocks, stamp_cols).transpose(
        0, 2, 1, 3
    )
    blocks = blocks.reshape((row_blocks + 1) * col_blocks, block_rows * stamp_cols)
    windows = lax.dot_general(
        placing, blocks, (((0,), (0,)), ((), ())), preferred_element_type=jnp.float32
    )
    windows = windows.astype(jnp.bfloat16).reshape(slot_total, stamp_rows, stamp_cols)
    slot_grads = apply_all(transpose_some, windows, info_flat[:, 3], row_ops, col_ops)
    slot_grads = slot_grads.reshape(peer_count, capacity, stamp_rows, stamp_cols)
    returned = lax.all_to_all(
        for_sending(slot_grads), "tile", split_axis=0, concat_axis=0, tiled=True
    ).astype(slot_grads.dtype)
    stamp_grad = lax.dot_general(
        place,
        returned.reshape((slot_total, stamp_rows * stamp_cols)),
        (((0,), (0,)), ((), ())),
        preferred_element_type=jnp.float32,
    )
    stamp_grad = stamp_grad.astype(jnp.bfloat16).reshape(stamp_count, stamp_rows, stamp_cols)
    return (tile_image, stamp_grad)


MESH = pl.DeviceIdType.MESH


def band_matrix(row, count, rows):
    lanes = row.shape[1]
    half = (count - 1) // 2
    spread = jnp.broadcast_to(row, (rows, lanes))
    turned = pltpu.roll(spread, lanes - half, 1, stride=1, stride_axis=0)
    down = lax.broadcasted_iota(jnp.int32, (rows, lanes), 0)
    across = lax.broadcasted_iota(jnp.int32, (rows, lanes), 1)
    return jnp.where(jnp.abs(across - down) <= half, turned, 0.0).astype(jnp.bfloat16)


def turn_taps(raw, turned):
    _, terms, count, models = raw.shape
    lanes = turned.shape[2]
    for a in range(2):
        for k in range(terms):
            values = raw[a, k]
            for way in range(2):
                rows = [values[count - 1 - t:count - t] for t in range(count)] if way else [values]
                tall = jnp.concatenate(rows + [jnp.zeros((lanes - count, models), jnp.float32)], axis=0)
                square = jnp.concatenate(
                    [tall, jnp.zeros((lanes, lanes - models), jnp.float32)], axis=1)
                turned[(a * 2 + way) * terms + k] = square.T[:turned.shape[1]]


def build_bands(turned, row_base, col_base, count, row_ops, col_ops):
    models, size, width = row_ops.shape
    lanes = col_ops.shape[1]
    terms = width // size

    def build(m, carry):
        row_ops[m] = jnp.concatenate(
            [band_matrix(turned[row_base * terms + k, pl.ds(m, 1)], count, size)[:, :size]
             for k in range(terms)], axis=1)
        for k in range(terms):
            col_ops[m, :, k * lanes:(k + 1) * lanes] = band_matrix(
                turned[col_base * terms + k, pl.ds(m, 1)], count, lanes)
        return carry

    lax.fori_loop(0, models, build, 0)


def fill_lists(fields, lists, row_blocks, col_blocks, lasts):
    lanes = fields.shape[2]
    upper = fields[0] * row_blocks + fields[1]
    block = upper * col_blocks + fields[2]
    square = jnp.broadcast_to(block, (lanes, lanes))
    turned = square.T
    down = lax.broadcasted_iota(jnp.int32, (lanes, lanes), 0)
    across = lax.broadcasted_iota(jnp.int32, (lanes, lanes), 1)
    lists[0:1, :] = jnp.zeros((1, lanes), jnp.int32)
    for r in range(lasts):
        hit = jnp.where(turned == across + r * lanes, down + 1, 0)
        lists[1 + r:2 + r, :] = jnp.max(hit, axis=0, keepdims=True)
    earlier = jnp.where((turned == square) & (down < across), down + 1, 0)
    lists[lasts + 1:lasts + 2, :] = jnp.max(earlier, axis=0, keepdims=True)
    lists[lasts + 2:lasts + 3, :] = upper
    lists[lasts + 3:lasts + 4, :] = fields[2]
    lists[lasts + 4:lasts + 5, :] = fields[3]


def remote(src, dst, send, recv, device):
    return pltpu.make_async_remote_copy(src_ref=src, dst_ref=dst, send_sem=send, recv_sem=recv,
                                        device_id={"tile": device}, device_id_type=MESH)


def whole_kernel(peers, cut, cut2, group, tile_of, row_of, col_of, model_of, row_taps, col_taps,
                 stamps_hbm, cot_hbm, tile_hbm, grads_hbm,
                 sky, sums, stamps_ref, row_fwd, col_fwd, row_bwd, col_bwd, fields, raw, turned,
                 tile_ref, grads_ref, lists_v, lists,
                 out_c, from_c, out_y, from_y, out_z, from_z, out_zb, from_zb, out_yb, from_yb,
                 own_sem, end_sem, za_s, za_r, zb_s, zb_r, ya_s, ya_r, yb_s, yb_r, ca_s, ca_r, cb_s, cb_r,
                 rc_s, rc_r, ry_s, ry_r, rz_s, rz_r, rzb_s, rzb_r, ryb_s, ryb_r):
    planes = peers // 4
    last = planes - 1
    me = lax.axis_index("tile")
    core = lax.rem(me, 2)
    row = lax.rem(me // 2, 2)
    p = me // 4
    count, stamp_rows, stamp_cols = stamps_ref.shape
    groups = count // group
    col_blocks, _, block_rows, _ = sky.shape
    row_blocks = tile_ref.shape[0]
    models = row_fwd.shape[0]
    lasts = peers * row_blocks * col_blocks // count
    PREV, UPPER, COL, MODEL = (lasts + 1 + i for i in range(4))
    rest = row_blocks - cut
    up_ok, down_ok = p < last, p > 0

    def tile_at(q, v=0, c=0):
        y = 1 - row if v else row
        return q * 4 + y * 2 + (1 - core if c else core)

    def part(tile, low, size):
        return sky.at[:, pl.ds(tile * row_blocks + low, size)]

    y_peer, c_peer = tile_at(p, 1), tile_at(p, 0, 1)
    up_peer, down_peer = tile_at(lax.min(p + 1, last)), tile_at(lax.max(p - 1, 0))

    def za(q, way):
        spot = part(tile_at(q), 0, cut)
        slot = way * planes + q
        return remote(spot, spot, za_s.at[slot], za_r.at[slot], down_peer if way else up_peer)

    def zb(q, v, way):
        spot = part(tile_at(q, v), cut, rest)
        slot = (way * 2 + v) * planes + q
        return remote(spot, spot, zb_s.at[slot], zb_r.at[slot], down_peer if way else up_peer)

    def ya(q, far=0):
        spot = part(tile_at(q, far), 0, cut)
        return remote(spot, spot, ya_s.at[q], ya_r.at[q], y_peer)

    def yb(far=0):
        spot = part(tile_at(p, far), cut, rest)
        return remote(spot, spot, yb_s, yb_r, y_peer)

    def ca(q, v, far=0):
        spot = part(tile_at(q, v, far), 0, cut)
        slot = v * planes + q
        return remote(spot, spot, ca_s.at[slot], ca_r.at[slot], c_peer)

    def cb(q, v, far=0):
        spot = part(tile_at(q, v, far), cut, rest)
        slot = v * planes + q
        return remote(spot, spot, cb_s.at[slot], cb_r.at[slot], c_peer)

    def streams(i, body):
        pl.when(p >= i)(lambda: body(p - i, 0, up_ok))
        pl.when(p + i <= last)(lambda: body(p + i, 1, down_ok))

    def a_step(i):
        def body(q, way, more):
            za(q, way).wait_recv()
            if i < last:
                pl.when(more)(lambda: za(q, way).start())
            ya(q).start()
            ca(q, 0).start()
        streams(i, body)

    def b_step(i):
        def body(q, way, more):
            for v in range(2):
                zb(q, v, way).wait_recv()
                if i < last:
                    pl.when(more)(lambda: zb(q, v, way).start())
                cb(q, v).start()
        streams(i, body)

    def y_step(i):
        def body(q, way, more):
            ya(q, 1).wait_recv()
            ca(q, 1).start()
        if i:
            streams(i, body)
        else:
            body(p, 0, None)

    def apply(g, row_ops, col_ops, image, put):
        chosen_models = [lists[MODEL, g * group + u] for u in range(group)]
        firsts = [jnp.dot(image(g * group + u), col_ops[chosen_models[u]],
                          preferred_element_type=jnp.float32).astype(jnp.bfloat16)
                  for u in range(group)]
        for u in range(group):
            tall = jnp.concatenate(
                [firsts[u][:, k * stamp_cols:(k + 1) * stamp_cols]
                 for k in range(firsts[u].shape[1] // stamp_cols)], axis=0)
            put(g * group + u, jnp.dot(row_ops[chosen_models[u]], tall,
                                       preferred_element_type=jnp.float32).astype(jnp.bfloat16))

    def add(s, value):
        sums[s + 1] = value.astype(jnp.float32) + sums[lists[PREV, s]]

    def forward(g, carry):
        apply(g, row_fwd, col_fwd, lambda s: stamps_ref[s], add)
        return carry

    def window(s):
        upper, col = lists[UPPER, s], lists[COL, s]
        return jnp.concatenate([sky[col, upper], sky[col, upper + 1]], axis=0)

    def grads_out(g):
        spot = pl.ds(g * group, group)
        return pltpu.make_async_copy(grads_ref.at[spot], grads_hbm.at[spot], end_sem.at[2 + g])

    def tile_out(slot, low, high):
        spot = pl.ds(low, high - low)
        return pltpu.make_async_copy(tile_ref.at[spot], tile_hbm.at[spot], end_sem.at[slot])

    def keep_grad(s, value):
        grads_ref[s] = value

    def backward(g, carry):
        apply(g, row_bwd, col_bwd, window, keep_grad)
        grads_out(g).start()
        return carry

    def runner(step):
        reached = [0]

        def run(number):
            stop = min(groups, reached[0] + number)
            if stop > reached[0]:
                lax.fori_loop(reached[0], stop, step, 0)
            reached[0] = stop
        return run

    compute, pull = runner(forward), runner(backward)

    def summed(tile, low, high, put, *others):
        base = tile * (row_blocks * col_blocks)
        width = lists.shape[1]

        def body(r, carry):
            for b in range(col_blocks):
                lower = base + (r * col_blocks + b + width)
                above = lower - col_blocks
                out = (sums[lists[lower // width, lax.rem(lower, width)], :block_rows]
                       + sums[lists[above // width, lax.rem(above, width)], block_rows:])
                for ref, index, shift in others:
                    out = out + ref[index, b, r - shift].astype(jnp.float32)
                put(b, r, out.astype(jnp.bfloat16))
            return carry

        lax.fori_loop(low, high, body, 0)

    half = p // 2
    mirrored = (1 - 2 * half) * p + last * half
    targets = [last * half + (1 - 2 * half) * q for q in (3, 2, 1 - mirrored, mirrored)]

    def rc(v, i):
        slot = v * planes + i
        return remote(out_c.at[slot], from_c.at[slot], rc_s.at[slot], rc_r.at[slot], c_peer)

    def ry(i):
        return remote(out_y.at[i], from_y.at[i], ry_s.at[i], ry_r.at[i], y_peer)

    def way_of(q):
        return jnp.where(q > p, 0, 1)

    def rz(i, slot, device):
        return remote(out_z.at[i], from_z.at[slot], rz_s.at[i], rz_r.at[slot], device)

    def rzb(v, i, slot, device):
        return remote(out_zb.at[v * planes + i], from_zb.at[v * 2 * planes + slot],
                      rzb_s.at[v * planes + i], rzb_r.at[v * 2 * planes + slot], device)

    def ryb():
        return remote(out_yb.at[0], from_yb.at[0], ryb_s, ryb_r, y_peer)

    def into(ref, index, shift):
        def put(b, r, value):
            ref[index, b, r - shift] = value
        return put

    def c_out(v, i):
        slot = v * planes + i
        summed(tile_at(targets[i], v, 1), 0, row_blocks, into(out_c, slot, 0))
        rc(v, i).start()

    def c_in(i):
        rc(0, i).wait_recv()
        rc(1, i).wait_recv()

    def y_out(i):
        summed(tile_at(targets[i], 1), 0, cut2, into(out_y, i, 0), (from_c, planes + i, 0))
        ry(i).start()

    def chain(i, make, tile, low, high, put, *others):
        q = targets[i]
        way = way_of(q)
        slot = way * planes + q
        device = jnp.where(q > p, up_peer, down_peer)
        first = jnp.logical_or(jnp.logical_and(q > p, p == 0), jnp.logical_and(q < p, p == last))
        copy, source, offset = make(slot, device)
        pl.when(first)(lambda: summed(tile, low, high, put, *others))

        @pl.when(jnp.logical_not(first))
        def _():
            copy.wait_recv()
            summed(tile, low, high, put, *others, (source, offset + slot, low))

        copy.start()

    def za_out(i):
        ry(i).wait_recv()
        chain(i, lambda slot, device: (rz(i, slot, device), from_z, 0), tile_at(targets[i]), 0, cut2,
              into(out_z, i, 0), (from_c, i, 0), (from_y, i, 0))

    def zb_out(v, i):
        chain(i, lambda slot, device: (rzb(v, i, slot, device), from_zb, v * 2 * planes),
              tile_at(targets[i], v), cut2, row_blocks, into(out_zb, v * planes + i, cut2),
              (from_c, v * planes + i, 0))

    def ending(make, body):
        def some(*ways):
            made = [make(way * planes + p) for way in ways]
            for copy, _ in made:
                copy.wait_recv()
            body(*[source for _, source in made])

        pl.when(p == 0)(lambda: some(1))
        pl.when(p == last)(lambda: some(0))
        pl.when(jnp.logical_and(p > 0, p < last))(lambda: some(0, 1))

    def yb_out():
        ending(lambda slot: (rzb(1, 0, slot, up_peer), (from_zb, 2 * planes + slot, cut2)),
               lambda *more: summed(tile_at(p, 1), cut2, row_blocks, into(out_yb, 0, cut2),
                                    (from_c, planes + last, 0), *more))
        ryb().start()

    def to_tile(b, r, value):
        tile_ref[r, :, b * stamp_cols:(b + 1) * stamp_cols] = value

    def a_end():
        ry(last).wait_recv()
        ending(lambda slot: (rz(0, slot, up_peer), (from_z, slot, 0)),
               lambda *more: summed(me, 0, cut2, to_tile, (from_c, last, 0), (from_y, last, 0), *more))

    def b_end():
        ryb().wait_recv()
        ending(lambda slot: (rzb(0, 0, slot, up_peer), (from_zb, slot, cut2)),
               lambda *more: summed(me, cut2, row_blocks, to_tile, (from_c, last, 0),
                                    (from_yb, 0, cut2), *more))

    barrier = pltpu.get_barrier_semaphore()

    def greet(device):
        pl.semaphore_signal(barrier, inc=1, device_id={"tile": device}, device_id_type=MESH)

    pl.when(up_ok)(lambda: greet(up_peer))
    pl.when(down_ok)(lambda: greet(down_peer))
    greet(y_peer)
    greet(c_peer)
    own = [pltpu.make_async_copy(cot_hbm.at[:, :, pl.ds(b * stamp_cols, stamp_cols)],
                                 sky.at[b, pl.ds(me * row_blocks, row_blocks)], own_sem.at[b])
           for b in range(col_blocks)]
    small = [pltpu.make_async_copy(source, target, own_sem.at[col_blocks + 2 + n])
             for n, (source, target) in enumerate(
                 [(array, fields.at[n]) for n, array in enumerate((tile_of, row_of, col_of, model_of))]
                 + [(row_taps, raw.at[0]), (col_taps, raw.at[1])])]
    fetch = pltpu.make_async_copy(stamps_hbm, stamps_ref, own_sem.at[col_blocks])
    for copy in own + small:
        copy.start()
    fetch.start()
    for b in range(col_blocks):
        sky[b, peers * row_blocks] = jnp.zeros((block_rows, stamp_cols), jnp.bfloat16)
    sums[0] = jnp.zeros((stamp_rows, stamp_cols), jnp.float32)
    for copy in small:
        copy.wait()
    fill_lists(fields, lists_v, row_blocks, col_blocks, lasts)
    listing = pltpu.make_async_copy(lists_v, lists, own_sem.at[col_blocks + 1])
    listing.start()
    turn_taps(raw, turned)
    taps = raw.shape[2]
    for copy in own:
        copy.wait()
    pl.semaphore_wait(barrier, 2 + jnp.where(up_ok, 1, 0) + jnp.where(down_ok, 1, 0))
    whole = part(me, 0, row_blocks)
    own_c = remote(whole, whole, ca_s.at[p], ca_r.at[p], c_peer)
    pl.when(up_ok)(lambda: za(p, 0).start())
    pl.when(down_ok)(lambda: za(p, 1).start())
    yb().start()
    ya(p).start()
    own_c.start()
    build_bands(turned, 0, 3, taps, row_fwd, col_fwd)
    listing.wait()
    fetch.wait()

    def ends(body):
        pl.when(jnp.logical_or(p == 0, p == last))(body)

    def middles(body):
        pl.when(jnp.logical_and(p > 0, p < last))(body)

    def zb_both(i):
        for v in range(2):
            zb_out(v, i)

    compute(4)
    yb(1).wait_recv()
    cb(p, 1).start()
    a_step(1)
    for v in range(2):
        pl.when(up_ok)(lambda: zb(p, v, 0).start())
        pl.when(down_ok)(lambda: zb(p, v, 1).start())
    compute(groups)
    for i in range(2):
        c_out(0, i)
        c_out(1, i)
    a_step(2)
    y_step(0)
    c_in(0)
    ends(lambda: zb_both(0))
    y_out(0)
    for i in range(2, 4):
        c_out(0, i)
        c_out(1, i)
    c_in(1)
    y_out(1)
    b_step(1)
    y_step(1)
    c_in(2)
    c_in(3)
    a_step(3)
    y_out(2)
    build_bands(turned, 1, 2, taps, row_bwd, col_bwd)

    @ends
    def _():
        za_out(0)
        zb_both(1)

    b_step(2)
    y_step(2)
    y_out(3)

    @middles
    def _():
        zb_both(0)
        za_out(0)

    @ends
    def _():
        za_out(1)
        zb_both(2)

    y_step(3)
    b_step(3)

    @middles
    def _():
        zb_both(2)
        za_out(2)

    def arrived():
        for v in range(2):
            for q in range(planes):
                def two():
                    ca(q, v, 1).wait_recv()
                    cb(q, v, 1).wait_recv()

                if v:
                    two()
                else:
                    pl.when(q != p)(two)
        whole_far = part(c_peer, 0, row_blocks)
        remote(whole_far, whole_far, ca_s.at[p], ca_r.at[p], c_peer).wait_recv()

    arrived()
    pull(2)

    @middles
    def _():
        zb_both(1)
        za_out(1)

    ends(lambda: za_out(2))
    pull(2)
    yb_out()
    pull(groups)
    a_end()
    tile_out(0, 0, cut2).start()
    b_end()
    tile_out(1, cut2, row_blocks).start()
    for copy in (tile_out(0, 0, cut2), tile_out(1, cut2, row_blocks)):
        copy.wait()

    def written(g, carry):
        grads_out(g).wait()
        return carry

    lax.fori_loop(0, groups, written, 0)

    pl.when(up_ok)(lambda: za(p, 0).wait_send())
    pl.when(down_ok)(lambda: za(p, 1).wait_send())
    yb().wait_send()
    own_c.wait_send()
    cb(p, 1).wait_send()
    ca(p, 1).wait_send()
    ya(p).wait_send()
    for v in range(2):
        pl.when(up_ok)(lambda: zb(p, v, 0).wait_send())
        pl.when(down_ok)(lambda: zb(p, v, 1).wait_send())
    for i in range(1, planes):
        def ended(q, way, more):
            ya(q).wait_send()
            for v in range(2):
                ca(q, v).wait_send()
                cb(q, v).wait_send()
            if i < last:
                @pl.when(more)
                def _():
                    za(q, way).wait_send()
                    for v in range(2):
                        zb(q, v, way).wait_send()
        streams(i, ended)
    for i in range(planes):
        for v in range(2):
            rc(v, i).wait_send()
        ry(i).wait_send()
    for i in range(last):
        rz(i, i, up_peer).wait_send()
        for v in range(2):
            rzb(v, i, i, up_peer).wait_send()
    ryb().wait_send()


def divisor(number, wanted):
    return max(d for d in range(1, wanted + 1) if number % d == 0)


def hand_over(parts, tile_from, grads_from, tile_to, grads_to, tile_held, grads_held, sem_in, sem_out):
    size = grads_from.shape[0] // parts
    spots = [pl.ds(n * size, size) for n in range(parts)]
    copies = [(tile_from, tile_held, tile_to)] + [
        (grads_from.at[spot], grads_held.at[spot], grads_to.at[spot]) for spot in spots]
    copies = [(pltpu.make_async_copy(source, held, sem_in.at[n]),
               pltpu.make_async_copy(held, target, sem_out.at[n]))
              for n, (source, held, target) in enumerate(copies)]
    for fetch, _ in copies:
        fetch.start()
    for fetch, put in copies:
        fetch.wait()
        put.start()
    for _, put in copies:
        put.wait()


def in_place(stamps, tile_of, row_offset, col_offset, psf_model, psf_rows, psf_cols, cotangent):
    peers = lax.axis_size("tile")
    planes = peers // 4
    stamp_count, stamp_rows, stamp_cols = stamps.shape
    models, terms, taps = psf_rows.shape
    block_rows = stamp_rows // 2
    tile_rows, tile_cols = cotangent.shape
    row_blocks = tile_rows // block_rows
    col_blocks = tile_cols // stamp_cols
    cut = row_blocks * 5 // 8
    cut2 = row_blocks * 5 // 8
    group = divisor(stamp_count, 16)
    lasts = peers * row_blocks * col_blocks // stamp_count
    list_rows = -(-(lasts + 5) // 8) * 8
    model_rows = -(-models // 8) * 8
    flops = 2 * stamp_count * terms * stamp_rows * stamp_cols * (stamp_rows + stamp_cols)
    cost = pl.CostEstimate(flops=8 * flops, bytes_accessed=40 << 20, transcendentals=0)
    hbm = pl.BlockSpec(memory_space=pltpu.HBM)
    short = jnp.bfloat16
    dma = pltpu.SemaphoreType.DMA
    piece = (block_rows, stamp_cols)
    full, upper, lower = ((col_blocks, rows) + piece for rows in (row_blocks, cut2, row_blocks - cut2))
    line = lambda array: array.reshape((1, stamp_count))
    outs = (
        jax.ShapeDtypeStruct((row_blocks, block_rows, tile_cols), short),
        jax.ShapeDtypeStruct(stamps.shape, short),
    )
    row_op, col_op = ((models, size, terms * size) for size in (stamp_rows, stamp_cols))

    made = pl.pallas_call(
        partial(whole_kernel, peers, cut, cut2, group),
        out_shape=outs,
        in_specs=[hbm] * 8,
        out_specs=(hbm, hbm),
        scratch_shapes=[
            pltpu.VMEM((col_blocks, peers * row_blocks + 1) + piece, short),
            pltpu.VMEM((stamp_count + 1, stamp_rows, stamp_cols), jnp.float32),
            pltpu.VMEM(stamps.shape, short),
            pltpu.VMEM(row_op, short),
            pltpu.VMEM(col_op, short),
            pltpu.VMEM(row_op, short),
            pltpu.VMEM(col_op, short),
            pltpu.VMEM((4, 1, stamp_count), jnp.int32),
            pltpu.VMEM((2, terms, taps, models), jnp.float32),
            pltpu.VMEM((4 * terms, model_rows, stamp_count), jnp.float32),
            pltpu.VMEM(outs[0].shape, short),
            pltpu.VMEM(stamps.shape, short),
            pltpu.VMEM((list_rows, stamp_count), jnp.int32),
            pltpu.SMEM((list_rows, stamp_count), jnp.int32),
            pltpu.VMEM((2 * planes,) + full, short),
            pltpu.VMEM((2 * planes,) + full, short),
            pltpu.VMEM((planes,) + upper, short),
            pltpu.VMEM((planes,) + upper, short),
            pltpu.VMEM((planes,) + upper, short),
            pltpu.VMEM((2 * planes,) + upper, short),
            pltpu.VMEM((2 * planes,) + lower, short),
            pltpu.VMEM((4 * planes,) + lower, short),
            pltpu.VMEM((1,) + lower, short),
            pltpu.VMEM((1,) + lower, short),
            dma((col_blocks + 8,)), dma((2 + stamp_count // group,)),
        ] + [dma((2 * planes,))] * 2 + [dma((4 * planes,))] * 2 + [dma((planes,))] * 2 + [dma, dma]
        + [dma((2 * planes,))] * 4
        + [dma((2 * planes,))] * 2 + [dma((planes,))] * 2 + [dma((planes,)), dma((2 * planes,))]
        + [dma((2 * planes,)), dma((4 * planes,))] + [dma, dma],
        compiler_params=pltpu.CompilerParams(collective_id=0, has_side_effects=True,
                                             vmem_limit_bytes=60 << 20),
        cost_estimate=cost,
    )(tile_of.reshape((1, stamp_count)), line(row_offset), line(col_offset), line(psf_model),
      psf_rows.transpose(1, 2, 0), psf_cols.transpose(1, 2, 0),
      stamps, cotangent.reshape(outs[0].shape))
    parts = divisor(stamp_count, 8)
    tile_image, stamp_grad = pl.pallas_call(
        partial(hand_over, parts), out_shape=outs, in_specs=[hbm, hbm], out_specs=(hbm, hbm),
        scratch_shapes=[pltpu.VMEM(out.shape, short) for out in outs] + [dma((parts + 1,))] * 2,
    )(*made)
    return tile_image.reshape(cotangent.shape), stamp_grad


def fits(stamps, cotangent):
    count, rows, cols = stamps.shape
    peers = lax.axis_size("tile")
    return (peers == 16 and count == 128 and cols == 128 and rows % 32 == 0 and rows <= 128
            and peers * cotangent.shape[0] * cotangent.shape[1] * 4 <= 12 << 20)


def per_device_any(*args):
    if fits(args[0], args[-1]):
        return in_place(*args)
    return per_device(*args)


def solution(mesh):
    in_specs = (
        P(("band", "tile"), None, None),
        P(("band", "tile"), None),
        P(("band", "tile")),
        P(("band", "tile")),
        P(("band", "tile")),
        P("band", None, None),
        P("band", None, None),
        P(("band", "tile"), None),
    )
    out_specs = (P(("band", "tile"), None), P(("band", "tile"), None, None))
    return jax.shard_map(
        per_device_any, mesh=mesh, in_specs=in_specs, out_specs=out_specs, check_vma=False
    )
```

```python
from functools import partial

import jax
import jax.numpy as jnp
from jax import lax
from jax.experimental import pallas as pl
from jax.experimental.pallas import tpu as pltpu
from jax.sharding import PartitionSpec as P


def passed_along(array, axis, by):
    peers = lax.axis_size(axis)
    pairs = [(i, i + by) for i in range(peers) if 0 <= i + by < peers]
    return lax.ppermute(array, axis, pairs)


def for_sending(array):

    def short(part):
        return part.astype(jnp.bfloat16) if part.dtype == jnp.float32 else part

    return jax.tree.map(short, array)


def band_table(taps_count, size):
    half_width = (taps_count - 1) // 2
    places = jnp.arange(size, dtype=jnp.int32)
    offsets = places[None, :] - places[:, None] + half_width
    taps_index = jnp.arange(taps_count, dtype=jnp.int32)
    table = (offsets[None, :, :] == taps_index[:, None, None]).astype(jnp.float32)
    return table.reshape((taps_count, size * size))


def build_ops(profiles, size):
    model_total, term_total, taps_count = profiles.shape
    table = band_table(taps_count, size)
    mats = jnp.dot(
        profiles.reshape((model_total * term_total, taps_count)),
        table,
        precision=lax.Precision.HIGHEST,
    )
    return mats.reshape((model_total, term_total, size, size)).astype(jnp.bfloat16)


def chosen(ops, models):
    model_total, term_total, size, _ = ops.shape
    picks = (models[:, None] == jnp.arange(model_total, dtype=jnp.int32)[None, :]).astype(ops.dtype)
    mats = jnp.dot(picks, ops.reshape((model_total, -1)), preferred_element_type=jnp.float32)
    return mats.astype(ops.dtype).reshape((models.shape[0], term_total, size, size))


def convolve_some(images, row_mats, col_mats):
    row_pass = jnp.einsum(
        "bkij,bjx->bkix", row_mats, images, preferred_element_type=jnp.float32
    ).astype(jnp.bfloat16)
    return jnp.einsum(
        "bkix,bkyx->biy", row_pass, col_mats, preferred_element_type=jnp.float32
    ).astype(jnp.bfloat16)


def transpose_some(windows, row_mats, col_mats):
    back_pass = jnp.einsum(
        "biy,bkyx->bkix", windows, col_mats, preferred_element_type=jnp.float32
    ).astype(jnp.bfloat16)
    return jnp.einsum(
        "bkji,bkjx->bix", row_mats, back_pass, preferred_element_type=jnp.float32
    ).astype(jnp.bfloat16)


def apply_all(function, images, models, row_ops, col_ops):
    batch = divisor(images.shape[0], 32)

    def some(inputs):
        part, part_models = inputs
        return function(part, chosen(row_ops, part_models), chosen(col_ops, part_models))

    cut = images.reshape((-1, batch) + images.shape[1:])
    return lax.map(some, (cut, models.astype(jnp.int32).reshape((-1, batch)))).reshape(images.shape)


def per_device(stamps, tile_of, row_offset, col_offset, psf_model, psf_rows, psf_cols, cotangent):
    peer_count = lax.axis_size("tile")
    stamp_count, stamp_rows, stamp_cols = stamps.shape
    block_rows = stamp_rows // 2
    tile_rows, tile_cols = cotangent.shape
    row_blocks = tile_rows // block_rows
    col_blocks = tile_cols // stamp_cols
    capacity = max(2, (5 * stamp_count + 4 * peer_count - 1) // (4 * peer_count))
    slot_total = peer_count * capacity
    row_ops = build_ops(psf_rows, stamp_rows)
    col_ops = build_ops(psf_cols, stamp_cols)
    target = tile_of[:, 0]
    order = jnp.arange(stamp_count, dtype=jnp.int32)
    earlier = (target[None, :] == target[:, None]) & (order[None, :] < order[:, None])
    slots = target * capacity + jnp.sum(earlier.astype(jnp.int32), axis=1)
    slot_ids = jnp.arange(slot_total, dtype=jnp.int32)
    matches = slots[None, :] == slot_ids[:, None]
    place = matches.astype(jnp.bfloat16)
    details = jnp.stack([jnp.ones_like(target), row_offset, col_offset, psf_model], axis=1)
    detail_send = jnp.sum(jnp.where(matches[:, :, None], details[None, :, :], 0), axis=1)
    detail_send = detail_send.reshape(peer_count, capacity, 4)
    raw_send = jnp.dot(
        place,
        stamps.reshape((stamp_count, stamp_rows * stamp_cols)),
        preferred_element_type=jnp.float32,
    )
    raw_send = raw_send.astype(jnp.bfloat16).reshape(peer_count, capacity, stamp_rows, stamp_cols)
    raw_part = lax.all_to_all(raw_send, "tile", split_axis=0, concat_axis=0, tiled=True)
    info_part = lax.all_to_all(detail_send, "tile", split_axis=0, concat_axis=0, tiled=True)
    flat = raw_part.reshape((-1, stamp_rows, stamp_cols))
    result = apply_all(convolve_some, flat, info_part.reshape((-1, 4))[:, 3], row_ops, col_ops)
    received = result.reshape(raw_part.shape)
    info_flat = info_part.reshape((slot_total, 4))
    upper_block = info_flat[:, 1]
    block_ids = jnp.stack([upper_block, upper_block + 1], axis=1) * col_blocks + info_flat[:, 2:3]
    targets = jnp.arange((row_blocks + 1) * col_blocks, dtype=jnp.int32)
    placing = (block_ids.reshape(-1)[None, :] == targets[:, None]).astype(jnp.bfloat16)
    pieces = received.reshape((slot_total * 2, block_rows * stamp_cols))
    extended = jnp.dot(placing, pieces, preferred_element_type=jnp.float32)
    extended = extended.reshape(row_blocks + 1, col_blocks, block_rows, stamp_cols).transpose(
        0, 2, 1, 3
    )
    extended = extended.reshape((row_blocks + 1) * block_rows, tile_cols)
    arriving = passed_along(extended[tile_rows:].astype(jnp.bfloat16), "tile", 1).astype(
        jnp.float32
    )
    tile_sum = extended[:tile_rows].at[:block_rows].add(arriving)
    tile_image = tile_sum.astype(jnp.bfloat16)
    rim = passed_along(cotangent[:block_rows], "tile", -1)
    padded = jnp.concatenate([cotangent, rim], axis=0)
    blocks = padded.reshape(row_blocks + 1, block_rows, col_blocks, stamp_cols).transpose(
        0, 2, 1, 3
    )
    blocks = blocks.reshape((row_blocks + 1) * col_blocks, block_rows * stamp_cols)
    windows = lax.dot_general(
        placing, blocks, (((0,), (0,)), ((), ())), preferred_element_type=jnp.float32
    )
    windows = windows.astype(jnp.bfloat16).reshape(slot_total, stamp_rows, stamp_cols)
    slot_grads = apply_all(transpose_some, windows, info_flat[:, 3], row_ops, col_ops)
    slot_grads = slot_grads.reshape(peer_count, capacity, stamp_rows, stamp_cols)
    returned = lax.all_to_all(
        for_sending(slot_grads), "tile", split_axis=0, concat_axis=0, tiled=True
    ).astype(slot_grads.dtype)
    stamp_grad = lax.dot_general(
        place,
        returned.reshape((slot_total, stamp_rows * stamp_cols)),
        (((0,), (0,)), ((), ())),
        preferred_element_type=jnp.float32,
    )
    stamp_grad = stamp_grad.astype(jnp.bfloat16).reshape(stamp_count, stamp_rows, stamp_cols)
    return (tile_image, stamp_grad)


MESH = pl.DeviceIdType.MESH


def band_matrix(row, count, rows):
    lanes = row.shape[1]
    half = (count - 1) // 2
    spread = jnp.broadcast_to(row, (rows, lanes))
    turned = pltpu.roll(spread, lanes - half, 1, stride=1, stride_axis=0)
    down = lax.broadcasted_iota(jnp.int32, (rows, lanes), 0)
    across = lax.broadcasted_iota(jnp.int32, (rows, lanes), 1)
    return jnp.where(jnp.abs(across - down) <= half, turned, 0.0).astype(jnp.bfloat16)


def turn_taps(raw, turned):
    _, terms, count, models = raw.shape
    lanes = turned.shape[2]
    for a in range(2):
        for k in range(terms):
            values = raw[a, k]
            for way in range(2):
                rows = [values[count - 1 - t:count - t] for t in range(count)] if way else [values]
                tall = jnp.concatenate(rows + [jnp.zeros((lanes - count, models), jnp.float32)], axis=0)
                square = jnp.concatenate(
                    [tall, jnp.zeros((lanes, lanes - models), jnp.float32)], axis=1)
                turned[(a * 2 + way) * terms + k] = square.T[:turned.shape[1]]


def build_bands(turned, row_base, col_base, count, row_ops, col_ops):
    models, size, width = row_ops.shape
    lanes = col_ops.shape[1]
    terms = width // size

    def build(m, carry):
        row_ops[m] = jnp.concatenate(
            [band_matrix(turned[row_base * terms + k, pl.ds(m, 1)], count, size)[:, :size]
             for k in range(terms)], axis=1)
        for k in range(terms):
            col_ops[m, :, k * lanes:(k + 1) * lanes] = band_matrix(
                turned[col_base * terms + k, pl.ds(m, 1)], count, lanes)
        return carry

    lax.fori_loop(0, models, build, 0)


def fill_lists(fields, lists, row_blocks, col_blocks, lasts):
    lanes = fields.shape[2]
    upper = fields[0] * row_blocks + fields[1]
    block = upper * col_blocks + fields[2]
    square = jnp.broadcast_to(block, (lanes, lanes))
    turned = square.T
    down = lax.broadcasted_iota(jnp.int32, (lanes, lanes), 0)
    across = lax.broadcasted_iota(jnp.int32, (lanes, lanes), 1)
    lists[0:1, :] = jnp.zeros((1, lanes), jnp.int32)
    for r in range(lasts):
        hit = jnp.where(turned == across + r * lanes, down + 1, 0)
        lists[1 + r:2 + r, :] = jnp.max(hit, axis=0, keepdims=True)
    earlier = jnp.where((turned == square) & (down < across), down + 1, 0)
    lists[lasts + 1:lasts + 2, :] = jnp.max(earlier, axis=0, keepdims=True)
    lists[lasts + 2:lasts + 3, :] = upper
    lists[lasts + 3:lasts + 4, :] = fields[2]
    lists[lasts + 4:lasts + 5, :] = fields[3]


def remote(src, dst, send, recv, device):
    return pltpu.make_async_remote_copy(src_ref=src, dst_ref=dst, send_sem=send, recv_sem=recv,
                                        device_id={"tile": device}, device_id_type=MESH)


def whole_kernel(peers, cut, cut2, group, tile_of, row_of, col_of, model_of, row_taps, col_taps,
                 stamps_hbm, cot_hbm, tile_hbm, grads_hbm,
                 sky, sums, stamps_ref, row_fwd, col_fwd, row_bwd, col_bwd, fields, raw, turned,
                 tile_ref, grads_ref, lists_v, lists,
                 out_c, from_c, out_y, from_y, out_z, from_z, out_zb, from_zb, out_yb, from_yb,
                 own_sem, end_sem, za_s, za_r, zb_s, zb_r, ya_s, ya_r, yb_s, yb_r, ca_s, ca_r, cb_s, cb_r,
                 rc_s, rc_r, ry_s, ry_r, rz_s, rz_r, rzb_s, rzb_r, ryb_s, ryb_r):
    planes = peers // 4
    last = planes - 1
    me = lax.axis_index("tile")
    core = lax.rem(me, 2)
    row = lax.rem(me // 2, 2)
    p = me // 4
    count, stamp_rows, stamp_cols = stamps_ref.shape
    groups = count // group
    col_blocks, _, block_rows, _ = sky.shape
    row_blocks = tile_ref.shape[0]
    models = row_fwd.shape[0]
    lasts = peers * row_blocks * col_blocks // count
    PREV, UPPER, COL, MODEL = (lasts + 1 + i for i in range(4))
    rest = row_blocks - cut
    up_ok, down_ok = p < last, p > 0

    def tile_at(q, v=0, c=0):
        y = 1 - row if v else row
        return q * 4 + y * 2 + (1 - core if c else core)

    def part(tile, low, size):
        return sky.at[:, pl.ds(tile * row_blocks + low, size)]

    y_peer, c_peer = tile_at(p, 1), tile_at(p, 0, 1)
    up_peer, down_peer = tile_at(lax.min(p + 1, last)), tile_at(lax.max(p - 1, 0))

    def za(q, way):
        spot = part(tile_at(q), 0, cut)
        slot = way * planes + q
        return remote(spot, spot, za_s.at[slot], za_r.at[slot], down_peer if way else up_peer)

    def zb(q, v, way):
        spot = part(tile_at(q, v), cut, rest)
        slot = (way * 2 + v) * planes + q
        return remote(spot, spot, zb_s.at[slot], zb_r.at[slot], down_peer if way else up_peer)

    def ya(q, far=0):
        spot = part(tile_at(q, far), 0, cut)
        return remote(spot, spot, ya_s.at[q], ya_r.at[q], y_peer)

    def yb(far=0):
        spot = part(tile_at(p, far), cut, rest)
        return remote(spot, spot, yb_s, yb_r, y_peer)

    def ca(q, v, far=0):
        spot = part(tile_at(q, v, far), 0, cut)
        slot = v * planes + q
        return remote(spot, spot, ca_s.at[slot], ca_r.at[slot], c_peer)

    def cb(q, v, far=0):
        spot = part(tile_at(q, v, far), cut, rest)
        slot = v * planes + q
        return remote(spot, spot, cb_s.at[slot], cb_r.at[slot], c_peer)

    def streams(i, body, side=None):
        low = p < planes // 2
        below = True if side is None else (low if side == 0 else jnp.logical_not(low))
        above = True if side is None else (low if side == 1 else jnp.logical_not(low))
        pl.when(jnp.logical_and(p >= i, below))(lambda: body(p - i, 0, up_ok))
        pl.when(jnp.logical_and(p + i <= last, above))(lambda: body(p + i, 1, down_ok))

    def a_step(i):
        def body(q, way, more):
            za(q, way).wait_recv()
            if i < last:
                pl.when(more)(lambda: za(q, way).start())
            ya(q).start()
            ca(q, 0).start()
        streams(i, body)

    def b_step(i, side=None):
        def body(q, way, more):
            for v in range(2):
                zb(q, v, way).wait_recv()
                if i < last:
                    pl.when(more)(lambda: zb(q, v, way).start())
                cb(q, v).start()
        streams(i, body, side)

    def y_step(i):
        def body(q, way, more):
            ya(q, 1).wait_recv()
            ca(q, 1).start()
        if i:
            streams(i, body)
        else:
            body(p, 0, None)

    def apply(g, row_ops, col_ops, image, put):
        chosen_models = [lists[MODEL, g * group + u] for u in range(group)]
        firsts = [jnp.dot(image(g * group + u), col_ops[chosen_models[u]],
                          preferred_element_type=jnp.float32).astype(jnp.bfloat16)
                  for u in range(group)]
        for u in range(group):
            tall = jnp.concatenate(
                [firsts[u][:, k * stamp_cols:(k + 1) * stamp_cols]
                 for k in range(firsts[u].shape[1] // stamp_cols)], axis=0)
            put(g * group + u, jnp.dot(row_ops[chosen_models[u]], tall,
                                       preferred_element_type=jnp.float32).astype(jnp.bfloat16))

    def add(s, value):
        sums[s + 1] = value.astype(jnp.float32) + sums[lists[PREV, s]]

    def forward(g, carry):
        apply(g, row_fwd, col_fwd, lambda s: stamps_ref[s], add)
        return carry

    def window(s):
        upper, col = lists[UPPER, s], lists[COL, s]
        return jnp.concatenate([sky[col, upper], sky[col, upper + 1]], axis=0)

    def grads_out(g):
        spot = pl.ds(g * group, group)
        return pltpu.make_async_copy(grads_ref.at[spot], grads_hbm.at[spot], end_sem.at[2 + g])

    def tile_out(slot, low, high):
        spot = pl.ds(low, high - low)
        return pltpu.make_async_copy(tile_ref.at[spot], tile_hbm.at[spot], end_sem.at[slot])

    def keep_grad(s, value):
        grads_ref[s] = value

    def backward(g, carry):
        apply(g, row_bwd, col_bwd, window, keep_grad)
        grads_out(g).start()
        return carry

    def runner(step):
        reached = [0]

        def run(number):
            stop = min(groups, reached[0] + number)
            if stop > reached[0]:
                lax.fori_loop(reached[0], stop, step, 0)
            reached[0] = stop
        return run

    compute, pull = runner(forward), runner(backward)

    def summed(tile, low, high, put, *others):
        base = tile * (row_blocks * col_blocks)
        width = lists.shape[1]

        def body(r, carry):
            for b in range(col_blocks):
                lower = base + (r * col_blocks + b + width)
                above = lower - col_blocks
                out = (sums[lists[lower // width, lax.rem(lower, width)], :block_rows]
                       + sums[lists[above // width, lax.rem(above, width)], block_rows:])
                for ref, index, shift in others:
                    out = out + ref[index, b, r - shift].astype(jnp.float32)
                put(b, r, out.astype(jnp.bfloat16))
            return carry

        lax.fori_loop(low, high, body, 0)

    half = p // 2
    mirrored = (1 - 2 * half) * p + last * half
    targets = [last * half + (1 - 2 * half) * q for q in (3, 2, 1 - mirrored, mirrored)]

    def rc(v, i):
        slot = v * planes + i
        return remote(out_c.at[slot], from_c.at[slot], rc_s.at[slot], rc_r.at[slot], c_peer)

    def ry(i):
        return remote(out_y.at[i], from_y.at[i], ry_s.at[i], ry_r.at[i], y_peer)

    def way_of(q):
        return jnp.where(q > p, 0, 1)

    def rz(i, slot, device):
        return remote(out_z.at[i], from_z.at[slot], rz_s.at[i], rz_r.at[slot], device)

    def rzb(v, i, slot, device):
        return remote(out_zb.at[v * planes + i], from_zb.at[v * 2 * planes + slot],
                      rzb_s.at[v * planes + i], rzb_r.at[v * 2 * planes + slot], device)

    def ryb():
        return remote(out_yb.at[0], from_yb.at[0], ryb_s, ryb_r, y_peer)

    def into(ref, index, shift):
        def put(b, r, value):
            ref[index, b, r - shift] = value
        return put

    def c_out(v, i):
        slot = v * planes + i
        summed(tile_at(targets[i], v, 1), 0, row_blocks, into(out_c, slot, 0))
        rc(v, i).start()

    def c_in(i):
        rc(0, i).wait_recv()
        rc(1, i).wait_recv()

    def y_out(i):
        summed(tile_at(targets[i], 1), 0, cut2, into(out_y, i, 0), (from_c, planes + i, 0))
        ry(i).start()

    def chain(i, make, tile, low, high, put, *others):
        q = targets[i]
        way = way_of(q)
        slot = way * planes + q
        device = jnp.where(q > p, up_peer, down_peer)
        first = jnp.logical_or(jnp.logical_and(q > p, p == 0), jnp.logical_and(q < p, p == last))
        copy, source, offset = make(slot, device)
        pl.when(first)(lambda: summed(tile, low, high, put, *others))

        @pl.when(jnp.logical_not(first))
        def _():
            copy.wait_recv()
            summed(tile, low, high, put, *others, (source, offset + slot, low))

        copy.start()

    def za_out(i):
        ry(i).wait_recv()
        chain(i, lambda slot, device: (rz(i, slot, device), from_z, 0), tile_at(targets[i]), 0, cut2,
              into(out_z, i, 0), (from_c, i, 0), (from_y, i, 0))

    def zb_out(v, i):
        chain(i, lambda slot, device: (rzb(v, i, slot, device), from_zb, v * 2 * planes),
              tile_at(targets[i], v), cut2, row_blocks, into(out_zb, v * planes + i, cut2),
              (from_c, v * planes + i, 0))

    def ending(make, body):
        def some(*ways):
            made = [make(way * planes + p) for way in ways]
            for copy, _ in made:
                copy.wait_recv()
            body(*[source for _, source in made])

        pl.when(p == 0)(lambda: some(1))
        pl.when(p == last)(lambda: some(0))
        pl.when(jnp.logical_and(p > 0, p < last))(lambda: some(0, 1))

    def yb_out():
        ending(lambda slot: (rzb(1, 0, slot, up_peer), (from_zb, 2 * planes + slot, cut2)),
               lambda *more: summed(tile_at(p, 1), cut2, row_blocks, into(out_yb, 0, cut2),
                                    (from_c, planes + last, 0), *more))
        ryb().start()

    def to_tile(b, r, value):
        tile_ref[r, :, b * stamp_cols:(b + 1) * stamp_cols] = value

    def a_end():
        ry(last).wait_recv()
        ending(lambda slot: (rz(0, slot, up_peer), (from_z, slot, 0)),
               lambda *more: summed(me, 0, cut2, to_tile, (from_c, last, 0), (from_y, last, 0), *more))

    def b_end():
        ryb().wait_recv()
        ending(lambda slot: (rzb(0, 0, slot, up_peer), (from_zb, slot, cut2)),
               lambda *more: summed(me, cut2, row_blocks, to_tile, (from_c, last, 0),
                                    (from_yb, 0, cut2), *more))

    barrier = pltpu.get_barrier_semaphore()

    def greet(device):
        pl.semaphore_signal(barrier, inc=1, device_id={"tile": device}, device_id_type=MESH)

    pl.when(up_ok)(lambda: greet(up_peer))
    pl.when(down_ok)(lambda: greet(down_peer))
    greet(y_peer)
    greet(c_peer)
    own = [pltpu.make_async_copy(cot_hbm.at[:, :, pl.ds(b * stamp_cols, stamp_cols)],
                                 sky.at[b, pl.ds(me * row_blocks, row_blocks)], own_sem.at[b])
           for b in range(col_blocks)]
    small = [pltpu.make_async_copy(source, target, own_sem.at[col_blocks + 2 + n])
             for n, (source, target) in enumerate(
                 [(array, fields.at[n]) for n, array in enumerate((tile_of, row_of, col_of, model_of))]
                 + [(row_taps, raw.at[0]), (col_taps, raw.at[1])])]
    fetch = pltpu.make_async_copy(stamps_hbm, stamps_ref, own_sem.at[col_blocks])
    for copy in own + small:
        copy.start()
    fetch.start()
    for b in range(col_blocks):
        sky[b, peers * row_blocks] = jnp.zeros((block_rows, stamp_cols), jnp.bfloat16)
    sums[0] = jnp.zeros((stamp_rows, stamp_cols), jnp.float32)
    for copy in small:
        copy.wait()
    fill_lists(fields, lists_v, row_blocks, col_blocks, lasts)
    listing = pltpu.make_async_copy(lists_v, lists, own_sem.at[col_blocks + 1])
    listing.start()
    turn_taps(raw, turned)
    taps = raw.shape[2]
    for copy in own:
        copy.wait()
    pl.semaphore_wait(barrier, 2 + jnp.where(up_ok, 1, 0) + jnp.where(down_ok, 1, 0))
    whole = part(me, 0, row_blocks)
    own_c = remote(whole, whole, ca_s.at[p], ca_r.at[p], c_peer)
    pl.when(up_ok)(lambda: za(p, 0).start())
    pl.when(down_ok)(lambda: za(p, 1).start())
    yb().start()
    ya(p).start()
    own_c.start()
    build_bands(turned, 0, 3, taps, row_fwd, col_fwd)
    listing.wait()
    fetch.wait()

    def ends(body):
        pl.when(jnp.logical_or(p == 0, p == last))(body)

    def middles(body):
        pl.when(jnp.logical_and(p > 0, p < last))(body)

    def zb_own():
        for v in range(2):
            pl.when(up_ok)(lambda: zb(p, v, 0).start())
            pl.when(down_ok)(lambda: zb(p, v, 1).start())

    def c_pair(i):
        c_out(0, i)
        c_out(1, i)

    def zb_both(i):
        for v in range(2):
            zb_out(v, i)

    compute(4)
    yb(1).wait_recv()
    cb(p, 1).start()
    a_step(1)
    ends(zb_own)
    compute(groups)
    c_pair(0)
    c_pair(1)
    middles(zb_own)
    y_step(0)
    a_step(2)
    c_in(0)
    ends(lambda: zb_both(0))
    y_out(0)
    b_step(1, 0)
    c_pair(2)
    c_pair(3)
    c_in(1)
    y_out(1)
    y_step(1)
    build_bands(turned, 1, 2, taps, row_bwd, col_bwd)
    c_in(2)
    c_in(3)
    a_step(3)
    ends(lambda: zb_both(1))
    b_step(1, 1)
    middles(lambda: zb_both(0))
    y_out(2)
    ends(lambda: za_out(0))
    y_step(2)
    y_out(3)
    b_step(2)
    y_step(3)

    @middles
    def _():
        zb_both(1)
        zb_both(2)
        za_out(0)

    @ends
    def _():
        za_out(1)
        zb_both(2)

    b_step(3)
    ends(lambda: za_out(2))

    def arrived():
        for v in range(2):
            for q in range(planes):
                def two():
                    ca(q, v, 1).wait_recv()
                    cb(q, v, 1).wait_recv()

                if v:
                    two()
                else:
                    pl.when(q != p)(two)
        whole_far = part(c_peer, 0, row_blocks)
        remote(whole_far, whole_far, ca_s.at[p], ca_r.at[p], c_peer).wait_recv()

    arrived()
    pull(2)

    @middles
    def _():
        za_out(1)
        za_out(2)

    pull(2)
    yb_out()
    pull(groups)
    a_end()
    tile_out(0, 0, cut2).start()
    b_end()
    tile_out(1, cut2, row_blocks).start()
    for copy in (tile_out(0, 0, cut2), tile_out(1, cut2, row_blocks)):
        copy.wait()

    def written(g, carry):
        grads_out(g).wait()
        return carry

    lax.fori_loop(0, groups, written, 0)

    pl.when(up_ok)(lambda: za(p, 0).wait_send())
    pl.when(down_ok)(lambda: za(p, 1).wait_send())
    yb().wait_send()
    own_c.wait_send()
    cb(p, 1).wait_send()
    ca(p, 1).wait_send()
    ya(p).wait_send()
    for v in range(2):
        pl.when(up_ok)(lambda: zb(p, v, 0).wait_send())
        pl.when(down_ok)(lambda: zb(p, v, 1).wait_send())
    for i in range(1, planes):
        def ended(q, way, more):
            ya(q).wait_send()
            for v in range(2):
                ca(q, v).wait_send()
                cb(q, v).wait_send()
            if i < last:
                @pl.when(more)
                def _():
                    za(q, way).wait_send()
                    for v in range(2):
                        zb(q, v, way).wait_send()
        streams(i, ended)
    for i in range(planes):
        for v in range(2):
            rc(v, i).wait_send()
        ry(i).wait_send()
    for i in range(last):
        rz(i, i, up_peer).wait_send()
        for v in range(2):
            rzb(v, i, i, up_peer).wait_send()
    ryb().wait_send()


def divisor(number, wanted):
    return max(d for d in range(1, wanted + 1) if number % d == 0)


def hand_over(parts, tile_from, grads_from, tile_to, grads_to, tile_held, grads_held, sem_in, sem_out):
    size = grads_from.shape[0] // parts
    spots = [pl.ds(n * size, size) for n in range(parts)]
    copies = [(tile_from, tile_held, tile_to)] + [
        (grads_from.at[spot], grads_held.at[spot], grads_to.at[spot]) for spot in spots]
    copies = [(pltpu.make_async_copy(source, held, sem_in.at[n]),
               pltpu.make_async_copy(held, target, sem_out.at[n]))
              for n, (source, held, target) in enumerate(copies)]
    for fetch, _ in copies:
        fetch.start()
    for fetch, put in copies:
        fetch.wait()
        put.start()
    for _, put in copies:
        put.wait()


def in_place(stamps, tile_of, row_offset, col_offset, psf_model, psf_rows, psf_cols, cotangent):
    peers = lax.axis_size("tile")
    planes = peers // 4
    stamp_count, stamp_rows, stamp_cols = stamps.shape
    models, terms, taps = psf_rows.shape
    block_rows = stamp_rows // 2
    tile_rows, tile_cols = cotangent.shape
    row_blocks = tile_rows // block_rows
    col_blocks = tile_cols // stamp_cols
    cut = row_blocks * 5 // 8
    cut2 = row_blocks * 5 // 8
    group = divisor(stamp_count, 16)
    lasts = peers * row_blocks * col_blocks // stamp_count
    list_rows = -(-(lasts + 5) // 8) * 8
    model_rows = -(-models // 8) * 8
    flops = 2 * stamp_count * terms * stamp_rows * stamp_cols * (stamp_rows + stamp_cols)
    cost = pl.CostEstimate(flops=8 * flops, bytes_accessed=40 << 20, transcendentals=0)
    hbm = pl.BlockSpec(memory_space=pltpu.HBM)
    short = jnp.bfloat16
    dma = pltpu.SemaphoreType.DMA
    piece = (block_rows, stamp_cols)
    full, upper, lower = ((col_blocks, rows) + piece for rows in (row_blocks, cut2, row_blocks - cut2))
    line = lambda array: array.reshape((1, stamp_count))
    outs = (
        jax.ShapeDtypeStruct((row_blocks, block_rows, tile_cols), short),
        jax.ShapeDtypeStruct(stamps.shape, short),
    )
    row_op, col_op = ((models, size, terms * size) for size in (stamp_rows, stamp_cols))

    made = pl.pallas_call(
        partial(whole_kernel, peers, cut, cut2, group),
        out_shape=outs,
        in_specs=[hbm] * 8,
        out_specs=(hbm, hbm),
        scratch_shapes=[
            pltpu.VMEM((col_blocks, peers * row_blocks + 1) + piece, short),
            pltpu.VMEM((stamp_count + 1, stamp_rows, stamp_cols), jnp.float32),
            pltpu.VMEM(stamps.shape, short),
            pltpu.VMEM(row_op, short),
            pltpu.VMEM(col_op, short),
            pltpu.VMEM(row_op, short),
            pltpu.VMEM(col_op, short),
            pltpu.VMEM((4, 1, stamp_count), jnp.int32),
            pltpu.VMEM((2, terms, taps, models), jnp.float32),
            pltpu.VMEM((4 * terms, model_rows, stamp_count), jnp.float32),
            pltpu.VMEM(outs[0].shape, short),
            pltpu.VMEM(stamps.shape, short),
            pltpu.VMEM((list_rows, stamp_count), jnp.int32),
            pltpu.SMEM((list_rows, stamp_count), jnp.int32),
            pltpu.VMEM((2 * planes,) + full, short),
            pltpu.VMEM((2 * planes,) + full, short),
            pltpu.VMEM((planes,) + upper, short),
            pltpu.VMEM((planes,) + upper, short),
            pltpu.VMEM((planes,) + upper, short),
            pltpu.VMEM((2 * planes,) + upper, short),
            pltpu.VMEM((2 * planes,) + lower, short),
            pltpu.VMEM((4 * planes,) + lower, short),
            pltpu.VMEM((1,) + lower, short),
            pltpu.VMEM((1,) + lower, short),
            dma((col_blocks + 8,)), dma((2 + stamp_count // group,)),
        ] + [dma((2 * planes,))] * 2 + [dma((4 * planes,))] * 2 + [dma((planes,))] * 2 + [dma, dma]
        + [dma((2 * planes,))] * 4
        + [dma((2 * planes,))] * 2 + [dma((planes,))] * 2 + [dma((planes,)), dma((2 * planes,))]
        + [dma((2 * planes,)), dma((4 * planes,))] + [dma, dma],
        compiler_params=pltpu.CompilerParams(collective_id=0, has_side_effects=True,
                                             vmem_limit_bytes=60 << 20),
        cost_estimate=cost,
    )(tile_of.reshape((1, stamp_count)), line(row_offset), line(col_offset), line(psf_model),
      psf_rows.transpose(1, 2, 0), psf_cols.transpose(1, 2, 0),
      stamps, cotangent.reshape(outs[0].shape))
    parts = divisor(stamp_count, 8)
    tile_image, stamp_grad = pl.pallas_call(
        partial(hand_over, parts), out_shape=outs, in_specs=[hbm, hbm], out_specs=(hbm, hbm),
        scratch_shapes=[pltpu.VMEM(out.shape, short) for out in outs] + [dma((parts + 1,))] * 2,
    )(*made)
    return tile_image.reshape(cotangent.shape), stamp_grad


def fits(stamps, cotangent):
    count, rows, cols = stamps.shape
    peers = lax.axis_size("tile")
    return (peers == 16 and count == 128 and cols == 128 and rows % 32 == 0 and rows <= 128
            and peers * cotangent.shape[0] * cotangent.shape[1] * 4 <= 12 << 20)


def per_device_any(*args):
    if fits(args[0], args[-1]):
        return in_place(*args)
    return per_device(*args)


def solution(mesh):
    in_specs = (
        P(("band", "tile"), None, None),
        P(("band", "tile"), None),
        P(("band", "tile")),
        P(("band", "tile")),
        P(("band", "tile")),
        P("band", None, None),
        P("band", None, None),
        P(("band", "tile"), None),
    )
    out_specs = (P(("band", "tile"), None), P(("band", "tile"), None, None))
    return jax.shard_map(
        per_device_any, mesh=mesh, in_specs=in_specs, out_specs=out_specs, check_vma=False
    )
```

```python
from functools import partial

import jax
import jax.numpy as jnp
from jax import lax
from jax.experimental import pallas as pl
from jax.experimental.pallas import tpu as pltpu
from jax.sharding import PartitionSpec as P


def passed_along(array, axis, by):
    peers = lax.axis_size(axis)
    pairs = [(i, i + by) for i in range(peers) if 0 <= i + by < peers]
    return lax.ppermute(array, axis, pairs)


def for_sending(array):

    def short(part):
        return part.astype(jnp.bfloat16) if part.dtype == jnp.float32 else part

    return jax.tree.map(short, array)


def band_table(taps_count, size):
    half_width = (taps_count - 1) // 2
    places = jnp.arange(size, dtype=jnp.int32)
    offsets = places[None, :] - places[:, None] + half_width
    taps_index = jnp.arange(taps_count, dtype=jnp.int32)
    table = (offsets[None, :, :] == taps_index[:, None, None]).astype(jnp.float32)
    return table.reshape((taps_count, size * size))


def build_ops(profiles, size):
    model_total, term_total, taps_count = profiles.shape
    table = band_table(taps_count, size)
    mats = jnp.dot(
        profiles.reshape((model_total * term_total, taps_count)),
        table,
        precision=lax.Precision.HIGHEST,
    )
    return mats.reshape((model_total, term_total, size, size)).astype(jnp.bfloat16)


def chosen(ops, models):
    model_total, term_total, size, _ = ops.shape
    picks = (models[:, None] == jnp.arange(model_total, dtype=jnp.int32)[None, :]).astype(ops.dtype)
    mats = jnp.dot(picks, ops.reshape((model_total, -1)), preferred_element_type=jnp.float32)
    return mats.astype(ops.dtype).reshape((models.shape[0], term_total, size, size))


def convolve_some(images, row_mats, col_mats):
    row_pass = jnp.einsum(
        "bkij,bjx->bkix", row_mats, images, preferred_element_type=jnp.float32
    ).astype(jnp.bfloat16)
    return jnp.einsum(
        "bkix,bkyx->biy", row_pass, col_mats, preferred_element_type=jnp.float32
    ).astype(jnp.bfloat16)


def transpose_some(windows, row_mats, col_mats):
    back_pass = jnp.einsum(
        "biy,bkyx->bkix", windows, col_mats, preferred_element_type=jnp.float32
    ).astype(jnp.bfloat16)
    return jnp.einsum(
        "bkji,bkjx->bix", row_mats, back_pass, preferred_element_type=jnp.float32
    ).astype(jnp.bfloat16)


def apply_all(function, images, models, row_ops, col_ops):
    batch = divisor(images.shape[0], 32)

    def some(inputs):
        part, part_models = inputs
        return function(part, chosen(row_ops, part_models), chosen(col_ops, part_models))

    cut = images.reshape((-1, batch) + images.shape[1:])
    return lax.map(some, (cut, models.astype(jnp.int32).reshape((-1, batch)))).reshape(images.shape)


def per_device(stamps, tile_of, row_offset, col_offset, psf_model, psf_rows, psf_cols, cotangent):
    peer_count = lax.axis_size("tile")
    stamp_count, stamp_rows, stamp_cols = stamps.shape
    block_rows = stamp_rows // 2
    tile_rows, tile_cols = cotangent.shape
    row_blocks = tile_rows // block_rows
    col_blocks = tile_cols // stamp_cols
    capacity = max(2, (5 * stamp_count + 4 * peer_count - 1) // (4 * peer_count))
    slot_total = peer_count * capacity
    row_ops = build_ops(psf_rows, stamp_rows)
    col_ops = build_ops(psf_cols, stamp_cols)
    target = tile_of[:, 0]
    order = jnp.arange(stamp_count, dtype=jnp.int32)
    earlier = (target[None, :] == target[:, None]) & (order[None, :] < order[:, None])
    slots = target * capacity + jnp.sum(earlier.astype(jnp.int32), axis=1)
    slot_ids = jnp.arange(slot_total, dtype=jnp.int32)
    matches = slots[None, :] == slot_ids[:, None]
    place = matches.astype(jnp.bfloat16)
    details = jnp.stack([jnp.ones_like(target), row_offset, col_offset, psf_model], axis=1)
    detail_send = jnp.sum(jnp.where(matches[:, :, None], details[None, :, :], 0), axis=1)
    detail_send = detail_send.reshape(peer_count, capacity, 4)
    raw_send = jnp.dot(
        place,
        stamps.reshape((stamp_count, stamp_rows * stamp_cols)),
        preferred_element_type=jnp.float32,
    )
    raw_send = raw_send.astype(jnp.bfloat16).reshape(peer_count, capacity, stamp_rows, stamp_cols)
    raw_part = lax.all_to_all(raw_send, "tile", split_axis=0, concat_axis=0, tiled=True)
    info_part = lax.all_to_all(detail_send, "tile", split_axis=0, concat_axis=0, tiled=True)
    flat = raw_part.reshape((-1, stamp_rows, stamp_cols))
    result = apply_all(convolve_some, flat, info_part.reshape((-1, 4))[:, 3], row_ops, col_ops)
    received = result.reshape(raw_part.shape)
    info_flat = info_part.reshape((slot_total, 4))
    upper_block = info_flat[:, 1]
    block_ids = jnp.stack([upper_block, upper_block + 1], axis=1) * col_blocks + info_flat[:, 2:3]
    targets = jnp.arange((row_blocks + 1) * col_blocks, dtype=jnp.int32)
    placing = (block_ids.reshape(-1)[None, :] == targets[:, None]).astype(jnp.bfloat16)
    pieces = received.reshape((slot_total * 2, block_rows * stamp_cols))
    extended = jnp.dot(placing, pieces, preferred_element_type=jnp.float32)
    extended = extended.reshape(row_blocks + 1, col_blocks, block_rows, stamp_cols).transpose(
        0, 2, 1, 3
    )
    extended = extended.reshape((row_blocks + 1) * block_rows, tile_cols)
    arriving = passed_along(extended[tile_rows:].astype(jnp.bfloat16), "tile", 1).astype(
        jnp.float32
    )
    tile_sum = extended[:tile_rows].at[:block_rows].add(arriving)
    tile_image = tile_sum.astype(jnp.bfloat16)
    rim = passed_along(cotangent[:block_rows], "tile", -1)
    padded = jnp.concatenate([cotangent, rim], axis=0)
    blocks = padded.reshape(row_blocks + 1, block_rows, col_blocks, stamp_cols).transpose(
        0, 2, 1, 3
    )
    blocks = blocks.reshape((row_blocks + 1) * col_blocks, block_rows * stamp_cols)
    windows = lax.dot_general(
        placing, blocks, (((0,), (0,)), ((), ())), preferred_element_type=jnp.float32
    )
    windows = windows.astype(jnp.bfloat16).reshape(slot_total, stamp_rows, stamp_cols)
    slot_grads = apply_all(transpose_some, windows, info_flat[:, 3], row_ops, col_ops)
    slot_grads = slot_grads.reshape(peer_count, capacity, stamp_rows, stamp_cols)
    returned = lax.all_to_all(
        for_sending(slot_grads), "tile", split_axis=0, concat_axis=0, tiled=True
    ).astype(slot_grads.dtype)
    stamp_grad = lax.dot_general(
        place,
        returned.reshape((slot_total, stamp_rows * stamp_cols)),
        (((0,), (0,)), ((), ())),
        preferred_element_type=jnp.float32,
    )
    stamp_grad = stamp_grad.astype(jnp.bfloat16).reshape(stamp_count, stamp_rows, stamp_cols)
    return (tile_image, stamp_grad)


MESH = pl.DeviceIdType.MESH


def band_matrix(row, count, rows):
    lanes = row.shape[1]
    half = (count - 1) // 2
    spread = jnp.broadcast_to(row, (rows, lanes))
    turned = pltpu.roll(spread, lanes - half, 1, stride=1, stride_axis=0)
    down = lax.broadcasted_iota(jnp.int32, (rows, lanes), 0)
    across = lax.broadcasted_iota(jnp.int32, (rows, lanes), 1)
    return jnp.where(jnp.abs(across - down) <= half, turned, 0.0).astype(jnp.bfloat16)


def turn_taps(raw, turned):
    _, terms, count, models = raw.shape
    lanes = turned.shape[2]
    for a in range(2):
        for k in range(terms):
            values = raw[a, k]
            for way in range(2):
                rows = [values[count - 1 - t:count - t] for t in range(count)] if way else [values]
                tall = jnp.concatenate(rows + [jnp.zeros((lanes - count, models), jnp.float32)], axis=0)
                square = jnp.concatenate(
                    [tall, jnp.zeros((lanes, lanes - models), jnp.float32)], axis=1)
                turned[(a * 2 + way) * terms + k] = square.T[:turned.shape[1]]


def build_bands(turned, row_base, col_base, count, row_ops, col_ops):
    models, size, width = row_ops.shape
    lanes = col_ops.shape[1]
    terms = width // size

    def build(m, carry):
        row_ops[m] = jnp.concatenate(
            [band_matrix(turned[row_base * terms + k, pl.ds(m, 1)], count, size)[:, :size]
             for k in range(terms)], axis=1)
        for k in range(terms):
            col_ops[m, :, k * lanes:(k + 1) * lanes] = band_matrix(
                turned[col_base * terms + k, pl.ds(m, 1)], count, lanes)
        return carry

    lax.fori_loop(0, models, build, 0)


def fill_lists(fields, lists, row_blocks, col_blocks, lasts):
    lanes = fields.shape[2]
    upper = fields[0] * row_blocks + fields[1]
    block = upper * col_blocks + fields[2]
    square = jnp.broadcast_to(block, (lanes, lanes))
    turned = square.T
    down = lax.broadcasted_iota(jnp.int32, (lanes, lanes), 0)
    across = lax.broadcasted_iota(jnp.int32, (lanes, lanes), 1)
    lists[0:1, :] = jnp.zeros((1, lanes), jnp.int32)
    for r in range(lasts):
        hit = jnp.where(turned == across + r * lanes, down + 1, 0)
        lists[1 + r:2 + r, :] = jnp.max(hit, axis=0, keepdims=True)
    earlier = jnp.where((turned == square) & (down < across), down + 1, 0)
    lists[lasts + 1:lasts + 2, :] = jnp.max(earlier, axis=0, keepdims=True)
    lists[lasts + 2:lasts + 3, :] = upper
    lists[lasts + 3:lasts + 4, :] = fields[2]
    lists[lasts + 4:lasts + 5, :] = fields[3]


def remote(src, dst, send, recv, device):
    return pltpu.make_async_remote_copy(src_ref=src, dst_ref=dst, send_sem=send, recv_sem=recv,
                                        device_id={"tile": device}, device_id_type=MESH)


def whole_kernel(peers, cut, cut2, group, tile_of, row_of, col_of, model_of, row_taps, col_taps,
                 stamps_hbm, cot_hbm, tile_hbm, grads_hbm,
                 sky, sums, stamps_ref, row_fwd, col_fwd, row_bwd, col_bwd, fields, raw, turned,
                 tile_ref, grads_ref, lists_v, lists,
                 out_c, from_c, out_y, from_y, out_z, from_z, out_zb, from_zb, out_yb, from_yb,
                 own_sem, end_sem, za_s, za_r, zb_s, zb_r, ya_s, ya_r, yb_s, yb_r, ca_s, ca_r, cb_s, cb_r,
                 rc_s, rc_r, ry_s, ry_r, rz_s, rz_r, rzb_s, rzb_r, ryb_s, ryb_r):
    planes = peers // 4
    last = planes - 1
    me = lax.axis_index("tile")
    core = lax.rem(me, 2)
    row = lax.rem(me // 2, 2)
    p = me // 4
    count, stamp_rows, stamp_cols = stamps_ref.shape
    groups = count // group
    col_blocks, _, block_rows, _ = sky.shape
    row_blocks = tile_ref.shape[0]
    models = row_fwd.shape[0]
    lasts = peers * row_blocks * col_blocks // count
    PREV, UPPER, COL, MODEL = (lasts + 1 + i for i in range(4))
    rest = row_blocks - cut
    up_ok, down_ok = p < last, p > 0

    def tile_at(q, v=0, c=0):
        y = 1 - row if v else row
        return q * 4 + y * 2 + (1 - core if c else core)

    def part(tile, low, size):
        return sky.at[:, pl.ds(tile * row_blocks + low, size)]

    y_peer, c_peer = tile_at(p, 1), tile_at(p, 0, 1)
    up_peer, down_peer = tile_at(lax.min(p + 1, last)), tile_at(lax.max(p - 1, 0))

    def za(q, way):
        spot = part(tile_at(q), 0, cut)
        slot = way * planes + q
        return remote(spot, spot, za_s.at[slot], za_r.at[slot], down_peer if way else up_peer)

    def zb(q, v, way):
        spot = part(tile_at(q, v), cut, rest)
        slot = (way * 2 + v) * planes + q
        return remote(spot, spot, zb_s.at[slot], zb_r.at[slot], down_peer if way else up_peer)

    def ya(q, far=0):
        spot = part(tile_at(q, far), 0, cut)
        return remote(spot, spot, ya_s.at[q], ya_r.at[q], y_peer)

    def yb(far=0):
        spot = part(tile_at(p, far), cut, rest)
        return remote(spot, spot, yb_s, yb_r, y_peer)

    def ca(q, v, far=0):
        spot = part(tile_at(q, v, far), 0, cut)
        slot = v * planes + q
        return remote(spot, spot, ca_s.at[slot], ca_r.at[slot], c_peer)

    def cb(q, v, far=0):
        spot = part(tile_at(q, v, far), cut, rest)
        slot = v * planes + q
        return remote(spot, spot, cb_s.at[slot], cb_r.at[slot], c_peer)

    def streams(i, body, side=None):
        low = p < planes // 2
        below = True if side is None else (low if side == 0 else jnp.logical_not(low))
        above = True if side is None else (low if side == 1 else jnp.logical_not(low))
        pl.when(jnp.logical_and(p >= i, below))(lambda: body(p - i, 0, up_ok))
        pl.when(jnp.logical_and(p + i <= last, above))(lambda: body(p + i, 1, down_ok))

    def a_step(i):
        def body(q, way, more):
            za(q, way).wait_recv()
            if i < last:
                pl.when(more)(lambda: za(q, way).start())
            ya(q).start()
            ca(q, 0).start()
        streams(i, body)

    def b_step(i, side=None):
        def body(q, way, more):
            for v in range(2):
                zb(q, v, way).wait_recv()
                if i < last:
                    pl.when(more)(lambda: zb(q, v, way).start())
                cb(q, v).start()
        streams(i, body, side)

    def y_step(i):
        def body(q, way, more):
            ya(q, 1).wait_recv()
            ca(q, 1).start()
        if i:
            streams(i, body)
        else:
            body(p, 0, None)

    def apply(g, row_ops, col_ops, image, put):
        chosen_models = [lists[MODEL, g * group + u] for u in range(group)]
        firsts = [jnp.dot(image(g * group + u), col_ops[chosen_models[u]],
                          preferred_element_type=jnp.float32).astype(jnp.bfloat16)
                  for u in range(group)]
        for u in range(group):
            tall = jnp.concatenate(
                [firsts[u][:, k * stamp_cols:(k + 1) * stamp_cols]
                 for k in range(firsts[u].shape[1] // stamp_cols)], axis=0)
            put(g * group + u, jnp.dot(row_ops[chosen_models[u]], tall,
                                       preferred_element_type=jnp.float32).astype(jnp.bfloat16))

    def add(s, value):
        sums[s + 1] = value.astype(jnp.float32) + sums[lists[PREV, s]]

    def forward(g, carry):
        apply(g, row_fwd, col_fwd, lambda s: stamps_ref[s], add)
        return carry

    def window(s):
        upper, col = lists[UPPER, s], lists[COL, s]
        return jnp.concatenate([sky[col, upper], sky[col, upper + 1]], axis=0)

    def grads_out(g):
        spot = pl.ds(g * group, group)
        return pltpu.make_async_copy(grads_ref.at[spot], grads_hbm.at[spot], end_sem.at[2 + g])

    def tile_out(slot, low, high):
        spot = pl.ds(low, high - low)
        return pltpu.make_async_copy(tile_ref.at[spot], tile_hbm.at[spot], end_sem.at[slot])

    def keep_grad(s, value):
        grads_ref[s] = value

    def backward(g, carry):
        apply(g, row_bwd, col_bwd, window, keep_grad)
        grads_out(g).start()
        return carry

    def runner(step):
        reached = [0]

        def run(number):
            stop = min(groups, reached[0] + number)
            if stop > reached[0]:
                lax.fori_loop(reached[0], stop, step, 0)
            reached[0] = stop
        return run

    compute, pull = runner(forward), runner(backward)

    def summed(tile, low, high, put, *others, cols=None):
        base = tile * (row_blocks * col_blocks)
        width = lists.shape[1]

        def body(r, carry):
            for b in cols or range(col_blocks):
                lower = base + (r * col_blocks + b + width)
                above = lower - col_blocks
                out = (sums[lists[lower // width, lax.rem(lower, width)], :block_rows]
                       + sums[lists[above // width, lax.rem(above, width)], block_rows:])
                for ref, index, shift in others:
                    out = out + ref[index, b, r - shift].astype(jnp.float32)
                put(b, r, out.astype(jnp.bfloat16))
            return carry

        lax.fori_loop(low, high, body, 0)

    half = p // 2
    mirrored = (1 - 2 * half) * p + last * half
    targets = [last * half + (1 - 2 * half) * q for q in (3, 2, 1 - mirrored, mirrored)]

    def rc(v, i):
        slot = v * planes + i
        return remote(out_c.at[slot], from_c.at[slot], rc_s.at[slot], rc_r.at[slot], c_peer)

    wide = col_blocks // 2
    sides = [range(h * wide, (h + 1) * wide) for h in range(2)]

    def side(h):
        return pl.ds(h * wide, wide)

    def ry(i, h):
        return remote(out_y.at[i, side(h)], from_y.at[i, side(h)],
                      ry_s.at[2 * i + h], ry_r.at[2 * i + h], y_peer)

    def way_of(q):
        return jnp.where(q > p, 0, 1)

    def rz(i, slot, device, h):
        return remote(out_z.at[i, side(h)], from_z.at[slot, side(h)],
                      rz_s.at[2 * i + h], rz_r.at[2 * slot + h], device)

    def rzb(v, i, slot, device):
        return remote(out_zb.at[v * planes + i], from_zb.at[v * 2 * planes + slot],
                      rzb_s.at[v * planes + i], rzb_r.at[v * 2 * planes + slot], device)

    def ryb():
        return remote(out_yb.at[0], from_yb.at[0], ryb_s, ryb_r, y_peer)

    def into(ref, index, shift):
        def put(b, r, value):
            ref[index, b, r - shift] = value
        return put

    def c_out(v, i):
        slot = v * planes + i
        summed(tile_at(targets[i], v, 1), 0, row_blocks, into(out_c, slot, 0))
        rc(v, i).start()

    def c_in(i):
        rc(0, i).wait_recv()
        rc(1, i).wait_recv()

    def y_out(i):
        for h in range(2):
            summed(tile_at(targets[i], 1), 0, cut2, into(out_y, i, 0), (from_c, planes + i, 0),
                   cols=sides[h])
            ry(i, h).start()

    def chain(i, make, tile, low, high, put, *others, cols=None):
        q = targets[i]
        way = way_of(q)
        slot = way * planes + q
        device = jnp.where(q > p, up_peer, down_peer)
        first = jnp.logical_or(jnp.logical_and(q > p, p == 0), jnp.logical_and(q < p, p == last))
        copy, source, offset = make(slot, device)
        pl.when(first)(lambda: summed(tile, low, high, put, *others, cols=cols))

        @pl.when(jnp.logical_not(first))
        def _():
            copy.wait_recv()
            summed(tile, low, high, put, *others, (source, offset + slot, low), cols=cols)

        copy.start()

    def za_out(i):
        for h in range(2):
            ry(i, h).wait_recv()
            chain(i, lambda slot, device: (rz(i, slot, device, h), from_z, 0), tile_at(targets[i]),
                  0, cut2, into(out_z, i, 0), (from_c, i, 0), (from_y, i, 0), cols=sides[h])

    def zb_out(v, i):
        chain(i, lambda slot, device: (rzb(v, i, slot, device), from_zb, v * 2 * planes),
              tile_at(targets[i], v), cut2, row_blocks, into(out_zb, v * planes + i, cut2),
              (from_c, v * planes + i, 0))

    def ending(make, body):
        def some(*ways):
            made = [make(way * planes + p) for way in ways]
            for copy, _ in made:
                copy.wait_recv()
            body(*[source for _, source in made])

        pl.when(p == 0)(lambda: some(1))
        pl.when(p == last)(lambda: some(0))
        pl.when(jnp.logical_and(p > 0, p < last))(lambda: some(0, 1))

    def yb_out():
        ending(lambda slot: (rzb(1, 0, slot, up_peer), (from_zb, 2 * planes + slot, cut2)),
               lambda *more: summed(tile_at(p, 1), cut2, row_blocks, into(out_yb, 0, cut2),
                                    (from_c, planes + last, 0), *more))
        ryb().start()

    def to_tile(b, r, value):
        tile_ref[r, :, b * stamp_cols:(b + 1) * stamp_cols] = value

    def a_end():
        for h in range(2):
            ry(last, h).wait_recv()
            ending(lambda slot: (rz(0, slot, up_peer, h), (from_z, slot, 0)),
                   lambda *more: summed(me, 0, cut2, to_tile, (from_c, last, 0), (from_y, last, 0),
                                        *more, cols=sides[h]))

    def b_end():
        ryb().wait_recv()
        ending(lambda slot: (rzb(0, 0, slot, up_peer), (from_zb, slot, cut2)),
               lambda *more: summed(me, cut2, row_blocks, to_tile, (from_c, last, 0),
                                    (from_yb, 0, cut2), *more))

    barrier = pltpu.get_barrier_semaphore()

    def greet(device):
        pl.semaphore_signal(barrier, inc=1, device_id={"tile": device}, device_id_type=MESH)

    pl.when(up_ok)(lambda: greet(up_peer))
    pl.when(down_ok)(lambda: greet(down_peer))
    greet(y_peer)
    greet(c_peer)
    own = [pltpu.make_async_copy(cot_hbm.at[:, :, pl.ds(b * stamp_cols, stamp_cols)],
                                 sky.at[b, pl.ds(me * row_blocks, row_blocks)], own_sem.at[b])
           for b in range(col_blocks)]
    small = [pltpu.make_async_copy(source, target, own_sem.at[col_blocks + 2 + n])
             for n, (source, target) in enumerate(
                 [(array, fields.at[n]) for n, array in enumerate((tile_of, row_of, col_of, model_of))]
                 + [(row_taps, raw.at[0]), (col_taps, raw.at[1])])]
    fetch = pltpu.make_async_copy(stamps_hbm, stamps_ref, own_sem.at[col_blocks])
    for copy in own + small:
        copy.start()
    fetch.start()
    for b in range(col_blocks):
        sky[b, peers * row_blocks] = jnp.zeros((block_rows, stamp_cols), jnp.bfloat16)
    sums[0] = jnp.zeros((stamp_rows, stamp_cols), jnp.float32)
    for copy in small:
        copy.wait()
    fill_lists(fields, lists_v, row_blocks, col_blocks, lasts)
    listing = pltpu.make_async_copy(lists_v, lists, own_sem.at[col_blocks + 1])
    listing.start()
    turn_taps(raw, turned)
    taps = raw.shape[2]
    for copy in own:
        copy.wait()
    pl.semaphore_wait(barrier, 2 + jnp.where(up_ok, 1, 0) + jnp.where(down_ok, 1, 0))
    whole = part(me, 0, row_blocks)
    own_c = remote(whole, whole, ca_s.at[p], ca_r.at[p], c_peer)
    pl.when(up_ok)(lambda: za(p, 0).start())
    pl.when(down_ok)(lambda: za(p, 1).start())
    yb().start()
    ya(p).start()
    own_c.start()
    build_bands(turned, 0, 3, taps, row_fwd, col_fwd)
    listing.wait()
    fetch.wait()

    def ends(body):
        pl.when(jnp.logical_or(p == 0, p == last))(body)

    def middles(body):
        pl.when(jnp.logical_and(p > 0, p < last))(body)

    def zb_own():
        for v in range(2):
            pl.when(up_ok)(lambda: zb(p, v, 0).start())
            pl.when(down_ok)(lambda: zb(p, v, 1).start())

    def c_pair(i):
        c_out(0, i)
        c_out(1, i)

    def zb_both(i):
        for v in range(2):
            zb_out(v, i)

    compute(4)
    yb(1).wait_recv()
    cb(p, 1).start()
    a_step(1)
    ends(zb_own)
    compute(groups)
    c_pair(0)
    c_pair(1)
    middles(zb_own)
    y_step(0)
    a_step(2)
    c_in(0)
    ends(lambda: zb_both(0))
    y_out(0)
    b_step(1, 0)
    c_pair(2)
    c_pair(3)
    c_in(1)
    y_out(1)
    y_step(1)
    build_bands(turned, 1, 2, taps, row_bwd, col_bwd)
    c_in(2)
    c_in(3)
    a_step(3)
    ends(lambda: zb_both(1))
    b_step(1, 1)
    middles(lambda: zb_both(0))
    y_out(2)
    ends(lambda: za_out(0))
    y_step(2)
    y_out(3)
    b_step(2)
    y_step(3)

    @middles
    def _():
        zb_both(1)
        zb_both(2)
        za_out(0)

    @ends
    def _():
        za_out(1)
        zb_both(2)

    b_step(3)
    ends(lambda: za_out(2))

    def arrived():
        for v in range(2):
            for q in range(planes):
                def two():
                    ca(q, v, 1).wait_recv()
                    cb(q, v, 1).wait_recv()

                if v:
                    two()
                else:
                    pl.when(q != p)(two)
        whole_far = part(c_peer, 0, row_blocks)
        remote(whole_far, whole_far, ca_s.at[p], ca_r.at[p], c_peer).wait_recv()

    arrived()
    pull(2)

    @middles
    def _():
        za_out(1)
        za_out(2)

    pull(2)
    yb_out()
    pull(groups)
    a_end()
    tile_out(0, 0, cut2).start()
    b_end()
    tile_out(1, cut2, row_blocks).start()
    for copy in (tile_out(0, 0, cut2), tile_out(1, cut2, row_blocks)):
        copy.wait()

    def written(g, carry):
        grads_out(g).wait()
        return carry

    lax.fori_loop(0, groups, written, 0)

    pl.when(up_ok)(lambda: za(p, 0).wait_send())
    pl.when(down_ok)(lambda: za(p, 1).wait_send())
    yb().wait_send()
    own_c.wait_send()
    cb(p, 1).wait_send()
    ca(p, 1).wait_send()
    ya(p).wait_send()
    for v in range(2):
        pl.when(up_ok)(lambda: zb(p, v, 0).wait_send())
        pl.when(down_ok)(lambda: zb(p, v, 1).wait_send())
    for i in range(1, planes):
        def ended(q, way, more):
            ya(q).wait_send()
            for v in range(2):
                ca(q, v).wait_send()
                cb(q, v).wait_send()
            if i < last:
                @pl.when(more)
                def _():
                    za(q, way).wait_send()
                    for v in range(2):
                        zb(q, v, way).wait_send()
        streams(i, ended)
    for i in range(planes):
        for v in range(2):
            rc(v, i).wait_send()
        for h in range(2):
            ry(i, h).wait_send()
    for i in range(last):
        for h in range(2):
            rz(i, i, up_peer, h).wait_send()
        for v in range(2):
            rzb(v, i, i, up_peer).wait_send()
    ryb().wait_send()


def divisor(number, wanted):
    return max(d for d in range(1, wanted + 1) if number % d == 0)


def hand_over(parts, tile_from, grads_from, tile_to, grads_to, tile_held, grads_held, sem_in, sem_out):
    size = grads_from.shape[0] // parts
    spots = [pl.ds(n * size, size) for n in range(parts)]
    copies = [(tile_from, tile_held, tile_to)] + [
        (grads_from.at[spot], grads_held.at[spot], grads_to.at[spot]) for spot in spots]
    copies = [(pltpu.make_async_copy(source, held, sem_in.at[n]),
               pltpu.make_async_copy(held, target, sem_out.at[n]))
              for n, (source, held, target) in enumerate(copies)]
    for fetch, _ in copies:
        fetch.start()
    for fetch, put in copies:
        fetch.wait()
        put.start()
    for _, put in copies:
        put.wait()


def in_place(stamps, tile_of, row_offset, col_offset, psf_model, psf_rows, psf_cols, cotangent):
    peers = lax.axis_size("tile")
    planes = peers // 4
    stamp_count, stamp_rows, stamp_cols = stamps.shape
    models, terms, taps = psf_rows.shape
    block_rows = stamp_rows // 2
    tile_rows, tile_cols = cotangent.shape
    row_blocks = tile_rows // block_rows
    col_blocks = tile_cols // stamp_cols
    cut = row_blocks * 5 // 8
    cut2 = row_blocks * 5 // 8
    group = divisor(stamp_count, 16)
    lasts = peers * row_blocks * col_blocks // stamp_count
    list_rows = -(-(lasts + 5) // 8) * 8
    model_rows = -(-models // 8) * 8
    flops = 2 * stamp_count * terms * stamp_rows * stamp_cols * (stamp_rows + stamp_cols)
    cost = pl.CostEstimate(flops=8 * flops, bytes_accessed=40 << 20, transcendentals=0)
    hbm = pl.BlockSpec(memory_space=pltpu.HBM)
    short = jnp.bfloat16
    dma = pltpu.SemaphoreType.DMA
    piece = (block_rows, stamp_cols)
    full, upper, lower = ((col_blocks, rows) + piece for rows in (row_blocks, cut2, row_blocks - cut2))
    line = lambda array: array.reshape((1, stamp_count))
    outs = (
        jax.ShapeDtypeStruct((row_blocks, block_rows, tile_cols), short),
        jax.ShapeDtypeStruct(stamps.shape, short),
    )
    row_op, col_op = ((models, size, terms * size) for size in (stamp_rows, stamp_cols))

    made = pl.pallas_call(
        partial(whole_kernel, peers, cut, cut2, group),
        out_shape=outs,
        in_specs=[hbm] * 8,
        out_specs=(hbm, hbm),
        scratch_shapes=[
            pltpu.VMEM((col_blocks, peers * row_blocks + 1) + piece, short),
            pltpu.VMEM((stamp_count + 1, stamp_rows, stamp_cols), jnp.float32),
            pltpu.VMEM(stamps.shape, short),
            pltpu.VMEM(row_op, short),
            pltpu.VMEM(col_op, short),
            pltpu.VMEM(row_op, short),
            pltpu.VMEM(col_op, short),
            pltpu.VMEM((4, 1, stamp_count), jnp.int32),
            pltpu.VMEM((2, terms, taps, models), jnp.float32),
            pltpu.VMEM((4 * terms, model_rows, stamp_count), jnp.float32),
            pltpu.VMEM(outs[0].shape, short),
            pltpu.VMEM(stamps.shape, short),
            pltpu.VMEM((list_rows, stamp_count), jnp.int32),
            pltpu.SMEM((list_rows, stamp_count), jnp.int32),
            pltpu.VMEM((2 * planes,) + full, short),
            pltpu.VMEM((2 * planes,) + full, short),
            pltpu.VMEM((planes,) + upper, short),
            pltpu.VMEM((planes,) + upper, short),
            pltpu.VMEM((planes,) + upper, short),
            pltpu.VMEM((2 * planes,) + upper, short),
            pltpu.VMEM((2 * planes,) + lower, short),
            pltpu.VMEM((4 * planes,) + lower, short),
            pltpu.VMEM((1,) + lower, short),
            pltpu.VMEM((1,) + lower, short),
            dma((col_blocks + 8,)), dma((2 + stamp_count // group,)),
        ] + [dma((2 * planes,))] * 2 + [dma((4 * planes,))] * 2 + [dma((planes,))] * 2 + [dma, dma]
        + [dma((2 * planes,))] * 4
        + [dma((2 * planes,))] * 2 + [dma((2 * planes,))] * 2 + [dma((2 * planes,)), dma((4 * planes,))]
        + [dma((2 * planes,)), dma((4 * planes,))] + [dma, dma],
        compiler_params=pltpu.CompilerParams(collective_id=0, has_side_effects=True,
                                             vmem_limit_bytes=60 << 20),
        cost_estimate=cost,
    )(tile_of.reshape((1, stamp_count)), line(row_offset), line(col_offset), line(psf_model),
      psf_rows.transpose(1, 2, 0), psf_cols.transpose(1, 2, 0),
      stamps, cotangent.reshape(outs[0].shape))
    parts = divisor(stamp_count, 8)
    tile_image, stamp_grad = pl.pallas_call(
        partial(hand_over, parts), out_shape=outs, in_specs=[hbm, hbm], out_specs=(hbm, hbm),
        scratch_shapes=[pltpu.VMEM(out.shape, short) for out in outs] + [dma((parts + 1,))] * 2,
    )(*made)
    return tile_image.reshape(cotangent.shape), stamp_grad


def fits(stamps, cotangent):
    count, rows, cols = stamps.shape
    peers = lax.axis_size("tile")
    return (peers == 16 and count == 128 and cols == 128 and rows % 32 == 0 and rows <= 128
            and peers * cotangent.shape[0] * cotangent.shape[1] * 4 <= 12 << 20)


def per_device_any(*args):
    if fits(args[0], args[-1]):
        return in_place(*args)
    return per_device(*args)


def solution(mesh):
    in_specs = (
        P(("band", "tile"), None, None),
        P(("band", "tile"), None),
        P(("band", "tile")),
        P(("band", "tile")),
        P(("band", "tile")),
        P("band", None, None),
        P("band", None, None),
        P(("band", "tile"), None),
    )
    out_specs = (P(("band", "tile"), None), P(("band", "tile"), None, None))
    return jax.shard_map(
        per_device_any, mesh=mesh, in_specs=in_specs, out_specs=out_specs, check_vma=False
    )
```

```python
from functools import partial

import jax
import jax.numpy as jnp
from jax import lax
from jax.experimental import pallas as pl
from jax.experimental.pallas import tpu as pltpu
from jax.sharding import PartitionSpec as P


def passed_along(array, axis, by):
    peers = lax.axis_size(axis)
    pairs = [(i, i + by) for i in range(peers) if 0 <= i + by < peers]
    return lax.ppermute(array, axis, pairs)


def for_sending(array):

    def short(part):
        return part.astype(jnp.bfloat16) if part.dtype == jnp.float32 else part

    return jax.tree.map(short, array)


def band_table(taps_count, size):
    half_width = (taps_count - 1) // 2
    places = jnp.arange(size, dtype=jnp.int32)
    offsets = places[None, :] - places[:, None] + half_width
    taps_index = jnp.arange(taps_count, dtype=jnp.int32)
    table = (offsets[None, :, :] == taps_index[:, None, None]).astype(jnp.float32)
    return table.reshape((taps_count, size * size))


def build_ops(profiles, size):
    model_total, term_total, taps_count = profiles.shape
    table = band_table(taps_count, size)
    mats = jnp.dot(
        profiles.reshape((model_total * term_total, taps_count)),
        table,
        precision=lax.Precision.HIGHEST,
    )
    return mats.reshape((model_total, term_total, size, size)).astype(jnp.bfloat16)


def chosen(ops, models):
    model_total, term_total, size, _ = ops.shape
    picks = (models[:, None] == jnp.arange(model_total, dtype=jnp.int32)[None, :]).astype(ops.dtype)
    mats = jnp.dot(picks, ops.reshape((model_total, -1)), preferred_element_type=jnp.float32)
    return mats.astype(ops.dtype).reshape((models.shape[0], term_total, size, size))


def convolve_some(images, row_mats, col_mats):
    row_pass = jnp.einsum(
        "bkij,bjx->bkix", row_mats, images, preferred_element_type=jnp.float32
    ).astype(jnp.bfloat16)
    return jnp.einsum(
        "bkix,bkyx->biy", row_pass, col_mats, preferred_element_type=jnp.float32
    ).astype(jnp.bfloat16)


def transpose_some(windows, row_mats, col_mats):
    back_pass = jnp.einsum(
        "biy,bkyx->bkix", windows, col_mats, preferred_element_type=jnp.float32
    ).astype(jnp.bfloat16)
    return jnp.einsum(
        "bkji,bkjx->bix", row_mats, back_pass, preferred_element_type=jnp.float32
    ).astype(jnp.bfloat16)


def apply_all(function, images, models, row_ops, col_ops):
    batch = divisor(images.shape[0], 32)

    def some(inputs):
        part, part_models = inputs
        return function(part, chosen(row_ops, part_models), chosen(col_ops, part_models))

    cut = images.reshape((-1, batch) + images.shape[1:])
    return lax.map(some, (cut, models.astype(jnp.int32).reshape((-1, batch)))).reshape(images.shape)


def per_device(stamps, tile_of, row_offset, col_offset, psf_model, psf_rows, psf_cols, cotangent):
    peer_count = lax.axis_size("tile")
    stamp_count, stamp_rows, stamp_cols = stamps.shape
    block_rows = stamp_rows // 2
    tile_rows, tile_cols = cotangent.shape
    row_blocks = tile_rows // block_rows
    col_blocks = tile_cols // stamp_cols
    capacity = max(2, (5 * stamp_count + 4 * peer_count - 1) // (4 * peer_count))
    slot_total = peer_count * capacity
    row_ops = build_ops(psf_rows, stamp_rows)
    col_ops = build_ops(psf_cols, stamp_cols)
    target = tile_of[:, 0]
    order = jnp.arange(stamp_count, dtype=jnp.int32)
    earlier = (target[None, :] == target[:, None]) & (order[None, :] < order[:, None])
    slots = target * capacity + jnp.sum(earlier.astype(jnp.int32), axis=1)
    slot_ids = jnp.arange(slot_total, dtype=jnp.int32)
    matches = slots[None, :] == slot_ids[:, None]
    place = matches.astype(jnp.bfloat16)
    details = jnp.stack([jnp.ones_like(target), row_offset, col_offset, psf_model], axis=1)
    detail_send = jnp.sum(jnp.where(matches[:, :, None], details[None, :, :], 0), axis=1)
    detail_send = detail_send.reshape(peer_count, capacity, 4)
    raw_send = jnp.dot(
        place,
        stamps.reshape((stamp_count, stamp_rows * stamp_cols)),
        preferred_element_type=jnp.float32,
    )
    raw_send = raw_send.astype(jnp.bfloat16).reshape(peer_count, capacity, stamp_rows, stamp_cols)
    raw_part = lax.all_to_all(raw_send, "tile", split_axis=0, concat_axis=0, tiled=True)
    info_part = lax.all_to_all(detail_send, "tile", split_axis=0, concat_axis=0, tiled=True)
    flat = raw_part.reshape((-1, stamp_rows, stamp_cols))
    result = apply_all(convolve_some, flat, info_part.reshape((-1, 4))[:, 3], row_ops, col_ops)
    received = result.reshape(raw_part.shape)
    info_flat = info_part.reshape((slot_total, 4))
    upper_block = info_flat[:, 1]
    block_ids = jnp.stack([upper_block, upper_block + 1], axis=1) * col_blocks + info_flat[:, 2:3]
    targets = jnp.arange((row_blocks + 1) * col_blocks, dtype=jnp.int32)
    placing = (block_ids.reshape(-1)[None, :] == targets[:, None]).astype(jnp.bfloat16)
    pieces = received.reshape((slot_total * 2, block_rows * stamp_cols))
    extended = jnp.dot(placing, pieces, preferred_element_type=jnp.float32)
    extended = extended.reshape(row_blocks + 1, col_blocks, block_rows, stamp_cols).transpose(
        0, 2, 1, 3
    )
    extended = extended.reshape((row_blocks + 1) * block_rows, tile_cols)
    arriving = passed_along(extended[tile_rows:].astype(jnp.bfloat16), "tile", 1).astype(
        jnp.float32
    )
    tile_sum = extended[:tile_rows].at[:block_rows].add(arriving)
    tile_image = tile_sum.astype(jnp.bfloat16)
    rim = passed_along(cotangent[:block_rows], "tile", -1)
    padded = jnp.concatenate([cotangent, rim], axis=0)
    blocks = padded.reshape(row_blocks + 1, block_rows, col_blocks, stamp_cols).transpose(
        0, 2, 1, 3
    )
    blocks = blocks.reshape((row_blocks + 1) * col_blocks, block_rows * stamp_cols)
    windows = lax.dot_general(
        placing, blocks, (((0,), (0,)), ((), ())), preferred_element_type=jnp.float32
    )
    windows = windows.astype(jnp.bfloat16).reshape(slot_total, stamp_rows, stamp_cols)
    slot_grads = apply_all(transpose_some, windows, info_flat[:, 3], row_ops, col_ops)
    slot_grads = slot_grads.reshape(peer_count, capacity, stamp_rows, stamp_cols)
    returned = lax.all_to_all(
        for_sending(slot_grads), "tile", split_axis=0, concat_axis=0, tiled=True
    ).astype(slot_grads.dtype)
    stamp_grad = lax.dot_general(
        place,
        returned.reshape((slot_total, stamp_rows * stamp_cols)),
        (((0,), (0,)), ((), ())),
        preferred_element_type=jnp.float32,
    )
    stamp_grad = stamp_grad.astype(jnp.bfloat16).reshape(stamp_count, stamp_rows, stamp_cols)
    return (tile_image, stamp_grad)


MESH = pl.DeviceIdType.MESH


def band_matrix(row, count, rows):
    lanes = row.shape[1]
    half = (count - 1) // 2
    spread = jnp.broadcast_to(row, (rows, lanes))
    turned = pltpu.roll(spread, lanes - half, 1, stride=1, stride_axis=0)
    down = lax.broadcasted_iota(jnp.int32, (rows, lanes), 0)
    across = lax.broadcasted_iota(jnp.int32, (rows, lanes), 1)
    return jnp.where(jnp.abs(across - down) <= half, turned, 0.0).astype(jnp.bfloat16)


def turn_taps(raw, turned):
    _, terms, count, models = raw.shape
    lanes = turned.shape[2]
    for a in range(2):
        for k in range(terms):
            values = raw[a, k]
            for way in range(2):
                rows = [values[count - 1 - t:count - t] for t in range(count)] if way else [values]
                tall = jnp.concatenate(rows + [jnp.zeros((lanes - count, models), jnp.float32)], axis=0)
                square = jnp.concatenate(
                    [tall, jnp.zeros((lanes, lanes - models), jnp.float32)], axis=1)
                turned[(a * 2 + way) * terms + k] = square.T[:turned.shape[1]]


def build_bands(turned, row_base, col_base, count, row_ops, col_ops):
    models, size, width = row_ops.shape
    lanes = col_ops.shape[1]
    terms = width // size

    def build(m, carry):
        row_ops[m] = jnp.concatenate(
            [band_matrix(turned[row_base * terms + k, pl.ds(m, 1)], count, size)[:, :size]
             for k in range(terms)], axis=1)
        for k in range(terms):
            col_ops[m, :, k * lanes:(k + 1) * lanes] = band_matrix(
                turned[col_base * terms + k, pl.ds(m, 1)], count, lanes)
        return carry

    lax.fori_loop(0, models, build, 0)


def fill_lists(fields, lists, row_blocks, col_blocks, lasts):
    lanes = fields.shape[2]
    upper = fields[0] * row_blocks + fields[1]
    block = upper * col_blocks + fields[2]
    square = jnp.broadcast_to(block, (lanes, lanes))
    turned = square.T
    down = lax.broadcasted_iota(jnp.int32, (lanes, lanes), 0)
    across = lax.broadcasted_iota(jnp.int32, (lanes, lanes), 1)
    lists[0:1, :] = jnp.zeros((1, lanes), jnp.int32)
    for r in range(lasts):
        hit = jnp.where(turned == across + r * lanes, down + 1, 0)
        lists[1 + r:2 + r, :] = jnp.max(hit, axis=0, keepdims=True)
    earlier = jnp.where((turned == square) & (down < across), down + 1, 0)
    lists[lasts + 1:lasts + 2, :] = jnp.max(earlier, axis=0, keepdims=True)
    lists[lasts + 2:lasts + 3, :] = upper
    lists[lasts + 3:lasts + 4, :] = fields[2]
    lists[lasts + 4:lasts + 5, :] = fields[3]


def remote(src, dst, send, recv, device):
    return pltpu.make_async_remote_copy(src_ref=src, dst_ref=dst, send_sem=send, recv_sem=recv,
                                        device_id={"tile": device}, device_id_type=MESH)


def whole_kernel(peers, cut, cut2, group, tile_of, row_of, col_of, model_of, row_taps, col_taps,
                 stamps_hbm, cot_hbm, tile_hbm, grads_hbm,
                 sky, sums, stamps_ref, row_fwd, col_fwd, row_bwd, col_bwd, fields, raw, turned,
                 tile_ref, grads_ref, lists_v, lists,
                 out_c, from_c, out_y, from_y, out_z, from_z, out_zb, from_zb, out_yb, from_yb,
                 own_sem, end_sem, za_s, za_r, zb_s, zb_r, ya_s, ya_r, yb_s, yb_r, ca_s, ca_r, cb_s, cb_r,
                 rc_s, rc_r, ry_s, ry_r, rz_s, rz_r, rzb_s, rzb_r, ryb_s, ryb_r):
    planes = peers // 4
    last = planes - 1
    me = lax.axis_index("tile")
    core = lax.rem(me, 2)
    row = lax.rem(me // 2, 2)
    p = me // 4
    count, stamp_rows, stamp_cols = stamps_ref.shape
    groups = count // group
    col_blocks, _, block_rows, _ = sky.shape
    row_blocks = tile_ref.shape[0]
    models = row_fwd.shape[0]
    lasts = peers * row_blocks * col_blocks // count
    PREV, UPPER, COL, MODEL = (lasts + 1 + i for i in range(4))
    rest = row_blocks - cut
    up_ok, down_ok = p < last, p > 0

    def tile_at(q, v=0, c=0):
        y = 1 - row if v else row
        return q * 4 + y * 2 + (1 - core if c else core)

    def part(tile, low, size):
        return sky.at[:, pl.ds(tile * row_blocks + low, size)]

    y_peer, c_peer = tile_at(p, 1), tile_at(p, 0, 1)
    up_peer, down_peer = tile_at(lax.min(p + 1, last)), tile_at(lax.max(p - 1, 0))

    def za(q, way):
        spot = part(tile_at(q), 0, cut)
        slot = way * planes + q
        return remote(spot, spot, za_s.at[slot], za_r.at[slot], down_peer if way else up_peer)

    def zb(q, v, way):
        spot = part(tile_at(q, v), cut, rest)
        slot = (way * 2 + v) * planes + q
        return remote(spot, spot, zb_s.at[slot], zb_r.at[slot], down_peer if way else up_peer)

    def ya(q, far=0):
        spot = part(tile_at(q, far), 0, cut)
        return remote(spot, spot, ya_s.at[q], ya_r.at[q], y_peer)

    def yb(far=0):
        spot = part(tile_at(p, far), cut, rest)
        return remote(spot, spot, yb_s, yb_r, y_peer)

    def ca(q, v, far=0):
        spot = part(tile_at(q, v, far), 0, cut)
        slot = v * planes + q
        return remote(spot, spot, ca_s.at[slot], ca_r.at[slot], c_peer)

    def cb(q, v, far=0):
        spot = part(tile_at(q, v, far), cut, rest)
        slot = v * planes + q
        return remote(spot, spot, cb_s.at[slot], cb_r.at[slot], c_peer)

    def streams(i, body, side=None):
        low = p < planes // 2
        below = True if side is None else (low if side == 0 else jnp.logical_not(low))
        above = True if side is None else (low if side == 1 else jnp.logical_not(low))
        pl.when(jnp.logical_and(p >= i, below))(lambda: body(p - i, 0, up_ok))
        pl.when(jnp.logical_and(p + i <= last, above))(lambda: body(p + i, 1, down_ok))

    def a_step(i):
        def body(q, way, more):
            za(q, way).wait_recv()
            if i < last:
                pl.when(more)(lambda: za(q, way).start())
            ya(q).start()
            ca(q, 0).start()
        streams(i, body)

    def b_step(i, side=None):
        def body(q, way, more):
            for v in range(2):
                zb(q, v, way).wait_recv()
                if i < last:
                    pl.when(more)(lambda: zb(q, v, way).start())
                cb(q, v).start()
        streams(i, body, side)

    def y_step(i):
        def body(q, way, more):
            ya(q, 1).wait_recv()
            ca(q, 1).start()
        if i:
            streams(i, body)
        else:
            body(p, 0, None)

    def apply(g, row_ops, col_ops, image, put):
        chosen_models = [lists[MODEL, g * group + u] for u in range(group)]
        firsts = [jnp.dot(image(g * group + u), col_ops[chosen_models[u]],
                          preferred_element_type=jnp.float32).astype(jnp.bfloat16)
                  for u in range(group)]
        for u in range(group):
            tall = jnp.concatenate(
                [firsts[u][:, k * stamp_cols:(k + 1) * stamp_cols]
                 for k in range(firsts[u].shape[1] // stamp_cols)], axis=0)
            put(g * group + u, jnp.dot(row_ops[chosen_models[u]], tall,
                                       preferred_element_type=jnp.float32).astype(jnp.bfloat16))

    def add(s, value):
        sums[s + 1] = value.astype(jnp.float32) + sums[lists[PREV, s]]

    def forward(g, carry):
        apply(g, row_fwd, col_fwd, lambda s: stamps_ref[s], add)
        return carry

    def window(s):
        upper, col = lists[UPPER, s], lists[COL, s]
        return jnp.concatenate([sky[col, upper], sky[col, upper + 1]], axis=0)

    def grads_out(g):
        spot = pl.ds(g * group, group)
        return pltpu.make_async_copy(grads_ref.at[spot], grads_hbm.at[spot], end_sem.at[2 + g])

    def tile_out(slot, low, high):
        spot = pl.ds(low, high - low)
        return pltpu.make_async_copy(tile_ref.at[spot], tile_hbm.at[spot], end_sem.at[slot])

    def keep_grad(s, value):
        grads_ref[s] = value

    def backward(g, carry):
        apply(g, row_bwd, col_bwd, window, keep_grad)
        grads_out(g).start()
        return carry

    def runner(step):
        reached = [0]

        def run(number):
            stop = min(groups, reached[0] + number)
            if stop > reached[0]:
                lax.fori_loop(reached[0], stop, step, 0)
            reached[0] = stop
        return run

    compute, pull = runner(forward), runner(backward)

    def summed(tile, low, high, put, *others, cols=None):
        base = tile * (row_blocks * col_blocks)
        width = lists.shape[1]

        def body(r, carry):
            for b in cols or range(col_blocks):
                lower = base + (r * col_blocks + b + width)
                above = lower - col_blocks
                out = (sums[lists[lower // width, lax.rem(lower, width)], :block_rows]
                       + sums[lists[above // width, lax.rem(above, width)], block_rows:])
                for ref, index, shift in others:
                    out = out + ref[index, b, r - shift].astype(jnp.float32)
                put(b, r, out.astype(jnp.bfloat16))
            return carry

        lax.fori_loop(low, high, body, 0)

    half = p // 2
    mirrored = (1 - 2 * half) * p + last * half
    targets = [last * half + (1 - 2 * half) * q for q in (3, 2, 1 - mirrored, mirrored)]

    def rc(v, i):
        slot = v * planes + i
        return remote(out_c.at[slot], from_c.at[slot], rc_s.at[slot], rc_r.at[slot], c_peer)

    wide = col_blocks // 2
    sides = [range(h * wide, (h + 1) * wide) for h in range(2)]

    def side(h):
        return pl.ds(h * wide, wide)

    def ry(i, h):
        return remote(out_y.at[i, side(h)], from_y.at[i, side(h)],
                      ry_s.at[2 * i + h], ry_r.at[2 * i + h], y_peer)

    def way_of(q):
        return jnp.where(q > p, 0, 1)

    def rz(i, slot, device, h):
        return remote(out_z.at[i, side(h)], from_z.at[slot, side(h)],
                      rz_s.at[2 * i + h], rz_r.at[2 * slot + h], device)

    def rzb(v, i, slot, device):
        return remote(out_zb.at[v * planes + i], from_zb.at[v * 2 * planes + slot],
                      rzb_s.at[v * planes + i], rzb_r.at[v * 2 * planes + slot], device)

    def ryb():
        return remote(out_yb.at[0], from_yb.at[0], ryb_s, ryb_r, y_peer)

    def into(ref, index, shift):
        def put(b, r, value):
            ref[index, b, r - shift] = value
        return put

    def c_out(v, i):
        slot = v * planes + i
        summed(tile_at(targets[i], v, 1), 0, row_blocks, into(out_c, slot, 0))
        rc(v, i).start()

    def c_in(i):
        rc(0, i).wait_recv()
        rc(1, i).wait_recv()

    def y_out(i):
        for h in range(2):
            summed(tile_at(targets[i], 1), 0, cut2, into(out_y, i, 0), (from_c, planes + i, 0),
                   cols=sides[h])
            ry(i, h).start()

    def chain(i, make, tile, low, high, put, *others, cols=None):
        q = targets[i]
        way = way_of(q)
        slot = way * planes + q
        device = jnp.where(q > p, up_peer, down_peer)
        first = jnp.logical_or(jnp.logical_and(q > p, p == 0), jnp.logical_and(q < p, p == last))
        copy, source, offset = make(slot, device)
        pl.when(first)(lambda: summed(tile, low, high, put, *others, cols=cols))

        @pl.when(jnp.logical_not(first))
        def _():
            copy.wait_recv()
            summed(tile, low, high, put, *others, (source, offset + slot, low), cols=cols)

        copy.start()

    def za_out(i):
        for h in range(2):
            ry(i, h).wait_recv()
            chain(i, lambda slot, device: (rz(i, slot, device, h), from_z, 0), tile_at(targets[i]),
                  0, cut2, into(out_z, i, 0), (from_c, i, 0), (from_y, i, 0), cols=sides[h])

    def zb_out(v, i):
        chain(i, lambda slot, device: (rzb(v, i, slot, device), from_zb, v * 2 * planes),
              tile_at(targets[i], v), cut2, row_blocks, into(out_zb, v * planes + i, cut2),
              (from_c, v * planes + i, 0))

    def ending(make, body):
        def some(*ways):
            made = [make(way * planes + p) for way in ways]
            for copy, _ in made:
                copy.wait_recv()
            body(*[source for _, source in made])

        pl.when(p == 0)(lambda: some(1))
        pl.when(p == last)(lambda: some(0))
        pl.when(jnp.logical_and(p > 0, p < last))(lambda: some(0, 1))

    def yb_out():
        ending(lambda slot: (rzb(1, 0, slot, up_peer), (from_zb, 2 * planes + slot, cut2)),
               lambda *more: summed(tile_at(p, 1), cut2, row_blocks, into(out_yb, 0, cut2),
                                    (from_c, planes + last, 0), *more))
        ryb().start()

    def to_tile(b, r, value):
        tile_ref[r, :, b * stamp_cols:(b + 1) * stamp_cols] = value

    def a_end():
        for h in range(2):
            ry(last, h).wait_recv()
            ending(lambda slot: (rz(0, slot, up_peer, h), (from_z, slot, 0)),
                   lambda *more: summed(me, 0, cut2, to_tile, (from_c, last, 0), (from_y, last, 0),
                                        *more, cols=sides[h]))

    def b_end():
        ryb().wait_recv()
        ending(lambda slot: (rzb(0, 0, slot, up_peer), (from_zb, slot, cut2)),
               lambda *more: summed(me, cut2, row_blocks, to_tile, (from_c, last, 0),
                                    (from_yb, 0, cut2), *more))

    barrier = pltpu.get_barrier_semaphore()

    def greet(device):
        pl.semaphore_signal(barrier, inc=1, device_id={"tile": device}, device_id_type=MESH)

    pl.when(up_ok)(lambda: greet(up_peer))
    pl.when(down_ok)(lambda: greet(down_peer))
    greet(y_peer)
    greet(c_peer)
    own = [pltpu.make_async_copy(cot_hbm.at[:, :, pl.ds(b * stamp_cols, stamp_cols)],
                                 sky.at[b, pl.ds(me * row_blocks, row_blocks)], own_sem.at[b])
           for b in range(col_blocks)]
    small = [pltpu.make_async_copy(source, target, own_sem.at[col_blocks + 2 + n])
             for n, (source, target) in enumerate(
                 [(array, fields.at[n]) for n, array in enumerate((tile_of, row_of, col_of, model_of))]
                 + [(row_taps, raw.at[0]), (col_taps, raw.at[1])])]
    fetch = pltpu.make_async_copy(stamps_hbm, stamps_ref, own_sem.at[col_blocks])
    for copy in own + small:
        copy.start()
    fetch.start()
    for b in range(col_blocks):
        sky[b, peers * row_blocks] = jnp.zeros((block_rows, stamp_cols), jnp.bfloat16)
    sums[0] = jnp.zeros((stamp_rows, stamp_cols), jnp.float32)
    for copy in small:
        copy.wait()
    fill_lists(fields, lists_v, row_blocks, col_blocks, lasts)
    listing = pltpu.make_async_copy(lists_v, lists, own_sem.at[col_blocks + 1])
    listing.start()
    turn_taps(raw, turned)
    taps = raw.shape[2]
    for copy in own:
        copy.wait()
    pl.semaphore_wait(barrier, 2 + jnp.where(up_ok, 1, 0) + jnp.where(down_ok, 1, 0))
    whole = part(me, 0, row_blocks)
    own_c = remote(whole, whole, ca_s.at[p], ca_r.at[p], c_peer)
    pl.when(up_ok)(lambda: za(p, 0).start())
    pl.when(down_ok)(lambda: za(p, 1).start())
    yb().start()
    ya(p).start()
    own_c.start()
    build_bands(turned, 0, 3, taps, row_fwd, col_fwd)
    listing.wait()
    fetch.wait()

    def ends(body):
        pl.when(jnp.logical_or(p == 0, p == last))(body)

    def middles(body):
        pl.when(jnp.logical_and(p > 0, p < last))(body)

    def zb_own():
        for v in range(2):
            pl.when(up_ok)(lambda: zb(p, v, 0).start())
            pl.when(down_ok)(lambda: zb(p, v, 1).start())

    def c_pair(i):
        c_out(0, i)
        c_out(1, i)

    def zb_both(i):
        for v in range(2):
            zb_out(v, i)

    compute(3)
    yb(1).wait_recv()
    cb(p, 1).start()
    a_step(1)
    ends(zb_own)
    compute(groups)
    c_pair(0)
    c_pair(1)
    middles(zb_own)
    y_step(0)
    a_step(2)
    c_in(0)
    ends(lambda: zb_both(0))
    y_out(0)
    b_step(1, 0)
    c_pair(2)
    c_pair(3)
    c_in(1)
    y_out(1)
    y_step(1)
    build_bands(turned, 1, 2, taps, row_bwd, col_bwd)
    c_in(2)
    c_in(3)
    a_step(3)
    ends(lambda: zb_both(1))
    b_step(1, 1)
    middles(lambda: zb_both(0))
    y_out(2)
    ends(lambda: za_out(0))
    y_step(2)
    y_out(3)
    b_step(2)
    y_step(3)

    @middles
    def _():
        zb_both(1)
        zb_both(2)
        za_out(0)

    @ends
    def _():
        za_out(1)
        zb_both(2)

    b_step(3)
    ends(lambda: za_out(2))

    def arrived():
        for v in range(2):
            for q in range(planes):
                def two():
                    ca(q, v, 1).wait_recv()
                    cb(q, v, 1).wait_recv()

                if v:
                    two()
                else:
                    pl.when(q != p)(two)
        whole_far = part(c_peer, 0, row_blocks)
        remote(whole_far, whole_far, ca_s.at[p], ca_r.at[p], c_peer).wait_recv()

    arrived()
    pull(2)

    @middles
    def _():
        za_out(1)
        za_out(2)

    pull(2)
    yb_out()
    pull(groups)
    a_end()
    tile_out(0, 0, cut2).start()
    b_end()
    tile_out(1, cut2, row_blocks).start()
    for copy in (tile_out(0, 0, cut2), tile_out(1, cut2, row_blocks)):
        copy.wait()

    def written(g, carry):
        grads_out(g).wait()
        return carry

    lax.fori_loop(0, groups, written, 0)

    pl.when(up_ok)(lambda: za(p, 0).wait_send())
    pl.when(down_ok)(lambda: za(p, 1).wait_send())
    yb().wait_send()
    own_c.wait_send()
    cb(p, 1).wait_send()
    ca(p, 1).wait_send()
    ya(p).wait_send()
    for v in range(2):
        pl.when(up_ok)(lambda: zb(p, v, 0).wait_send())
        pl.when(down_ok)(lambda: zb(p, v, 1).wait_send())
    for i in range(1, planes):
        def ended(q, way, more):
            ya(q).wait_send()
            for v in range(2):
                ca(q, v).wait_send()
                cb(q, v).wait_send()
            if i < last:
                @pl.when(more)
                def _():
                    za(q, way).wait_send()
                    for v in range(2):
                        zb(q, v, way).wait_send()
        streams(i, ended)
    for i in range(planes):
        for v in range(2):
            rc(v, i).wait_send()
        for h in range(2):
            ry(i, h).wait_send()
    for i in range(last):
        for h in range(2):
            rz(i, i, up_peer, h).wait_send()
        for v in range(2):
            rzb(v, i, i, up_peer).wait_send()
    ryb().wait_send()


def divisor(number, wanted):
    return max(d for d in range(1, wanted + 1) if number % d == 0)


def hand_over(parts, tile_from, grads_from, tile_to, grads_to, tile_held, grads_held, sem_in, sem_out):
    size = grads_from.shape[0] // parts
    spots = [pl.ds(n * size, size) for n in range(parts)]
    copies = [(tile_from, tile_held, tile_to)] + [
        (grads_from.at[spot], grads_held.at[spot], grads_to.at[spot]) for spot in spots]
    copies = [(pltpu.make_async_copy(source, held, sem_in.at[n]),
               pltpu.make_async_copy(held, target, sem_out.at[n]))
              for n, (source, held, target) in enumerate(copies)]
    for fetch, _ in copies:
        fetch.start()
    for fetch, put in copies:
        fetch.wait()
        put.start()
    for _, put in copies:
        put.wait()


def in_place(stamps, tile_of, row_offset, col_offset, psf_model, psf_rows, psf_cols, cotangent):
    peers = lax.axis_size("tile")
    planes = peers // 4
    stamp_count, stamp_rows, stamp_cols = stamps.shape
    models, terms, taps = psf_rows.shape
    block_rows = stamp_rows // 2
    tile_rows, tile_cols = cotangent.shape
    row_blocks = tile_rows // block_rows
    col_blocks = tile_cols // stamp_cols
    cut = row_blocks * 5 // 8
    cut2 = row_blocks * 5 // 8
    group = divisor(stamp_count, 16)
    lasts = peers * row_blocks * col_blocks // stamp_count
    list_rows = -(-(lasts + 5) // 8) * 8
    model_rows = -(-models // 8) * 8
    flops = 2 * stamp_count * terms * stamp_rows * stamp_cols * (stamp_rows + stamp_cols)
    cost = pl.CostEstimate(flops=8 * flops, bytes_accessed=40 << 20, transcendentals=0)
    hbm = pl.BlockSpec(memory_space=pltpu.HBM)
    short = jnp.bfloat16
    dma = pltpu.SemaphoreType.DMA
    piece = (block_rows, stamp_cols)
    full, upper, lower = ((col_blocks, rows) + piece for rows in (row_blocks, cut2, row_blocks - cut2))
    line = lambda array: array.reshape((1, stamp_count))
    outs = (
        jax.ShapeDtypeStruct((row_blocks, block_rows, tile_cols), short),
        jax.ShapeDtypeStruct(stamps.shape, short),
    )
    row_op, col_op = ((models, size, terms * size) for size in (stamp_rows, stamp_cols))

    made = pl.pallas_call(
        partial(whole_kernel, peers, cut, cut2, group),
        out_shape=outs,
        in_specs=[hbm] * 8,
        out_specs=(hbm, hbm),
        scratch_shapes=[
            pltpu.VMEM((col_blocks, peers * row_blocks + 1) + piece, short),
            pltpu.VMEM((stamp_count + 1, stamp_rows, stamp_cols), jnp.float32),
            pltpu.VMEM(stamps.shape, short),
            pltpu.VMEM(row_op, short),
            pltpu.VMEM(col_op, short),
            pltpu.VMEM(row_op, short),
            pltpu.VMEM(col_op, short),
            pltpu.VMEM((4, 1, stamp_count), jnp.int32),
            pltpu.VMEM((2, terms, taps, models), jnp.float32),
            pltpu.VMEM((4 * terms, model_rows, stamp_count), jnp.float32),
            pltpu.VMEM(outs[0].shape, short),
            pltpu.VMEM(stamps.shape, short),
            pltpu.VMEM((list_rows, stamp_count), jnp.int32),
            pltpu.SMEM((list_rows, stamp_count), jnp.int32),
            pltpu.VMEM((2 * planes,) + full, short),
            pltpu.VMEM((2 * planes,) + full, short),
            pltpu.VMEM((planes,) + upper, short),
            pltpu.VMEM((planes,) + upper, short),
            pltpu.VMEM((planes,) + upper, short),
            pltpu.VMEM((2 * planes,) + upper, short),
            pltpu.VMEM((2 * planes,) + lower, short),
            pltpu.VMEM((4 * planes,) + lower, short),
            pltpu.VMEM((1,) + lower, short),
            pltpu.VMEM((1,) + lower, short),
            dma((col_blocks + 8,)), dma((2 + stamp_count // group,)),
        ] + [dma((2 * planes,))] * 2 + [dma((4 * planes,))] * 2 + [dma((planes,))] * 2 + [dma, dma]
        + [dma((2 * planes,))] * 4
        + [dma((2 * planes,))] * 2 + [dma((2 * planes,))] * 2 + [dma((2 * planes,)), dma((4 * planes,))]
        + [dma((2 * planes,)), dma((4 * planes,))] + [dma, dma],
        compiler_params=pltpu.CompilerParams(collective_id=0, has_side_effects=True,
                                             vmem_limit_bytes=60 << 20),
        cost_estimate=cost,
    )(tile_of.reshape((1, stamp_count)), line(row_offset), line(col_offset), line(psf_model),
      psf_rows.transpose(1, 2, 0), psf_cols.transpose(1, 2, 0),
      stamps, cotangent.reshape(outs[0].shape))
    parts = divisor(stamp_count, 8)
    tile_image, stamp_grad = pl.pallas_call(
        partial(hand_over, parts), out_shape=outs, in_specs=[hbm, hbm], out_specs=(hbm, hbm),
        scratch_shapes=[pltpu.VMEM(out.shape, short) for out in outs] + [dma((parts + 1,))] * 2,
    )(*made)
    return tile_image.reshape(cotangent.shape), stamp_grad


def fits(stamps, cotangent):
    count, rows, cols = stamps.shape
    peers = lax.axis_size("tile")
    return (peers == 16 and count == 128 and cols == 128 and rows % 32 == 0 and rows <= 128
            and peers * cotangent.shape[0] * cotangent.shape[1] * 4 <= 12 << 20)


def per_device_any(*args):
    if fits(args[0], args[-1]):
        return in_place(*args)
    return per_device(*args)


def solution(mesh):
    in_specs = (
        P(("band", "tile"), None, None),
        P(("band", "tile"), None),
        P(("band", "tile")),
        P(("band", "tile")),
        P(("band", "tile")),
        P("band", None, None),
        P("band", None, None),
        P(("band", "tile"), None),
    )
    out_specs = (P(("band", "tile"), None), P(("band", "tile"), None, None))
    return jax.shard_map(
        per_device_any, mesh=mesh, in_specs=in_specs, out_specs=out_specs, check_vma=False
    )
```
